512 devices in a mesh: dp: 8 (over z_lo, core), seq: 64 (over z_hi, y, x).
Axes of the slice: x: 4, y: 8, z: 8 (z_hi: 2, z_lo: 4; z = z_hi * 4 + z_lo), core: 2. Of those that a mesh axis runs over, the one named last changes fastest.
Arguments:
- value_branch: bfloat16 [512, 65536], P(None, ('dp', 'seq')), parts along dimension 1, may hold values from -6 to 6
- first_gate: bfloat16 [512, 65536], P(None, ('dp', 'seq')), parts along dimension 1, may hold values from -6 to 6
- second_gate: bfloat16 [512, 65536], P(None, ('dp', 'seq')), parts along dimension 1, may hold values from -6 to 6
- out_cotangent: bfloat16 [512, 65536], P(None, ('dp', 'seq')), parts along dimension 1, may hold values from -6 to 6
- pos_weight: float32 [64, 33], replicated, may hold values from -4 to 4
- pos_bias: float32 [64], replicated, may hold values from -3.140625 to 3.140625
- mid_weight: float32 [64, 64], replicated, may hold values from -0.75 to 0.75
- mid_bias: float32 [64], replicated, may hold values from -3.140625 to 3.140625
- out_weight: float32 [1024, 64], replicated, may hold values from -0.0234375 to 0.0234375
- decay_rates: float32 [1024], replicated, may hold values from 3.07 to 15.35
Outputs:
- value_grad: bfloat16 [512, 65536], P(None, ('dp', 'seq')), parts along dimension 1
- first_gate_grad: bfloat16 [512, 65536], P(None, ('dp', 'seq')), parts along dimension 1
- second_gate_grad: bfloat16 [512, 65536], P(None, ('dp', 'seq')), parts along dimension 1
- pos_weight_grad: float32 [512, 33], P('dp'), parts along dimension 0
- pos_bias_grad: float32 [512], P('dp'), parts along dimension 0
- mid_weight_grad: float32 [512, 64], P('dp'), parts along dimension 0
- mid_bias_grad: float32 [512], P('dp'), parts along dimension 0
- out_weight_grad: float32 [1024, 512], P('seq', 'dp'), parts along dimension 1
The draws below stay inside these ranges and needn't reach their ends.
There are 8 independent parts, one for each index of `dp`. The reference program is written for one: setup_inputs(seed, part) draws one part's arguments, and reference() takes and returns one part's arrays. A program takes and returns all parts, laid end to end along the dimension named above; an argument that names none is the same for every part. Nothing has to cross between parts.
All inputs are finite; a program needn't handle non-finite values.
Results may differ from the reference program's by a relative error of at most 0.017.
Values may be sent and summed in bfloat16 or wider, within the bound.
No kernel may reach another device: no remote copies, remote signals or barrier semaphores. Data moves between devices by JAX's collectives and lax.ppermute only.
A program may use at most 64 MiB of HBM per device.

```python
import math
import jax
import jax.numpy as jnp
from jax import lax

D = 512
FILTER_WIDTH = 64
BANDS = 16
RADIX = 128
PE_FEATURES = 33
SEQLEN = 8192
FREQ_ROWS = 128


def levels(own_key, shape, split, least, high):
    gain, own = 1.0, jax.random.fold_in(own_key, 6)
    for axis_at, parts in split:
        steps = jnp.exp(jax.random.uniform(jax.random.fold_in(own, axis_at), (parts,), jnp.float32, least / len(split), high / len(split)))
        gain = gain * jnp.repeat(steps, shape[axis_at] // parts).reshape([-1 if axis == axis_at else 1 for axis in range(len(shape))])
    return gain


def bell_draw(own_key, dims, scale, most, split=(), kind=jnp.bfloat16):
    loudness = levels(own_key, dims, split, -0.22, 0.18) if split else 1.0
    result = jax.random.normal(own_key, dims, jnp.float32) * scale * loudness
    return jnp.minimum(jnp.maximum(result, -most), most).astype(kind)


def setup_inputs(seed: int = 0, part: int = 0) -> dict:
    splits = jax.random.split(jax.random.key(seed), 11)
    part_keys = jax.random.split(jax.random.fold_in(splits[10], part), 11)
    return {
        "value_branch": bell_draw(part_keys[0], (D, SEQLEN), 1.0, 6.0, ((1, 64),)),
        "first_gate": bell_draw(part_keys[1], (D, SEQLEN), 1.0, 6.0, ((1, 64),)),
        "second_gate": bell_draw(part_keys[2], (D, SEQLEN), 1.0, 6.0, ((1, 64),)),
        "out_cotangent": bell_draw(part_keys[3], (D, SEQLEN), 1.0, 6.0, ((1, 64),)),
        "pos_weight": bell_draw(splits[4], (FILTER_WIDTH, PE_FEATURES), 1.0, 4.0, (), jnp.float32),
        "pos_bias": jnp.clip(jax.random.uniform(splits[5], (FILTER_WIDTH,), jnp.float32, -3.140625, 3.140625), -3.140625, 3.140625),
        "mid_weight": bell_draw(splits[6], (FILTER_WIDTH, FILTER_WIDTH), FILTER_WIDTH ** -0.5, 0.75, (), jnp.float32),
        "mid_bias": jnp.clip(jax.random.uniform(splits[7], (FILTER_WIDTH,), jnp.float32, -3.140625, 3.140625), -3.140625, 3.140625),
        "out_weight": bell_draw(splits[8], (2 * D, FILTER_WIDTH), (FILTER_WIDTH * SEQLEN // 8) ** -0.5, 0.0234375, (), jnp.float32),
        "decay_rates": jnp.clip(jnp.exp(jax.random.uniform(splits[9], (2 * D,), jnp.float32, math.log(3.07), math.log(15.35))), 3.07, 15.35),
    }


def rounded(value):
    return lax.optimization_barrier(value.astype(jnp.bfloat16)).astype(jnp.float32)


def make_tables(freq_rows, radix):
    length_all = freq_rows * radix
    freq_index = jnp.arange(freq_rows, dtype=jnp.int32)
    half_index = jnp.arange(freq_rows // 2, dtype=jnp.int32)
    inner_index = jnp.arange(radix, dtype=jnp.int32)
    angle_one = ((freq_index[:, None] * half_index[None, :]) % freq_rows).astype(jnp.float32) * (2.0 * math.pi / freq_rows)
    angle_two = ((inner_index[:, None] * inner_index[None, :]) % radix).astype(jnp.float32) * (2.0 * math.pi / radix)
    angle_twid = ((freq_index[:, None] * inner_index[None, :]) % length_all).astype(jnp.float32) * (2.0 * math.pi / length_all)
    return (rounded(jnp.cos(angle_one)), rounded(jnp.sin(angle_one)), rounded(jnp.cos(angle_two)),
            rounded(jnp.sin(angle_two)), jnp.cos(angle_twid), jnp.sin(angle_twid))


def section_left(table, data):
    return jnp.einsum("kn,rnm->rkm", table, data, precision=lax.Precision.HIGHEST)


def section_right(data, table):
    return jnp.einsum("rkn,nm->rkm", data, table, precision=lax.Precision.HIGHEST)


def final_section(table, data):
    return jnp.einsum("kn,rkm->rnm", table, data, precision=lax.Precision.HIGHEST)


def forward_spectrum(signal, tables, freq_rows, radix):
    cos_one, sin_one, cos_two, sin_two, twid_cos, twid_sin = tables
    count = signal.shape[0]
    shaped = signal.astype(jnp.float32).reshape(count, freq_rows // 2, radix)
    real_a = section_left(cos_one, shaped)
    imag_a = -section_left(sin_one, shaped)
    real_b = rounded(real_a * twid_cos + imag_a * twid_sin)
    imag_b = rounded(imag_a * twid_cos - real_a * twid_sin)
    real_x = section_right(real_b, cos_two) + section_right(imag_b, sin_two)
    imag_x = section_right(imag_b, cos_two) - section_right(real_b, sin_two)
    return real_x, imag_x


def inverse_signal(product, tables, freq_rows, radix):
    cos_one, sin_one, cos_two, sin_two, twid_cos, twid_sin = tables
    real_p, imag_p = product
    real_q = section_right(real_p, cos_two) - section_right(imag_p, sin_two)
    imag_q = section_right(imag_p, cos_two) + section_right(real_p, sin_two)
    real_r = rounded(real_q * twid_cos - imag_q * twid_sin)
    imag_r = rounded(imag_q * twid_cos + real_q * twid_sin)
    output = final_section(cos_one, real_r) - final_section(sin_one, imag_r)
    count = real_p.shape[0]
    return (output * (1.0 / (freq_rows * radix))).reshape(count, freq_rows // 2 * radix)


def spectral_product(left, right, conj_left, conj_right):
    sign_left = -1.0 if conj_left else 1.0
    sign_right = -1.0 if conj_right else 1.0
    real_part = left[0] * right[0] - sign_left * sign_right * left[1] * right[1]
    imag_part = sign_left * left[1] * right[0] + sign_right * left[0] * right[1]
    return rounded(real_part), rounded(imag_part)


def channel_block(value_blk, first_blk, second_blk, cot_blk, filt_blk, tables, freq_rows, radix):
    count = value_blk.shape[0]
    seq_len = value_blk.shape[1]
    filt_real, filt_imag = forward_spectrum(filt_blk, tables, freq_rows, radix)
    filt_real = filt_real.reshape(count, 2, freq_rows, radix)
    filt_imag = filt_imag.reshape(count, 2, freq_rows, radix)
    spec_one = (filt_real[:, 0], filt_imag[:, 0])
    spec_two = (filt_real[:, 1], filt_imag[:, 1])
    spec_val = forward_spectrum(value_blk, tables, freq_rows, radix)
    conv_one = inverse_signal(spectral_product(spec_one, spec_val, False, False), tables, freq_rows, radix)
    gated = rounded(first_blk.astype(jnp.float32) * conv_one)
    spec_gated = forward_spectrum(gated, tables, freq_rows, radix)
    conv_two = inverse_signal(spectral_product(spec_two, spec_gated, False, False), tables, freq_rows, radix)
    cot_wide = cot_blk.astype(jnp.float32)
    second_grad = (cot_wide * conv_two).astype(jnp.bfloat16)
    grad_two = rounded(cot_wide * second_blk.astype(jnp.float32))
    spec_gtwo = forward_spectrum(grad_two, tables, freq_rows, radix)
    gated_grad = inverse_signal(spectral_product(spec_two, spec_gtwo, True, False), tables, freq_rows, radix)
    filt_grad_two = inverse_signal(spectral_product(spec_gtwo, spec_gated, False, True), tables, freq_rows, radix)
    first_grad = (gated_grad * conv_one).astype(jnp.bfloat16)
    grad_one = rounded(gated_grad * first_blk.astype(jnp.float32))
    spec_gone = forward_spectrum(grad_one, tables, freq_rows, radix)
    value_grad = inverse_signal(spectral_product(spec_one, spec_gone, True, False), tables, freq_rows, radix).astype(jnp.bfloat16)
    filt_grad_one = inverse_signal(spectral_product(spec_gone, spec_val, False, True), tables, freq_rows, radix)
    filt_grads = jnp.stack([filt_grad_one, filt_grad_two], axis=1).reshape(2 * count, seq_len)
    return value_grad, first_grad, second_grad, filt_grads


def positional_features(positions, seq_len, bands):
    band_index = jnp.arange(1, bands + 1, dtype=jnp.int32)
    angles = ((band_index[:, None] * positions[None, :]) % seq_len).astype(jnp.float32) * (2.0 * math.pi / seq_len)
    ramp = positions.astype(jnp.float32)[None, :] / seq_len
    return jnp.concatenate([ramp, jnp.cos(angles), jnp.sin(angles)], axis=0)


def contract_last(left, right):
    return lax.dot_general(left, right, (((1,), (1,)), ((), ())), precision=lax.Precision.HIGHEST)


def reference(value_branch, first_gate, second_gate, out_cotangent, pos_weight, pos_bias, mid_weight, mid_bias, out_weight, decay_rates):
    positions = jnp.arange(SEQLEN, dtype=jnp.int32)
    features = positional_features(positions, SEQLEN, BANDS)
    pre_one = jnp.dot(pos_weight, features, precision=lax.Precision.HIGHEST) + pos_bias[:, None]
    act_one = jnp.sin(pre_one)
    pre_two = jnp.dot(mid_weight, act_one, precision=lax.Precision.HIGHEST) + mid_bias[:, None]
    act_two = jnp.sin(pre_two)
    window = jnp.exp(-decay_rates[:, None] * positions.astype(jnp.float32)[None, :] / SEQLEN)
    filters = (jnp.dot(out_weight, act_two, precision=lax.Precision.HIGHEST) * window).astype(jnp.bfloat16)
    tables = make_tables(FREQ_ROWS, RADIX)
    group_size = 16
    blocks = D // group_size

    def run_block(items):
        return channel_block(items[0], items[1], items[2], items[3], items[4], tables, FREQ_ROWS, RADIX)

    results = lax.map(run_block, (value_branch.reshape(blocks, group_size, SEQLEN),
                                  first_gate.reshape(blocks, group_size, SEQLEN),
                                  second_gate.reshape(blocks, group_size, SEQLEN),
                                  out_cotangent.reshape(blocks, group_size, SEQLEN),
                                  filters.reshape(blocks, 2 * group_size, SEQLEN)))
    value_grad = results[0].reshape(D, SEQLEN)
    first_gate_grad = results[1].reshape(D, SEQLEN)
    second_gate_grad = results[2].reshape(D, SEQLEN)
    filter_grad = results[3].reshape(2 * D, SEQLEN) * window / SEQLEN
    out_weight_grad = contract_last(filter_grad, act_two)
    pre_two_grad = jnp.dot(out_weight.T, filter_grad, precision=lax.Precision.HIGHEST) * jnp.cos(pre_two)
    mid_weight_grad = contract_last(pre_two_grad, act_one)
    mid_bias_grad = jnp.sum(pre_two_grad, axis=1)
    pre_one_grad = jnp.dot(mid_weight.T, pre_two_grad, precision=lax.Precision.HIGHEST) * jnp.cos(pre_one)
    pos_weight_grad = contract_last(pre_one_grad, features)
    pos_bias_grad = jnp.sum(pre_one_grad, axis=1)
    return (value_grad, first_gate_grad, second_gate_grad, pos_weight_grad, pos_bias_grad,
            mid_weight_grad, mid_bias_grad, out_weight_grad)
```

```python
import math

import jax
import jax.numpy as jnp
import numpy as np
from jax import lax
from jax.experimental import pallas as pl
from jax.experimental.pallas import tpu as pltpu
from jax.sharding import Mesh
from jax.sharding import PartitionSpec as P

F32 = jnp.float32
BF16 = jnp.bfloat16
RADIX = 128
HALF_ROWS = 64
SEQLEN = HALF_ROWS * RADIX
KROWS = 80
WIDTH = 64
PE = 33
PE_PAD = 208
CHUNK = 1024
CHANNELS = 8
ROWS = 2 * CHANNELS


def dft_tables():
    n1, n2 = 2 * HALF_ROWS, RADIX
    k1 = np.arange(KROWS)[:, None]
    live = (k1 <= n1 // 2).astype(np.float64)
    angle_one = 2.0 * np.pi * ((k1 * np.arange(n1 // 2)[None, :]) % n1) / n1
    cos_one = np.cos(angle_one) * live
    sin_one = np.sin(angle_one) * live
    left = np.concatenate([cos_one, -sin_one], axis=0)
    weight = np.where((k1 == 0) | (k1 == n1 // 2), 1.0, 2.0) / (n1 * n2)
    back = np.concatenate([cos_one * weight, -sin_one * weight], axis=0).T
    grid = np.arange(n2)
    angle_two = 2.0 * np.pi * ((grid[:, None] * grid[None, :]) % n2) / n2
    cos_two, sin_two = np.cos(angle_two), np.sin(angle_two)
    right = np.block([[cos_two, -sin_two], [sin_two, cos_two]])
    right_inv = np.block([[cos_two, sin_two], [-sin_two, cos_two]])
    angle_tw = 2.0 * np.pi * ((k1 * grid[None, :]) % (n1 * n2)) / (n1 * n2)
    bf = lambda a: np.asarray(a, np.float32).astype(jnp.bfloat16)
    return (
        bf(left),
        bf(back),
        bf(right),
        bf(right_inv),
        np.cos(angle_tw).astype(np.float32),
        np.sin(angle_tw).astype(np.float32),
    )


def features():
    positions = np.arange(SEQLEN)
    bands = np.arange(1, (PE - 1) // 2 + 1)
    angles = 2.0 * np.pi * ((bands[:, None] * positions[None, :]) % SEQLEN) / SEQLEN
    ramp = positions[None, :] / SEQLEN
    return np.concatenate([ramp, np.cos(angles), np.sin(angles)], axis=0).astype(np.float32)


def np_split(value, parts):
    pieces = []
    for _ in range(parts):
        piece = value.astype(jnp.bfloat16)
        pieces.append(piece)
        value = value - piece.astype(np.float32)
    return pieces


def feature_tables():
    table = features()
    hi, mid, lo = np_split(table, 3)
    pad = np.zeros((PE_PAD - 6 * PE, SEQLEN), jnp.bfloat16)
    stack = np.concatenate([hi, mid, lo, hi, mid, hi, pad], axis=0)
    tail = np.zeros((64, SEQLEN), jnp.bfloat16)
    tail[:PE] = hi
    tail[PE] = 1.0
    return stack, tail


def poly_tables():
    top = (math.pi / 2) ** 2 * 1.0001
    nodes = (np.cos(np.pi * (np.arange(64) + 0.5) / 64) + 1) * top / 2
    root = np.sqrt(nodes)
    cheb = np.polynomial.chebyshev.Chebyshev
    sin_fit = cheb.fit(nodes, np.sin(root) / root, 4, domain=[0, top])
    cos_fit = cheb.fit(nodes, np.cos(root), 5, domain=[0, top])
    to_poly = lambda c: [float(x) for x in c.convert(kind=np.polynomial.Polynomial).coef]
    return to_poly(sin_fit), to_poly(cos_fit)


SIN_COEF, COS_COEF = poly_tables()
PI_HI = 3.140625
PI_MID = float(np.float32(int((math.pi - PI_HI) * 2**22) / 2**22))
PI_LO = float(np.float32(math.pi - PI_HI - PI_MID))


def sin_cos(value):
    turns = jnp.round(value * (1.0 / math.pi))
    rest = ((value - turns * PI_HI) - turns * PI_MID) - turns * PI_LO
    half = turns * 0.5
    sign = 1.0 - 4.0 * (half - jnp.floor(half))
    square = rest * rest

    def horner(coefs):
        total = jnp.full_like(square, coefs[-1])
        for coef in coefs[-2::-1]:
            total = total * square + coef
        return total

    return (rest * sign) * horner(SIN_COEF), sign * horner(COS_COEF)


def dot(left, right):
    return lax.dot_general(left, right, (((1,), (0,)), ((), ())), preferred_element_type=F32)


def dot_last(left, right):
    return lax.dot_general(left, right, (((1,), (1,)), ((), ())), preferred_element_type=F32)


def split_four(value):
    high = value.astype(BF16)
    low = (value - high.astype(F32)).astype(BF16)
    return high, jnp.concatenate([high, low, high, low], axis=0)


def forward_pair(signal, left, right, twid_cos, twid_sin):
    stacked = dot(left, signal)
    rows = []
    for j in range(2):
        cols = slice(j * RADIX, (j + 1) * RADIX)
        real_a, imag_a = stacked[:KROWS, cols], stacked[KROWS:, cols]
        real_b = (real_a * twid_cos + imag_a * twid_sin).astype(BF16)
        imag_b = (imag_a * twid_cos - real_a * twid_sin).astype(BF16)
        rows.append(jnp.concatenate([real_b, imag_b], axis=1))
    return dot(jnp.concatenate(rows, axis=0), right)


def inverse_pair(product, back, right_inv, twid_cos, twid_sin):
    section = dot(product, right_inv)
    cols = []
    for j in range(2):
        real_q = section[j * KROWS : (j + 1) * KROWS, :RADIX]
        imag_q = section[j * KROWS : (j + 1) * KROWS, RADIX:]
        real_r = (real_q * twid_cos - imag_q * twid_sin).astype(BF16)
        imag_r = (imag_q * twid_cos + real_q * twid_sin).astype(BF16)
        cols.append(jnp.concatenate([real_r, imag_r], axis=0))
    return dot(back, jnp.concatenate(cols, axis=1))


def spectral_product(left, right, sign_left, sign_right):
    left_re, left_im = left[:, :RADIX], left[:, RADIX:]
    right_re, right_im = right[:, :RADIX], right[:, RADIX:]
    cross = left_im * right_im
    real = left_re * right_re + cross if sign_left * sign_right < 0 else left_re * right_re - cross
    one, two = left_im * right_re, left_re * right_im
    if sign_left > 0:
        imag = one + two if sign_right > 0 else one - two
    else:
        imag = two - one
    return jnp.concatenate([real.astype(BF16), imag.astype(BF16)], axis=1)


def network_kernel(
    pe_ref, wp_ref, bp_ref, wm_ref, bm_ref, wo_ref, rate_ref, left_ref, right_ref, tc_ref, ts_ref,
    a1_ref, a2_ref, c1_ref, c2_ref, spec_ref, filt,
):
    step = pl.program_id(0)
    span = 256
    for part in range(CHUNK // span):
        cols = slice(part * span, (part + 1) * span)
        pre_one = dot(wp_ref[...], pe_ref[:, cols]) + bp_ref[...]
        act_one, cos_one = sin_cos(pre_one)
        high, stack = split_four(act_one)
        a1_ref[:, cols] = high
        c1_ref[:, cols] = cos_one.astype(BF16)
        pre_two = dot(wm_ref[...], stack) + bm_ref[...]
        act_two, cos_two = sin_cos(pre_two)
        high, stack = split_four(act_two)
        a2_ref[:, cols] = high
        c2_ref[:, cols] = cos_two.astype(BF16)
        start = (step * CHUNK + part * span).astype(F32)
        times = (lax.broadcasted_iota(jnp.int32, (ROWS, span), 1).astype(F32) + start) * (1.0 / SEQLEN)
        rows = dot(wo_ref[...], stack) * jnp.exp(-rate_ref[...] * times)
        for j in range(span // RADIX):
            base = pl.multiple_of(step * (CHUNK // RADIX * ROWS) + (part * (span // RADIX) + j) * ROWS, ROWS)
            filt[pl.ds(base, ROWS), :] = rows[:, j * RADIX : (j + 1) * RADIX]

    @pl.when(step == SEQLEN // CHUNK - 1)
    def _():
        for o in range(2):
            for pair in range(CHANNELS // 2):
                signal = jnp.concatenate(
                    [filt[pl.ds(2 * (2 * pair + j) + o, HALF_ROWS, stride=ROWS), :] for j in range(2)], axis=1
                ).astype(BF16)
                spec_ref[o, pair * 2 * KROWS : (pair + 1) * 2 * KROWS, :] = forward_pair(
                    signal, left_ref[...], right_ref[...], tc_ref[...], ts_ref[...]
                )


def spectral_kernel(
    x_ref, spec_ref, left_ref, back_ref, right_ref, inv_ref, tc_ref, ts_ref,
    y_ref, dh_ref,
    xs, ys, sv, sg2, sz, sg1, conv, dz,
):
    xs[...] = x_ref[...].astype(F32)
    tables_f = (left_ref[...], right_ref[...], tc_ref[...], ts_ref[...])
    tables_i = (back_ref[...], inv_ref[...], tc_ref[...], ts_ref[...])
    stride = 3 * CHANNELS
    pairs = range(CHANNELS // 2)

    def signal(kind, pair):
        return jnp.concatenate(
            [xs[pl.ds(kind * CHANNELS + 2 * pair + j, HALF_ROWS, stride=stride), :] for j in range(2)], axis=1
        )

    def rows(pair):
        return slice(pair * 2 * KROWS, (pair + 1) * 2 * KROWS)

    def lanes(pair):
        return slice(pair * 2 * RADIX, (pair + 1) * 2 * RADIX)

    def emit(kind, pair, value):
        for j in range(2):
            ys[pl.ds(kind * CHANNELS + 2 * pair + j, HALF_ROWS, stride=stride), :] = value[
                :, j * RADIX : (j + 1) * RADIX
            ]

    def emit_filter(o, pair, value):
        for j in range(2):
            dh_ref[pl.ds(2 * (2 * pair + j) + o, HALF_ROWS, stride=ROWS), :] = value[:, j * RADIX : (j + 1) * RADIX]

    def product(left, right, sign_left, sign_right):
        return spectral_product(left, right, sign_left, sign_right)

    for p in pairs:
        sv[rows(p), :] = forward_pair(signal(0, p).astype(BF16), *tables_f)
    for p in pairs:
        sg2[rows(p), :] = forward_pair(signal(2, p).astype(BF16), *tables_f)
    for p in pairs:
        conv[:, lanes(p)] = inverse_pair(product(spec_ref[0, rows(p), :], sv[rows(p), :], 1, 1), *tables_i)
    for p in pairs:
        dz[:, lanes(p)] = inverse_pair(product(spec_ref[1, rows(p), :], sg2[rows(p), :], -1, 1), *tables_i)
    for p in pairs:
        gated = (signal(1, p) * conv[:, lanes(p)]).astype(BF16)
        sz[rows(p), :] = forward_pair(gated, *tables_f)
    for p in pairs:
        emit(1, p, dz[:, lanes(p)] * conv[:, lanes(p)])
        grad = (dz[:, lanes(p)] * signal(1, p)).astype(BF16)
        sg1[rows(p), :] = forward_pair(grad, *tables_f)
    for p in pairs:
        emit(0, p, inverse_pair(product(spec_ref[1, rows(p), :], sz[rows(p), :], 1, 1), *tables_i))
    for p in pairs:
        emit_filter(1, p, inverse_pair(product(sg2[rows(p), :], sz[rows(p), :], 1, -1), *tables_i))
    for p in pairs:
        emit(2, p, inverse_pair(product(spec_ref[0, rows(p), :], sg1[rows(p), :], -1, 1), *tables_i))
    for p in pairs:
        emit_filter(0, p, inverse_pair(product(sg1[rows(p), :], sv[rows(p), :], 1, -1), *tables_i))
    y_ref[...] = ys[...].astype(BF16)


def gradient_kernel(
    dh_ref, a1_ref, a2_ref, c1_ref, c2_ref, tail_ref, wo_ref, wm_ref, rate_ref, out_ref, inner_ref
):
    step = pl.program_id(0)

    @pl.when(step == 0)
    def _():
        out_ref[...] = jnp.zeros_like(out_ref)
        inner_ref[...] = jnp.zeros_like(inner_ref)

    per = CHUNK // RADIX
    wide = jnp.concatenate([dh_ref[i * ROWS : (i + 1) * ROWS, :] for i in range(per)], axis=1)
    start = (step * CHUNK).astype(F32)
    times = (lax.broadcasted_iota(jnp.int32, (ROWS, CHUNK), 1).astype(F32) + start) * (1.0 / SEQLEN)
    grad = (wide * jnp.exp(-rate_ref[...] * times) * (1.0 / SEQLEN)).astype(BF16)
    out_ref[...] += dot_last(grad, a2_ref[...])
    grad_two = dot(wo_ref[...], grad) * c2_ref[...].astype(F32)
    low_two = grad_two.astype(BF16)
    grad_one = dot(wm_ref[...], low_two) * c1_ref[...].astype(F32)
    low_one = grad_one.astype(BF16)
    inner_ref[:, :WIDTH] += dot_last(low_two, a1_ref[...])
    inner_ref[:, WIDTH:] += dot_last(low_one, tail_ref[...])
    lane = lax.broadcasted_iota(jnp.int32, (WIDTH, WIDTH), 1)
    bias = jnp.sum(grad_two, axis=1, keepdims=True)
    inner_ref[:, WIDTH:] += jnp.where(lane == PE + 1, bias, 0.0)


def full(shape):
    return pl.BlockSpec(shape, lambda i: (0,) * len(shape))


def network_forward(pos_weight, pos_bias, mid_weight, mid_bias, own_weight, own_rates, tables, stack):
    left, back, right, right_inv, twid_cos, twid_sin = tables
    ph = pos_weight.astype(BF16)
    pm = (pos_weight - ph.astype(F32)).astype(BF16)
    plo = (pos_weight - ph.astype(F32) - pm.astype(F32)).astype(BF16)
    wp = jnp.concatenate([ph, ph, ph, pm, pm, plo, jnp.zeros((WIDTH, PE_PAD - 6 * PE), BF16)], axis=1)

    def doubled(weight):
        high = weight.astype(BF16)
        low = (weight - high.astype(F32)).astype(BF16)
        return jnp.concatenate([high, high, low, low], axis=1)

    block = pl.BlockSpec((WIDTH, CHUNK), lambda i: (0, i))
    args = (
        stack, wp, pos_bias[:, None], doubled(mid_weight), mid_bias[:, None], doubled(own_weight),
        own_rates[:, None], left, right, twid_cos, twid_sin,
    )
    act = jax.ShapeDtypeStruct((WIDTH, SEQLEN), BF16)
    return pl.pallas_call(
        network_kernel,
        grid=(SEQLEN // CHUNK,),
        in_specs=[pl.BlockSpec((PE_PAD, CHUNK), lambda i: (0, i))] + [full(a.shape) for a in args[1:]],
        out_specs=[block] * 4 + [full((2, CHANNELS * KROWS, 2 * RADIX))],
        out_shape=[act] * 4 + [jax.ShapeDtypeStruct((2, CHANNELS * KROWS, 2 * RADIX), F32)],
        scratch_shapes=[pltpu.VMEM((HALF_ROWS * ROWS, RADIX), F32)],
        compiler_params=pltpu.CompilerParams(vmem_limit_bytes=12 << 20),
        cost_estimate=pl.CostEstimate(flops=1 << 30, bytes_accessed=10 << 20, transcendentals=1 << 20),
    )(*args)


def spectral_chain(x, spec, tables):
    left, back, right, right_inv, twid_cos, twid_sin = tables
    spectrum = pltpu.VMEM((CHANNELS * KROWS, 2 * RADIX), F32)
    wide = pltpu.VMEM((HALF_ROWS, CHANNELS * RADIX), F32)
    return pl.pallas_call(
        spectral_kernel,
        out_shape=[
            jax.ShapeDtypeStruct(x.shape, BF16),
            jax.ShapeDtypeStruct((HALF_ROWS * ROWS, RADIX), F32),
        ],
        scratch_shapes=[pltpu.VMEM(x.shape, F32)] * 2 + [spectrum] * 4 + [wide] * 2,
        compiler_params=pltpu.CompilerParams(vmem_limit_bytes=16 << 20),
        cost_estimate=pl.CostEstimate(flops=2 << 30, bytes_accessed=4 << 20, transcendentals=0),
    )(x, spec, left, back, right, right_inv, twid_cos, twid_sin)


def network_gradient(dh, acts, tail, own_weight, mid_weight, own_rates):
    block = pl.BlockSpec((WIDTH, CHUNK), lambda i: (0, i))
    args = (own_weight.T.astype(BF16), mid_weight.T.astype(BF16), own_rates[:, None])
    return pl.pallas_call(
        gradient_kernel,
        grid=(SEQLEN // CHUNK,),
        in_specs=[pl.BlockSpec((CHUNK // RADIX * ROWS, RADIX), lambda i: (i, 0))]
        + [block] * 5
        + [full(a.shape) for a in args],
        out_specs=[full((ROWS, WIDTH)), full((WIDTH, 2 * WIDTH))],
        out_shape=[jax.ShapeDtypeStruct((ROWS, WIDTH), F32), jax.ShapeDtypeStruct((WIDTH, 2 * WIDTH), F32)],
        compiler_params=pltpu.CompilerParams(vmem_limit_bytes=12 << 20),
        cost_estimate=pl.CostEstimate(flops=1 << 29, bytes_accessed=6 << 20, transcendentals=1 << 17),
    )(dh, *acts, tail, *args)


SEQ = ("z", "y", "x")


def on_device(
    value_branch, first_gate, second_gate, out_cotangent,
    pos_weight, pos_bias, mid_weight, mid_bias, out_weight, decay_rates,
):
    devices = lax.axis_size(SEQ)
    rank = lax.axis_index(SEQ)
    tables = dft_tables()
    stack, tail = feature_tables()
    grad_two = (out_cotangent.astype(F32) * second_gate.astype(F32)).astype(BF16)
    blocks = (devices, CHANNELS, RADIX)
    sent = jnp.concatenate([a.reshape(blocks) for a in (value_branch, first_gate, grad_two)], axis=1)
    x = lax.all_to_all(sent, SEQ, 0, 0, tiled=True)

    own_weight = lax.dynamic_slice_in_dim(out_weight, rank * ROWS, ROWS)
    own_rates = lax.dynamic_slice_in_dim(decay_rates, rank * ROWS, ROWS)
    a1, a2, c1, c2, spec = network_forward(
        pos_weight, pos_bias, mid_weight, mid_bias, own_weight, own_rates, tables, stack
    )
    y, dh = spectral_chain(x.reshape(HALF_ROWS * 3 * CHANNELS, RADIX), spec, tables)
    back = lax.all_to_all(y.reshape(devices, 3 * CHANNELS, RADIX), SEQ, 0, 0, tiled=True)
    out_weight_grad, inner = network_gradient(dh, (a1, a2, c1, c2), tail, own_weight, mid_weight, own_rates)
    inner = inner + lax.ppermute(inner, "z", [(0, 1), (1, 0)])
    peers = lax.axis_size(("y", "x"))
    shares = jnp.broadcast_to(inner.astype(BF16)[None], (peers,) + inner.shape)
    inner = jnp.sum(lax.all_to_all(shares, ("y", "x"), 0, 0, tiled=True).astype(F32), axis=0)

    shape = value_branch.shape
    conv_two = back[:, :CHANNELS].reshape(shape)
    return (
        back[:, 2 * CHANNELS :].reshape(shape),
        back[:, CHANNELS : 2 * CHANNELS].reshape(shape),
        (out_cotangent.astype(F32) * conv_two.astype(F32)).astype(BF16),
        inner[:, WIDTH : WIDTH + PE],
        inner[:, WIDTH + PE],
        inner[:, :WIDTH],
        inner[:, WIDTH + PE + 1],
        out_weight_grad,
    )


def solution(mesh):
    grid = Mesh(mesh.devices.reshape(mesh.shape["dp"], 2, 8, 4), ("dp",) + SEQ)
    part = P(None, ("dp",) + SEQ)
    in_specs = (part,) * 4 + (P(),) * 6
    out_specs = (part,) * 3 + (P("dp", None), P("dp"), P("dp", None), P("dp"), P(SEQ, "dp"))
    return jax.shard_map(on_device, mesh=grid, in_specs=in_specs, out_specs=out_specs, check_vma=False)
```

```python
import math

import jax
import jax.numpy as jnp
import numpy as np
from jax import lax
from jax.experimental import pallas as pl
from jax.experimental.pallas import tpu as pltpu
from jax.sharding import Mesh
from jax.sharding import PartitionSpec as P

F32 = jnp.float32
BF16 = jnp.bfloat16
RADIX = 128
HALF_ROWS = 64
SEQLEN = HALF_ROWS * RADIX
KROWS = 80
WIDTH = 64
PE = 33
PE_BLOCK = 40
CHUNK = 1024
CHANNELS = 8
ROWS = 2 * CHANNELS
SHARE = 56
DATA = 3 * CHANNELS
SEND = DATA + SHARE
VMEM_BYTES = 60 << 20
CHAIN_BYTES = 60 << 20


def dft_tables():
    n1, n2 = 2 * HALF_ROWS, RADIX
    k1 = np.arange(KROWS)[:, None]
    live = (k1 <= n1 // 2).astype(np.float64)
    angle_one = 2.0 * np.pi * ((k1 * np.arange(n1 // 2)[None, :]) % n1) / n1
    cos_one = np.cos(angle_one) * live
    sin_one = np.sin(angle_one) * live
    left = np.concatenate([cos_one, -sin_one], axis=0)
    weight = np.where((k1 == 0) | (k1 == n1 // 2), 1.0, 2.0) / (n1 * n2)
    back = np.concatenate([cos_one * weight, -sin_one * weight], axis=0).T
    grid = np.arange(n2)
    angle_two = 2.0 * np.pi * ((grid[:, None] * grid[None, :]) % n2) / n2
    cos_two, sin_two = np.cos(angle_two), np.sin(angle_two)
    right = np.block([[cos_two, -sin_two], [sin_two, cos_two]])
    right_inv = np.block([[cos_two, sin_two], [-sin_two, cos_two]])
    angle_tw = 2.0 * np.pi * ((k1 * grid[None, :]) % (n1 * n2)) / (n1 * n2)
    bf = lambda a: np.asarray(a, np.float32).astype(jnp.bfloat16)
    return (
        bf(left),
        bf(back),
        bf(right),
        bf(right_inv),
        np.cos(angle_tw).astype(np.float32),
        np.sin(angle_tw).astype(np.float32),
    )


def features():
    positions = np.arange(SEQLEN)
    bands = np.arange(1, (PE - 1) // 2 + 1)
    angles = 2.0 * np.pi * ((bands[:, None] * positions[None, :]) % SEQLEN) / SEQLEN
    ramp = positions[None, :] / SEQLEN
    return np.concatenate([ramp, np.cos(angles), np.sin(angles)], axis=0).astype(np.float32)


def np_split(value, parts):
    pieces = []
    for _ in range(parts):
        piece = value.astype(jnp.bfloat16)
        pieces.append(piece)
        value = value - piece.astype(np.float32)
    return pieces


def feature_tables():
    table = np.zeros((PE_BLOCK, SEQLEN), np.float32)
    table[:PE] = features()
    table[PE] = 1.0
    pieces = np_split(table, 3)
    pad = np.zeros((2 * WIDTH - 3 * PE_BLOCK, SEQLEN), jnp.bfloat16)
    return np.concatenate(pieces + [pad], axis=0), pieces[0]


def poly_tables():
    top = math.pi**2 * 1.0001
    nodes = (np.cos(np.pi * (np.arange(64) + 0.5) / 64) + 1) * top / 2
    root = np.sqrt(nodes)
    cheb = np.polynomial.chebyshev.Chebyshev
    sin_fit = cheb.fit(nodes, math.sqrt(2) * np.sin(root / 2) / root, 4, domain=[0, top])
    cos_fit = cheb.fit(nodes, math.sqrt(2) * np.cos(root / 2), 4, domain=[0, top])
    to_poly = lambda c: [float(x) for x in c.convert(kind=np.polynomial.Polynomial).coef]
    return to_poly(sin_fit), to_poly(cos_fit)


SIN_COEF, COS_COEF = poly_tables()
TURN_HI = 6.28125
TURN_LO = float(np.float32(2 * math.pi - TURN_HI))


def sin_cos(value):
    turns = jnp.round(value * (0.5 / math.pi))
    rest = (value - turns * TURN_HI) - turns * TURN_LO
    square = rest * rest

    def horner(coefs):
        total = square * coefs[-1] + coefs[-2]
        for coef in coefs[-3::-1]:
            total = total * square + coef
        return total

    half = rest * horner(SIN_COEF)
    return half * horner(COS_COEF), 1.0 - half * half


def dot(left, right):
    return lax.dot_general(left, right, (((1,), (0,)), ((), ())), preferred_element_type=F32)


def dot_last(left, right):
    return lax.dot_general(left, right, (((1,), (1,)), ((), ())), preferred_element_type=F32)


def split_two(value):
    high = value.astype(BF16)
    return high, (value - high.astype(F32)).astype(BF16)


def forward_pair(signal, left, right, twid_cos, twid_sin):
    stacked = dot(left, signal)
    rows = []
    for j in range(2):
        cols = slice(j * RADIX, (j + 1) * RADIX)
        real_a, imag_a = stacked[:KROWS, cols], stacked[KROWS:, cols]
        real_b = (real_a * twid_cos + imag_a * twid_sin).astype(BF16)
        imag_b = (imag_a * twid_cos - real_a * twid_sin).astype(BF16)
        rows.append(jnp.concatenate([real_b, imag_b], axis=1))
    return dot(jnp.concatenate(rows, axis=0), right)


def inverse_pair(product, back, right_inv, twid_cos, twid_sin):
    section = dot(product, right_inv)
    cols = []
    for j in range(2):
        real_q = section[j * KROWS : (j + 1) * KROWS, :RADIX]
        imag_q = section[j * KROWS : (j + 1) * KROWS, RADIX:]
        real_r = (real_q * twid_cos - imag_q * twid_sin).astype(BF16)
        imag_r = (imag_q * twid_cos + real_q * twid_sin).astype(BF16)
        cols.append(jnp.concatenate([real_r, imag_r], axis=0))
    return dot(back, jnp.concatenate(cols, axis=1))


def spectral_product(left, right, sign_left, sign_right):
    left_re, left_im = left[:, :RADIX], left[:, RADIX:]
    right_re, right_im = right[:, :RADIX], right[:, RADIX:]
    cross = left_im * right_im
    real = left_re * right_re + cross if sign_left * sign_right < 0 else left_re * right_re - cross
    one, two = left_im * right_re, left_re * right_im
    if sign_left > 0:
        imag = one + two if sign_right > 0 else one - two
    else:
        imag = two - one
    return jnp.concatenate([real.astype(BF16), imag.astype(BF16)], axis=1)


def pack_kernel(v_hbm, x1_hbm, x2_hbm, cot_hbm, out_hbm, x2, cot, grad, sems):
    loads = [pltpu.make_async_copy(cot_hbm, cot, sems.at[0]), pltpu.make_async_copy(x2_hbm, x2, sems.at[1])]
    moves = [
        pltpu.make_async_copy(v_hbm, out_hbm.at[:, pl.ds(0, CHANNELS), :], sems.at[2]),
        pltpu.make_async_copy(x1_hbm, out_hbm.at[:, pl.ds(CHANNELS, CHANNELS), :], sems.at[3]),
    ]
    for copy in loads + moves:
        copy.start()
    for copy in loads:
        copy.wait()
    grad[...] = (cot[...].astype(F32) * x2[...].astype(F32)).astype(BF16)
    last = pltpu.make_async_copy(grad, out_hbm.at[:, pl.ds(2 * CHANNELS, CHANNELS), :], sems.at[4])
    last.start()
    for copy in moves + [last]:
        copy.wait()


def network_kernel(
    pe_ref, ramp_ref, left_ref, right_ref, tc_ref, ts_ref,
    pos_hbm, pos_bias_hbm, mid_hbm, mid_bias_hbm, out_hbm, rate_hbm,
    act_ref, cos_ref, spec_ref, own_ref, own_rate_ref,
    filt, square, wp, wm, wo, bias, decay,
    pos_ref, pos_bias_ref, mid_ref, mid_bias_ref, out_ref, rate_ref, sems,
):
    step = pl.program_id(0)

    @pl.when(step == 0)
    def _():
        sources = (pos_hbm, pos_bias_hbm, mid_hbm, mid_bias_hbm, out_hbm, rate_hbm)
        targets = (pos_ref, pos_bias_ref, mid_ref, mid_bias_ref, out_ref, rate_ref)
        copies = [pltpu.make_async_copy(src, dst, sems.at[i]) for i, (src, dst) in enumerate(zip(sources, targets))]
        for copy in copies:
            copy.start()
        for copy in copies:
            copy.wait()
        rank = lax.axis_index(SEQ)
        lane = pl.multiple_of(rank // 8 * RADIX, RADIX)
        first = pl.multiple_of(rank % 8 * ROWS, ROWS)

        square[...] = jnp.zeros_like(square)
        for i in range(3):
            square[i * PE_BLOCK : i * PE_BLOCK + PE, :WIDTH] = pos_ref[...]
            square[i * PE_BLOCK + PE : i * PE_BLOCK + PE + 1, :WIDTH] = pos_bias_ref[...]
        wp[...] = jnp.concatenate(split_two(square[...].T[:WIDTH, :]), axis=0)

        square[...] = jnp.zeros_like(square)
        square[:WIDTH, :WIDTH] = mid_ref[...]
        own_ref[WIDTH:, :] = square[...].T[:WIDTH, :].astype(BF16)
        square[:WIDTH, WIDTH:] = mid_ref[...]
        wm[...] = jnp.concatenate(split_two(square[:WIDTH, :]), axis=0)

        square[:, :WIDTH] = jnp.broadcast_to(mid_bias_ref[...], (RADIX, WIDTH))
        bias[...] = square[...].T[:WIDTH, :]

        square[...] = jnp.broadcast_to(rate_ref[:, pl.ds(lane, RADIX)], (RADIX, RADIX)).T
        decay[...] = square[pl.ds(first, ROWS), :]
        own_rate_ref[...] = decay[...]

        block = out_ref[:, pl.ds(lane, RADIX)]
        square[...] = jnp.concatenate([block, block], axis=0).T
        mine = square[pl.ds(first, ROWS), :]
        wo[...] = jnp.concatenate(split_two(mine), axis=0)
        square[...] = jnp.zeros_like(square)
        square[:ROWS, :] = mine
        own_ref[:WIDTH, :] = square[...].T[:WIDTH, :].astype(BF16)

    span = 256
    parts = [slice(p * span, (p + 1) * span) for p in range(CHUNK // span)]
    wide_bias = jnp.concatenate([bias[...]] * (span // RADIX), axis=1)
    wide_rate = jnp.concatenate([decay[...]] * (span // RADIX), axis=1)
    for part, cols in enumerate(parts):
        both = dot(wp[...], pe_ref[:, cols])
        act, slope = sin_cos(both[:WIDTH] + both[WIDTH:])
        pieces = split_two(act)
        act_ref[:WIDTH, cols] = pieces[0]
        cos_ref[:WIDTH, cols] = slope.astype(BF16)
        both = dot(wm[...], jnp.concatenate(pieces, axis=0))
        act, slope = sin_cos(both[:WIDTH] + both[WIDTH:] + wide_bias)
        pieces = split_two(act)
        act_ref[WIDTH:, cols] = pieces[0]
        cos_ref[WIDTH:, cols] = slope.astype(BF16)
        both = dot(wo[...], jnp.concatenate(pieces, axis=0))
        rows = (both[:ROWS] + both[ROWS:]) * jnp.exp(-wide_rate * ramp_ref[:, cols])
        for j in range(span // RADIX):
            base = pl.multiple_of(step * (CHUNK // RADIX * ROWS) + (part * (span // RADIX) + j) * ROWS, ROWS)
            filt[pl.ds(base, ROWS), :] = rows[:, j * RADIX : (j + 1) * RADIX]

    @pl.when(step == SEQLEN // CHUNK - 1)
    def _():
        for o in range(2):
            for pair in range(CHANNELS // 2):
                signal = jnp.concatenate(
                    [filt[pl.ds(2 * (2 * pair + j) + o, HALF_ROWS, stride=ROWS), :] for j in range(2)], axis=1
                ).astype(BF16)
                spec_ref[o, pair * 2 * KROWS : (pair + 1) * 2 * KROWS, :] = forward_pair(
                    signal, left_ref[...], right_ref[...], tc_ref[...], ts_ref[...]
                )


def chain_kernel(
    x_ref, left_ref, back_ref, right_ref, inv_ref, tc_ref, ts_ref, own_ref, rate_ref, ramp_ref,
    spec, act_hbm, cos_hbm, tail_hbm,
    y_ref, out_ref,
    xs, ys, sv, sg2, sz, sg1, conv, dz, dh, act, cos, acc, share, sems,
):
    copies = [
        pltpu.make_async_copy(cos_hbm, cos, sems.at[0]),
        pltpu.make_async_copy(act_hbm, act.at[pl.ds(0, 2 * WIDTH)], sems.at[1]),
        pltpu.make_async_copy(tail_hbm, act.at[pl.ds(2 * WIDTH, PE_BLOCK)], sems.at[2]),
    ]
    for copy in copies:
        copy.start()
    xs[...] = x_ref[...].astype(F32)
    tables_f = (left_ref[...], right_ref[...], tc_ref[...], ts_ref[...])
    tables_i = (back_ref[...], inv_ref[...], tc_ref[...], ts_ref[...])
    pairs = range(CHANNELS // 2)

    def signal(kind, pair):
        return jnp.concatenate(
            [xs[pl.ds(kind * CHANNELS + 2 * pair + j, HALF_ROWS, stride=DATA), :] for j in range(2)], axis=1
        )

    def rows(pair):
        return slice(pair * 2 * KROWS, (pair + 1) * 2 * KROWS)

    def lanes(pair):
        return slice(pair * 2 * RADIX, (pair + 1) * 2 * RADIX)

    def emit(kind, pair, value):
        for j in range(2):
            ys[pl.ds(kind * CHANNELS + 2 * pair + j, HALF_ROWS, stride=SEND), :] = value[
                :, j * RADIX : (j + 1) * RADIX
            ]

    def emit_filter(o, pair, value):
        for j in range(2):
            dh[pl.ds(2 * (2 * pair + j) + o, HALF_ROWS, stride=ROWS), :] = value[:, j * RADIX : (j + 1) * RADIX]

    for p in pairs:
        sv[rows(p), :] = forward_pair(signal(0, p).astype(BF16), *tables_f)
    for p in pairs:
        sg2[rows(p), :] = forward_pair(signal(2, p).astype(BF16), *tables_f)
    for p in pairs:
        conv[:, lanes(p)] = inverse_pair(spectral_product(spec[0, rows(p), :], sv[rows(p), :], 1, 1), *tables_i)
    for p in pairs:
        dz[:, lanes(p)] = inverse_pair(spectral_product(spec[1, rows(p), :], sg2[rows(p), :], -1, 1), *tables_i)
    for p in pairs:
        gated = (signal(1, p) * conv[:, lanes(p)]).astype(BF16)
        sz[rows(p), :] = forward_pair(gated, *tables_f)
    for p in pairs:
        emit(1, p, dz[:, lanes(p)] * conv[:, lanes(p)])
        grad = (dz[:, lanes(p)] * signal(1, p)).astype(BF16)
        sg1[rows(p), :] = forward_pair(grad, *tables_f)
    for p in pairs:
        emit_filter(1, p, inverse_pair(spectral_product(sg2[rows(p), :], sz[rows(p), :], 1, -1), *tables_i))
    for p in pairs:
        emit_filter(0, p, inverse_pair(spectral_product(sg1[rows(p), :], sv[rows(p), :], 1, -1), *tables_i))
    for p in pairs:
        emit(0, p, inverse_pair(spectral_product(spec[1, rows(p), :], sz[rows(p), :], 1, 1), *tables_i))
    for p in pairs:
        emit(2, p, inverse_pair(spectral_product(spec[0, rows(p), :], sg1[rows(p), :], -1, 1), *tables_i))
    for copy in copies:
        copy.wait()

    acc[...] = jnp.zeros_like(acc)
    per = CHUNK // RADIX
    wide_rate = jnp.concatenate([rate_ref[...]] * per, axis=1)
    for step in range(SEQLEN // CHUNK):
        cols = slice(step * CHUNK, (step + 1) * CHUNK)
        wide = jnp.concatenate([dh[(step * per + i) * ROWS : (step * per + i + 1) * ROWS, :] for i in range(per)], axis=1)
        grad = (wide * (jnp.exp(-wide_rate * ramp_ref[:, cols]) * (1.0 / SEQLEN))).astype(BF16)
        low_two = (dot(own_ref[:WIDTH, :ROWS], grad) * cos[WIDTH:, cols].astype(F32)).astype(BF16)
        low_one = (dot(own_ref[WIDTH:, :WIDTH], low_two) * cos[:WIDTH, cols].astype(F32)).astype(BF16)
        acc[...] += dot_last(act[:, cols], jnp.concatenate([low_two, low_one, grad], axis=0))
    out_ref[...] = acc[WIDTH : 2 * WIDTH, 2 * WIDTH :].T
    half = WIDTH // 2
    tail = 2 * WIDTH
    share[:half, :WIDTH] = acc[:half, :WIDTH]
    share[:half, WIDTH:] = acc[half:WIDTH, :WIDTH]
    share[half:, :WIDTH] = acc[tail : tail + 24, WIDTH : 2 * WIDTH]
    share[half : half + 16, WIDTH:] = acc[tail + 24 : tail + 40, WIDTH : 2 * WIDTH]
    share[half + 16 :, WIDTH:] = acc[tail + 32 : tail + 40, :WIDTH]
    for i in range(HALF_ROWS):
        ys[i * SEND + DATA : (i + 1) * SEND, :] = share[...]
    y_ref[...] = ys[...].astype(BF16)


def finish_kernel(back_ref, cot_ref, value_ref, first_ref, second_ref, pos_ref, pos_bias_ref, mid_ref, mid_bias_ref, total):
    step = pl.program_id(0)
    value_ref[...] = back_ref[:, 2 * CHANNELS : DATA, :]
    first_ref[...] = back_ref[:, CHANNELS : 2 * CHANNELS, :]
    second_ref[...] = (cot_ref[...].astype(F32) * back_ref[:, :CHANNELS, :].astype(F32)).astype(BF16)
    part = jnp.sum(back_ref[:, DATA:, :].astype(F32), axis=0)

    @pl.when(step == 0)
    def _():
        total[...] = part

    @pl.when(step > 0)
    def _():
        total[...] += part

    @pl.when(step == pl.num_programs(0) - 1)
    def _():
        half = WIDTH // 2
        mid_ref[...] = jnp.concatenate([total[:half, :WIDTH], total[:half, WIDTH:]], axis=0).T
        pos_ref[:24, :] = total[half:, :WIDTH]
        pos_ref[24:, :] = total[half : half + PE - 24, WIDTH:]
        pos_bias_ref[...] = total[half + PE - 24 : half + PE - 23, WIDTH:]
        mid_bias_ref[...] = total[half + 17 : half + 18, WIDTH:]


def full(shape):
    return pl.BlockSpec(shape, lambda i: (0,) * len(shape))


def params(limit=VMEM_BYTES):
    return pltpu.CompilerParams(vmem_limit_bytes=limit)


def pack(value, first, second, cot):
    anywhere = pl.BlockSpec(memory_space=pltpu.HBM)
    buffer = pltpu.VMEM(value.shape, BF16)
    return pl.pallas_call(
        pack_kernel,
        in_specs=[anywhere] * 4,
        out_specs=anywhere,
        out_shape=jax.ShapeDtypeStruct((value.shape[0], DATA, RADIX), BF16),
        scratch_shapes=[buffer] * 3 + [pltpu.SemaphoreType.DMA((5,))],
        compiler_params=params(),
        cost_estimate=pl.CostEstimate(flops=1 << 17, bytes_accessed=1 << 20, transcendentals=0),
    )(value, first, second, cot)


def network_forward(pos_weight, pos_bias, mid_weight, mid_bias, out_weight, decay_rates, tables, stack, ramp):
    left, back, right, right_inv, twid_cos, twid_sin = tables
    block = pl.BlockSpec((2 * WIDTH, CHUNK), lambda i: (0, i))
    tabs = (left, right, twid_cos, twid_sin)
    args = (pos_weight.T, pos_bias[None, :], mid_weight, mid_bias[None, :], out_weight.T, decay_rates[None, :])
    outs = [
        jax.ShapeDtypeStruct((2 * WIDTH, SEQLEN), BF16),
        jax.ShapeDtypeStruct((2 * WIDTH, SEQLEN), BF16),
        jax.ShapeDtypeStruct((2, CHANNELS * KROWS, 2 * RADIX), F32),
        jax.ShapeDtypeStruct((2 * WIDTH, RADIX), BF16),
        jax.ShapeDtypeStruct((ROWS, RADIX), F32),
    ]
    return pl.pallas_call(
        network_kernel,
        grid=(SEQLEN // CHUNK,),
        in_specs=[block, pl.BlockSpec((1, CHUNK), lambda i: (0, i))]
        + [full(a.shape) for a in tabs]
        + [pl.BlockSpec(memory_space=pltpu.HBM)] * len(args),
        out_specs=[block] * 2 + [full(o.shape) for o in outs[2:]],
        out_shape=outs,
        scratch_shapes=[
            pltpu.VMEM((HALF_ROWS * ROWS, RADIX), F32),
            pltpu.VMEM((RADIX, RADIX), F32),
            pltpu.VMEM((2 * WIDTH, 2 * WIDTH), BF16),
            pltpu.VMEM((2 * WIDTH, 2 * WIDTH), BF16),
            pltpu.VMEM((2 * ROWS, 2 * WIDTH), BF16),
            pltpu.VMEM((WIDTH, RADIX), F32),
            pltpu.VMEM((ROWS, RADIX), F32),
        ]
        + [pltpu.VMEM(a.shape, F32) for a in args]
        + [pltpu.SemaphoreType.DMA((len(args),))],
        compiler_params=params(),
        cost_estimate=pl.CostEstimate(flops=1 << 30, bytes_accessed=10 << 20, transcendentals=1 << 20),
    )(stack, ramp, *tabs, *args)


def chain(x, net, tables, tail, ramp):
    act, cos, spec, own, own_rate = net
    left, back, right, right_inv, twid_cos, twid_sin = tables
    spectrum = pltpu.VMEM((CHANNELS * KROWS, 2 * RADIX), F32)
    wide = pltpu.VMEM((HALF_ROWS, CHANNELS * RADIX), F32)
    tall = 2 * WIDTH + PE_BLOCK
    anywhere = pl.BlockSpec(memory_space=pltpu.HBM)
    within = pl.BlockSpec(memory_space=pltpu.VMEM)
    return pl.pallas_call(
        chain_kernel,
        in_specs=[within] * 11 + [anywhere] * 3,
        out_specs=[within] * 2,
        out_shape=[
            jax.ShapeDtypeStruct((HALF_ROWS * SEND, RADIX), BF16),
            jax.ShapeDtypeStruct((ROWS, WIDTH), F32),
        ],
        scratch_shapes=[pltpu.VMEM(x.shape, F32), pltpu.VMEM((HALF_ROWS * SEND, RADIX), F32)]
        + [spectrum] * 4
        + [wide] * 2
        + [
            pltpu.VMEM((HALF_ROWS * ROWS, RADIX), F32),
            pltpu.VMEM((tall, SEQLEN), BF16),
            pltpu.VMEM((2 * WIDTH, SEQLEN), BF16),
            pltpu.VMEM((tall, 2 * WIDTH + ROWS), F32),
            pltpu.VMEM((SHARE, RADIX), F32),
            pltpu.SemaphoreType.DMA((3,)),
        ],
        compiler_params=params(CHAIN_BYTES),
        cost_estimate=pl.CostEstimate(flops=3 << 30, bytes_accessed=8 << 20, transcendentals=1 << 17),
    )(x, left, back, right, right_inv, twid_cos, twid_sin, own, own_rate, ramp, spec, act, cos, tail)


def finish(back, cot):
    devices = cot.shape[0]
    steps = 4
    data = pl.BlockSpec((devices // steps, CHANNELS, RADIX), lambda i: (i, 0, 0))
    outs = [jax.ShapeDtypeStruct(cot.shape, BF16)] * 3 + [
        jax.ShapeDtypeStruct((PE, WIDTH), F32),
        jax.ShapeDtypeStruct((1, WIDTH), F32),
        jax.ShapeDtypeStruct((WIDTH, WIDTH), F32),
        jax.ShapeDtypeStruct((1, WIDTH), F32),
    ]
    return pl.pallas_call(
        finish_kernel,
        grid=(steps,),
        in_specs=[pl.BlockSpec((devices // steps, SEND, RADIX), lambda i: (i, 0, 0)), data],
        out_specs=[data] * 3 + [full(o.shape) for o in outs[3:]],
        out_shape=outs,
        scratch_shapes=[pltpu.VMEM((SHARE, RADIX), F32)],
        compiler_params=params(),
        cost_estimate=pl.CostEstimate(flops=1 << 20, bytes_accessed=2 << 20, transcendentals=0),
    )(back, cot)


SEQ = ("z", "y", "x")


def on_device(
    value_branch, first_gate, second_gate, out_cotangent,
    pos_weight, pos_bias, mid_weight, mid_bias, out_weight, decay_rates,
):
    devices = lax.axis_size(SEQ)
    tables = dft_tables()
    stack, tail = feature_tables()
    ramp = (np.arange(SEQLEN) / SEQLEN).astype(np.float32)[None, :]
    blocks = (devices, CHANNELS, RADIX)
    cot = out_cotangent.reshape(blocks)
    sent = pack(value_branch.reshape(blocks), first_gate.reshape(blocks), second_gate.reshape(blocks), cot)
    x = lax.all_to_all(sent, SEQ, 0, 0, tiled=True)
    net = network_forward(
        pos_weight, pos_bias, mid_weight, mid_bias, out_weight, decay_rates, tables, stack, ramp
    )
    y, out_weight_grad = chain(x.reshape(HALF_ROWS * DATA, RADIX), net, tables, tail, ramp)
    back = lax.all_to_all(y.reshape(devices, SEND, RADIX), SEQ, 0, 0, tiled=True)
    value_grad, first_grad, second_grad, pos_grad, pos_bias_grad, mid_grad, mid_bias_grad = finish(back, cot)
    shape = value_branch.shape
    return (
        value_grad.reshape(shape),
        first_grad.reshape(shape),
        second_grad.reshape(shape),
        pos_grad.T,
        pos_bias_grad[0],
        mid_grad,
        mid_bias_grad[0],
        out_weight_grad,
    )


def solution(mesh):
    grid = Mesh(mesh.devices.reshape(mesh.shape["dp"], 2, 8, 4), ("dp",) + SEQ)
    part = P(None, ("dp",) + SEQ)
    in_specs = (part,) * 4 + (P(),) * 6
    out_specs = (part,) * 3 + (P("dp", None), P("dp"), P("dp", None), P("dp"), P(SEQ, "dp"))
    return jax.shard_map(on_device, mesh=grid, in_specs=in_specs, out_specs=out_specs, check_vma=False)
```

```python
import math

import jax
import jax.numpy as jnp
import numpy as np
from jax import lax
from jax.experimental import pallas as pl
from jax.experimental.pallas import tpu as pltpu
from jax.sharding import Mesh
from jax.sharding import PartitionSpec as P

F32 = jnp.float32
BF16 = jnp.bfloat16
RADIX = 128
HALF_ROWS = 64
SEQLEN = HALF_ROWS * RADIX
KROWS = 80
WIDTH = 64
PE = 33
PE_BLOCK = 40
CHUNK = 1024
NET_CHUNK = 4096
CHANNELS = 8
ROWS = 2 * CHANNELS
SHARE = 8
DATA = 3 * CHANNELS
SEND = DATA + SHARE
VMEM_BYTES = 60 << 20
CHAIN_BYTES = 60 << 20


def dft_tables():
    n1, n2 = 2 * HALF_ROWS, RADIX
    k1 = np.arange(KROWS)[:, None]
    live = (k1 <= n1 // 2).astype(np.float64)
    angle_one = 2.0 * np.pi * ((k1 * np.arange(n1 // 2)[None, :]) % n1) / n1
    cos_one = np.cos(angle_one) * live
    sin_one = np.sin(angle_one) * live
    left = np.concatenate([cos_one, -sin_one], axis=0)
    weight = np.where((k1 == 0) | (k1 == n1 // 2), 1.0, 2.0) / (n1 * n2)
    back = np.concatenate([cos_one * weight, -sin_one * weight], axis=0).T
    grid = np.arange(n2)
    angle_two = 2.0 * np.pi * ((grid[:, None] * grid[None, :]) % n2) / n2
    cos_two, sin_two = np.cos(angle_two), np.sin(angle_two)
    right = np.block([[cos_two, -sin_two], [sin_two, cos_two]])
    right_inv = np.block([[cos_two, sin_two], [-sin_two, cos_two]])
    angle_tw = 2.0 * np.pi * ((k1 * grid[None, :]) % (n1 * n2)) / (n1 * n2)
    bf = lambda a: np.asarray(a, np.float32).astype(jnp.bfloat16)
    return (
        bf(left),
        bf(back),
        bf(right),
        bf(right_inv),
        np.cos(angle_tw).astype(np.float32),
        np.sin(angle_tw).astype(np.float32),
    )


def features():
    positions = np.arange(SEQLEN)
    bands = np.arange(1, (PE - 1) // 2 + 1)
    angles = 2.0 * np.pi * ((bands[:, None] * positions[None, :]) % SEQLEN) / SEQLEN
    ramp = positions[None, :] / SEQLEN
    return np.concatenate([ramp, np.cos(angles), np.sin(angles)], axis=0).astype(np.float32)


def np_split(value, parts):
    pieces = []
    for _ in range(parts):
        piece = value.astype(jnp.bfloat16)
        pieces.append(piece)
        value = value - piece.astype(np.float32)
    return pieces


def feature_tables():
    table = np.zeros((PE_BLOCK, SEQLEN), np.float32)
    table[:PE] = features()
    table[PE] = 1.0
    pieces = np_split(table, 3)
    pad = np.zeros((2 * WIDTH - 3 * PE_BLOCK, SEQLEN), jnp.bfloat16)
    return np.concatenate(pieces + [pad], axis=0), pieces[0]


def poly_tables():
    top = math.pi**2 * 1.0001
    nodes = (np.cos(np.pi * (np.arange(64) + 0.5) / 64) + 1) * top / 2
    root = np.sqrt(nodes)
    cheb = np.polynomial.chebyshev.Chebyshev
    sin_fit = cheb.fit(nodes, math.sqrt(2) * np.sin(root / 2) / root, 4, domain=[0, top])
    cos_fit = cheb.fit(nodes, math.sqrt(2) * np.cos(root / 2), 4, domain=[0, top])
    to_poly = lambda c: [float(x) for x in c.convert(kind=np.polynomial.Polynomial).coef]
    return to_poly(sin_fit), to_poly(cos_fit)


SIN_COEF, COS_COEF = poly_tables()
TURN_HI = 6.28125
TURN_LO = float(np.float32(2 * math.pi - TURN_HI))


def sin_cos(value):
    turns = jnp.round(value * (0.5 / math.pi))
    rest = (value - turns * TURN_HI) - turns * TURN_LO
    square = rest * rest

    def horner(coefs):
        total = square * coefs[-1] + coefs[-2]
        for coef in coefs[-3::-1]:
            total = total * square + coef
        return total

    half = rest * horner(SIN_COEF)
    return half * horner(COS_COEF), 1.0 - half * half


def dot(left, right):
    return lax.dot_general(left, right, (((1,), (0,)), ((), ())), preferred_element_type=F32)


def dot_last(left, right):
    return lax.dot_general(left, right, (((1,), (1,)), ((), ())), preferred_element_type=F32)


def split_two(value):
    high = value.astype(BF16)
    return high, (value - high.astype(F32)).astype(BF16)


def forward_pair(signal, left, right, twid_cos, twid_sin):
    stacked = dot(left, signal)
    rows = []
    for j in range(2):
        cols = slice(j * RADIX, (j + 1) * RADIX)
        real_a, imag_a = stacked[:KROWS, cols], stacked[KROWS:, cols]
        real_b = (real_a * twid_cos + imag_a * twid_sin).astype(BF16)
        imag_b = (imag_a * twid_cos - real_a * twid_sin).astype(BF16)
        rows.append(jnp.concatenate([real_b, imag_b], axis=1))
    return dot(jnp.concatenate(rows, axis=0), right)


def inverse_pair(product, back, right_inv, twid_cos, twid_sin):
    section = dot(product, right_inv)
    cols = []
    for j in range(2):
        real_q = section[j * KROWS : (j + 1) * KROWS, :RADIX]
        imag_q = section[j * KROWS : (j + 1) * KROWS, RADIX:]
        real_r = (real_q * twid_cos - imag_q * twid_sin).astype(BF16)
        imag_r = (imag_q * twid_cos + real_q * twid_sin).astype(BF16)
        cols.append(jnp.concatenate([real_r, imag_r], axis=0))
    return dot(back, jnp.concatenate(cols, axis=1))


def spectral_product(left, right, sign_left, sign_right):
    left_re, left_im = left[:, :RADIX], left[:, RADIX:]
    right_re, right_im = right[:, :RADIX], right[:, RADIX:]
    cross = left_im * right_im
    real = left_re * right_re + cross if sign_left * sign_right < 0 else left_re * right_re - cross
    one, two = left_im * right_re, left_re * right_im
    if sign_left > 0:
        imag = one + two if sign_right > 0 else one - two
    else:
        imag = two - one
    return jnp.concatenate([real.astype(BF16), imag.astype(BF16)], axis=1)


def pack_kernel(v_hbm, x1_hbm, x2_hbm, cot_hbm, out_hbm, v, x1, x2, cot, sent, sems):
    loads = [
        pltpu.make_async_copy(src, dst, sems.at[i])
        for i, (src, dst) in enumerate(((v_hbm, v), (x1_hbm, x1), (x2_hbm, x2), (cot_hbm, cot)))
    ]
    for copy in loads:
        copy.start()
    for copy in loads:
        copy.wait()
    sent[:, :CHANNELS, :] = v[...]
    sent[:, CHANNELS : 2 * CHANNELS, :] = x1[...]
    sent[:, 2 * CHANNELS :, :] = (cot[...].astype(F32) * x2[...].astype(F32)).astype(BF16)
    last = pltpu.make_async_copy(sent, out_hbm, sems.at[4])
    last.start()
    last.wait()


def network_kernel(
    pe_ref, ramp_ref, left_ref, right_ref, tc_ref, ts_ref,
    pos_ref, pos_bias_ref, mid_ref, mid_bias_ref, out_ref, rate_ref,
    act_ref, cos_ref, spec_ref, own_ref, own_rate_ref,
    filt, square, wp, wm, wo, bias, decay,
):
    step = pl.program_id(0)

    @pl.when(step == 0)
    def _():
        rank = lax.axis_index(SEQ)
        lane = pl.multiple_of(rank // 8 * RADIX, RADIX)
        first = pl.multiple_of(rank % 8 * ROWS, ROWS)

        square[...] = jnp.zeros_like(square)
        for i in range(3):
            square[i * PE_BLOCK : i * PE_BLOCK + PE, :WIDTH] = pos_ref[...]
            square[i * PE_BLOCK + PE : i * PE_BLOCK + PE + 1, :WIDTH] = pos_bias_ref[...]
        wp[...] = jnp.concatenate(split_two(square[...].T[:WIDTH, :]), axis=0)

        square[...] = jnp.zeros_like(square)
        square[:WIDTH, :WIDTH] = mid_ref[...]
        own_ref[WIDTH:, :] = square[...].T[:WIDTH, :].astype(BF16)
        square[:WIDTH, WIDTH:] = mid_ref[...]
        wm[...] = jnp.concatenate(split_two(square[:WIDTH, :]), axis=0)

        square[:, :WIDTH] = jnp.broadcast_to(mid_bias_ref[...], (RADIX, WIDTH))
        bias[...] = square[...].T[:WIDTH, :]

        square[...] = jnp.broadcast_to(rate_ref[:, pl.ds(lane, RADIX)], (RADIX, RADIX)).T
        decay[...] = square[pl.ds(first, ROWS), :]
        own_rate_ref[...] = decay[...]

        block = out_ref[:, pl.ds(lane, RADIX)]
        square[...] = jnp.concatenate([block, block], axis=0).T
        mine = square[pl.ds(first, ROWS), :]
        wo[...] = jnp.concatenate(split_two(mine), axis=0)
        square[...] = jnp.zeros_like(square)
        square[:ROWS, :] = mine
        own_ref[:WIDTH, :] = square[...].T[:WIDTH, :].astype(BF16)

    span = 256
    parts = [slice(p * span, (p + 1) * span) for p in range(NET_CHUNK // span)]
    wide_bias = jnp.concatenate([bias[...]] * (span // RADIX), axis=1)
    wide_rate = jnp.concatenate([decay[...]] * (span // RADIX), axis=1)
    pres = []
    for cols in parts:
        both = dot(wp[...], pe_ref[:, cols])
        pres.append(both[:WIDTH] + both[WIDTH:])
    stacks = []
    for pre, cols in zip(pres, parts):
        act, slope = sin_cos(pre)
        pieces = split_two(act)
        act_ref[:WIDTH, cols] = pieces[0]
        cos_ref[:WIDTH, cols] = slope.astype(BF16)
        stacks.append(jnp.concatenate(pieces, axis=0))
    pres = []
    for stack in stacks:
        both = dot(wm[...], stack)
        pres.append(both[:WIDTH] + both[WIDTH:] + wide_bias)
    stacks = []
    for pre, cols in zip(pres, parts):
        act, slope = sin_cos(pre)
        pieces = split_two(act)
        act_ref[WIDTH:, cols] = pieces[0]
        cos_ref[WIDTH:, cols] = slope.astype(BF16)
        stacks.append(jnp.concatenate(pieces, axis=0))
    for part, (stack, cols) in enumerate(zip(stacks, parts)):
        both = dot(wo[...], stack)
        rows = (both[:ROWS] + both[ROWS:]) * jnp.exp(-wide_rate * ramp_ref[:, cols])
        for j in range(span // RADIX):
            base = pl.multiple_of(step * (NET_CHUNK // RADIX * ROWS) + (part * (span // RADIX) + j) * ROWS, ROWS)
            filt[pl.ds(base, ROWS), :] = rows[:, j * RADIX : (j + 1) * RADIX]

    @pl.when(step == SEQLEN // NET_CHUNK - 1)
    def _():
        for o in range(2):
            for pair in range(CHANNELS // 2):
                signal = jnp.concatenate(
                    [filt[pl.ds(2 * (2 * pair + j) + o, HALF_ROWS, stride=ROWS), :] for j in range(2)], axis=1
                ).astype(BF16)
                spec_ref[o, pair * 2 * KROWS : (pair + 1) * 2 * KROWS, :] = forward_pair(
                    signal, left_ref[...], right_ref[...], tc_ref[...], ts_ref[...]
                )


def chain_kernel(
    x_ref, left_ref, back_ref, right_ref, inv_ref, tc_ref, ts_ref, own_ref, rate_ref, ramp_ref,
    spec, act_hbm, cos_hbm, tail_hbm,
    y_ref, out_ref,
    xs, ys, sv, sg2, sz, sg1, conv, dz, dh, act, cos, acc, share, sems,
):
    copies = [
        pltpu.make_async_copy(cos_hbm, cos, sems.at[0]),
        pltpu.make_async_copy(act_hbm, act.at[pl.ds(0, 2 * WIDTH)], sems.at[1]),
        pltpu.make_async_copy(tail_hbm, act.at[pl.ds(2 * WIDTH, PE_BLOCK)], sems.at[2]),
    ]
    for copy in copies:
        copy.start()
    xs[...] = x_ref[...].astype(F32)
    tables_f = (left_ref[...], right_ref[...], tc_ref[...], ts_ref[...])
    tables_i = (back_ref[...], inv_ref[...], tc_ref[...], ts_ref[...])
    pairs = range(CHANNELS // 2)

    def signal(kind, pair):
        return jnp.concatenate(
            [xs[pl.ds(kind * CHANNELS + 2 * pair + j, HALF_ROWS, stride=DATA), :] for j in range(2)], axis=1
        )

    def rows(pair):
        return slice(pair * 2 * KROWS, (pair + 1) * 2 * KROWS)

    def lanes(pair):
        return slice(pair * 2 * RADIX, (pair + 1) * 2 * RADIX)

    def emit(kind, pair, value):
        for j in range(2):
            ys[pl.ds(kind * CHANNELS + 2 * pair + j, HALF_ROWS, stride=SEND), :] = value[
                :, j * RADIX : (j + 1) * RADIX
            ]

    def emit_filter(o, pair, value):
        for j in range(2):
            dh[pl.ds(2 * (2 * pair + j) + o, HALF_ROWS, stride=ROWS), :] = value[:, j * RADIX : (j + 1) * RADIX]

    for p in pairs:
        sv[rows(p), :] = forward_pair(signal(0, p).astype(BF16), *tables_f)
    for p in pairs:
        sg2[rows(p), :] = forward_pair(signal(2, p).astype(BF16), *tables_f)
    for p in pairs:
        conv[:, lanes(p)] = inverse_pair(spectral_product(spec[0, rows(p), :], sv[rows(p), :], 1, 1), *tables_i)
    for p in pairs:
        dz[:, lanes(p)] = inverse_pair(spectral_product(spec[1, rows(p), :], sg2[rows(p), :], -1, 1), *tables_i)
    for p in pairs:
        gated = (signal(1, p) * conv[:, lanes(p)]).astype(BF16)
        sz[rows(p), :] = forward_pair(gated, *tables_f)
    for p in pairs:
        emit(1, p, dz[:, lanes(p)] * conv[:, lanes(p)])
        grad = (dz[:, lanes(p)] * signal(1, p)).astype(BF16)
        sg1[rows(p), :] = forward_pair(grad, *tables_f)
    for p in pairs:
        emit_filter(1, p, inverse_pair(spectral_product(sg2[rows(p), :], sz[rows(p), :], 1, -1), *tables_i))
    for p in pairs:
        emit_filter(0, p, inverse_pair(spectral_product(sg1[rows(p), :], sv[rows(p), :], 1, -1), *tables_i))
    for p in pairs:
        emit(0, p, inverse_pair(spectral_product(spec[1, rows(p), :], sz[rows(p), :], 1, 1), *tables_i))
    for p in pairs:
        emit(2, p, inverse_pair(spectral_product(spec[0, rows(p), :], sg1[rows(p), :], -1, 1), *tables_i))
    for copy in copies:
        copy.wait()

    acc[...] = jnp.zeros_like(acc)
    per = CHUNK // RADIX
    wide_rate = jnp.concatenate([rate_ref[...]] * per, axis=1)
    for step in range(SEQLEN // CHUNK):
        cols = slice(step * CHUNK, (step + 1) * CHUNK)
        wide = jnp.concatenate([dh[(step * per + i) * ROWS : (step * per + i + 1) * ROWS, :] for i in range(per)], axis=1)
        grad = (wide * (jnp.exp(-wide_rate * ramp_ref[:, cols]) * (1.0 / SEQLEN))).astype(BF16)
        low_two = (dot(own_ref[:WIDTH, :ROWS], grad) * cos[WIDTH:, cols].astype(F32)).astype(BF16)
        low_one = (dot(own_ref[WIDTH:, :WIDTH], low_two) * cos[:WIDTH, cols].astype(F32)).astype(BF16)
        acc[...] += dot_last(act[:, cols], jnp.concatenate([low_two, low_one, grad], axis=0))
    out_ref[...] = acc[WIDTH : 2 * WIDTH, 2 * WIDTH :].T
    tail = 2 * WIDTH
    share[...] = jnp.zeros_like(share)
    share[:, :WIDTH] = acc[:WIDTH, :WIDTH]
    share[:PE_BLOCK, WIDTH:] = acc[tail:, WIDTH : 2 * WIDTH]
    share[PE_BLOCK : PE_BLOCK + 8, WIDTH:] = acc[tail + 32 :, :WIDTH]
    for i in range(HALF_ROWS):
        group = i // 4 % 8
        ys[i * SEND + DATA : (i + 1) * SEND, :] = share[group * SHARE : (group + 1) * SHARE, :]
    y_ref[...] = ys[...].astype(BF16)


def total_kernel(back_hbm, out_ref, shares, sem):
    copy = pltpu.make_async_copy(back_hbm.at[:, pl.ds(DATA, SHARE), :], shares, sem)
    copy.start()
    copy.wait()
    total = jnp.sum(shares[...].astype(F32), axis=0)
    out_ref[...] = jnp.broadcast_to(total[None], out_ref.shape)


def finish_kernel(back_ref, cot_ref, value_ref, first_ref, second_ref):
    value_ref[...] = back_ref[:, 2 * CHANNELS : DATA, :]
    first_ref[...] = back_ref[:, CHANNELS : 2 * CHANNELS, :]
    second_ref[...] = (cot_ref[...].astype(F32) * back_ref[:, :CHANNELS, :].astype(F32)).astype(BF16)


def inner_kernel(total_ref, pos_ref, pos_bias_ref, mid_ref, mid_bias_ref):
    mid_ref[...] = total_ref[...].T[:WIDTH, :]
    pos_ref[...] = total_ref[:PE, WIDTH:]
    pos_bias_ref[...] = total_ref[PE : PE + 1, WIDTH:]
    mid_bias_ref[...] = total_ref[PE_BLOCK + 1 : PE_BLOCK + 2, WIDTH:]


def full(shape):
    return pl.BlockSpec(shape, lambda i: (0,) * len(shape))


def params(limit=VMEM_BYTES):
    return pltpu.CompilerParams(vmem_limit_bytes=limit)


def pack(value, first, second, cot):
    anywhere = pl.BlockSpec(memory_space=pltpu.HBM)
    buffer = pltpu.VMEM(value.shape, BF16)
    return pl.pallas_call(
        pack_kernel,
        in_specs=[anywhere] * 4,
        out_specs=anywhere,
        out_shape=jax.ShapeDtypeStruct((value.shape[0], DATA, RADIX), BF16),
        scratch_shapes=[buffer] * 4 + [pltpu.VMEM((value.shape[0], DATA, RADIX), BF16), pltpu.SemaphoreType.DMA((5,))],
        compiler_params=params(),
        cost_estimate=pl.CostEstimate(flops=1 << 17, bytes_accessed=1 << 20, transcendentals=0),
    )(value, first, second, cot)


def network_forward(pos_weight, pos_bias, mid_weight, mid_bias, out_weight, decay_rates, tables, stack, ramp):
    left, back, right, right_inv, twid_cos, twid_sin = tables
    block = pl.BlockSpec((2 * WIDTH, NET_CHUNK), lambda i: (0, i))
    tabs = (left, right, twid_cos, twid_sin)
    args = (pos_weight.T, pos_bias[None, :], mid_weight, mid_bias[None, :], out_weight.T, decay_rates[None, :])
    outs = [
        jax.ShapeDtypeStruct((2 * WIDTH, SEQLEN), BF16),
        jax.ShapeDtypeStruct((2 * WIDTH, SEQLEN), BF16),
        jax.ShapeDtypeStruct((2, CHANNELS * KROWS, 2 * RADIX), F32),
        jax.ShapeDtypeStruct((2 * WIDTH, RADIX), BF16),
        jax.ShapeDtypeStruct((ROWS, RADIX), F32),
    ]
    return pl.pallas_call(
        network_kernel,
        grid=(SEQLEN // NET_CHUNK,),
        in_specs=[block, pl.BlockSpec((1, NET_CHUNK), lambda i: (0, i))]
        + [full(a.shape) for a in tabs]
        + [full(a.shape) for a in args],
        out_specs=[block] * 2 + [full(o.shape) for o in outs[2:]],
        out_shape=outs,
        scratch_shapes=[
            pltpu.VMEM((HALF_ROWS * ROWS, RADIX), F32),
            pltpu.VMEM((RADIX, RADIX), F32),
            pltpu.VMEM((2 * WIDTH, 2 * WIDTH), BF16),
            pltpu.VMEM((2 * WIDTH, 2 * WIDTH), BF16),
            pltpu.VMEM((2 * ROWS, 2 * WIDTH), BF16),
            pltpu.VMEM((WIDTH, RADIX), F32),
            pltpu.VMEM((ROWS, RADIX), F32),
        ],
        compiler_params=params(),
        cost_estimate=pl.CostEstimate(flops=1 << 30, bytes_accessed=10 << 20, transcendentals=1 << 20),
    )(stack, ramp, *tabs, *args)


def chain(x, net, tables, tail, ramp):
    act, cos, spec, own, own_rate = net
    left, back, right, right_inv, twid_cos, twid_sin = tables
    spectrum = pltpu.VMEM((CHANNELS * KROWS, 2 * RADIX), F32)
    wide = pltpu.VMEM((HALF_ROWS, CHANNELS * RADIX), F32)
    tall = 2 * WIDTH + PE_BLOCK
    anywhere = pl.BlockSpec(memory_space=pltpu.HBM)
    within = pl.BlockSpec(memory_space=pltpu.VMEM)
    return pl.pallas_call(
        chain_kernel,
        in_specs=[within] * 11 + [anywhere] * 3,
        out_specs=[within] * 2,
        out_shape=[
            jax.ShapeDtypeStruct((HALF_ROWS * SEND, RADIX), BF16),
            jax.ShapeDtypeStruct((ROWS, WIDTH), F32),
        ],
        scratch_shapes=[pltpu.VMEM(x.shape, F32), pltpu.VMEM((HALF_ROWS * SEND, RADIX), F32)]
        + [spectrum] * 4
        + [wide] * 2
        + [
            pltpu.VMEM((HALF_ROWS * ROWS, RADIX), F32),
            pltpu.VMEM((tall, SEQLEN), BF16),
            pltpu.VMEM((2 * WIDTH, SEQLEN), BF16),
            pltpu.VMEM((tall, 2 * WIDTH + ROWS), F32),
            pltpu.VMEM((WIDTH, RADIX), F32),
            pltpu.SemaphoreType.DMA((3,)),
        ],
        compiler_params=params(CHAIN_BYTES),
        cost_estimate=pl.CostEstimate(flops=3 << 30, bytes_accessed=8 << 20, transcendentals=1 << 17),
    )(x, left, back, right, right_inv, twid_cos, twid_sin, own, own_rate, ramp, spec, act, cos, tail)


def share_total(back, peers):
    return pl.pallas_call(
        total_kernel,
        in_specs=[pl.BlockSpec(memory_space=pltpu.HBM)],
        out_specs=pl.BlockSpec(memory_space=pltpu.VMEM),
        out_shape=jax.ShapeDtypeStruct((peers, SHARE, RADIX), F32),
        scratch_shapes=[pltpu.VMEM((back.shape[0], SHARE, RADIX), BF16), pltpu.SemaphoreType.DMA(())],
        compiler_params=params(),
        cost_estimate=pl.CostEstimate(flops=1 << 16, bytes_accessed=1 << 17, transcendentals=0),
    )(back)


def finish(back, cot):
    devices = cot.shape[0]
    steps = 2
    data = pl.BlockSpec((devices // steps, CHANNELS, RADIX), lambda i: (i, 0, 0))
    return pl.pallas_call(
        finish_kernel,
        grid=(steps,),
        in_specs=[pl.BlockSpec((devices // steps, SEND, RADIX), lambda i: (i, 0, 0)), data],
        out_specs=[data] * 3,
        out_shape=[jax.ShapeDtypeStruct(cot.shape, BF16)] * 3,
        compiler_params=params(),
        cost_estimate=pl.CostEstimate(flops=1 << 17, bytes_accessed=1 << 20, transcendentals=0),
    )(back, cot)


def inner_gradients(total):
    within = pl.BlockSpec(memory_space=pltpu.VMEM)
    return pl.pallas_call(
        inner_kernel,
        in_specs=[within],
        out_specs=[within] * 4,
        out_shape=[
            jax.ShapeDtypeStruct((PE, WIDTH), F32),
            jax.ShapeDtypeStruct((1, WIDTH), F32),
            jax.ShapeDtypeStruct((WIDTH, WIDTH), F32),
            jax.ShapeDtypeStruct((1, WIDTH), F32),
        ],
        compiler_params=params(),
        cost_estimate=pl.CostEstimate(flops=1 << 13, bytes_accessed=1 << 16, transcendentals=0),
    )(total)


SEQ = ("z", "y", "x")


def on_device(
    value_branch, first_gate, second_gate, out_cotangent,
    pos_weight, pos_bias, mid_weight, mid_bias, out_weight, decay_rates,
):
    devices = lax.axis_size(SEQ)
    tables = dft_tables()
    stack, tail = feature_tables()
    ramp = (np.arange(SEQLEN) / SEQLEN).astype(np.float32)[None, :]
    blocks = (devices, CHANNELS, RADIX)
    cot = out_cotangent.reshape(blocks)
    sent = pack(value_branch.reshape(blocks), first_gate.reshape(blocks), second_gate.reshape(blocks), cot)
    x = lax.all_to_all(sent, SEQ, 0, 0, tiled=True)
    net = network_forward(
        pos_weight, pos_bias, mid_weight, mid_bias, out_weight, decay_rates, tables, stack, ramp
    )
    y, out_weight_grad = chain(x.reshape(HALF_ROWS * DATA, RADIX), net, tables, tail, ramp)
    back = lax.all_to_all(y.reshape(devices, SEND, RADIX), SEQ, 0, 0, tiled=True)
    total = share_total(back, lax.axis_size("y"))
    total = lax.all_to_all(total, "y", 0, 0, tiled=True)
    value_grad, first_grad, second_grad = finish(back, cot)
    pos_grad, pos_bias_grad, mid_grad, mid_bias_grad = inner_gradients(total.reshape(WIDTH, RADIX))
    shape = value_branch.shape
    return (
        value_grad.reshape(shape),
        first_grad.reshape(shape),
        second_grad.reshape(shape),
        pos_grad.T,
        pos_bias_grad[0],
        mid_grad,
        mid_bias_grad[0],
        out_weight_grad,
    )


def solution(mesh):
    grid = Mesh(mesh.devices.reshape(mesh.shape["dp"], 2, 8, 4), ("dp",) + SEQ)
    part = P(None, ("dp",) + SEQ)
    in_specs = (part,) * 4 + (P(),) * 6
    out_specs = (part,) * 3 + (P("dp", None), P("dp"), P("dp", None), P("dp"), P(SEQ, "dp"))
    return jax.shard_map(on_device, mesh=grid, in_specs=in_specs, out_specs=out_specs, check_vma=False)
```

```python
import math

import jax
import jax.numpy as jnp
import numpy as np
from jax import lax
from jax.experimental import pallas as pl
from jax.experimental.pallas import tpu as pltpu
from jax.sharding import Mesh
from jax.sharding import PartitionSpec as P

F32 = jnp.float32
BF16 = jnp.bfloat16
RADIX = 128
HALF_ROWS = 64
SEQLEN = HALF_ROWS * RADIX
KROWS = 80
WIDTH = 64
PE = 33
PE_BLOCK = 40
CHUNK = 1024
NET_CHUNK = 2048
CHANNELS = 8
ROWS = 2 * CHANNELS
SHARE = 8
DATA = 3 * CHANNELS
SEND = DATA + SHARE
VMEM_BYTES = 64 << 20
CHAIN_BYTES = 64 << 20


def dft_tables():
    n1, n2 = 2 * HALF_ROWS, RADIX
    k1 = np.arange(KROWS)[:, None]
    live = (k1 <= n1 // 2).astype(np.float64)
    angle_one = 2.0 * np.pi * ((k1 * np.arange(n1 // 2)[None, :]) % n1) / n1
    cos_one = np.cos(angle_one) * live
    sin_one = np.sin(angle_one) * live
    left = np.concatenate([cos_one, -sin_one], axis=0)
    weight = np.where((k1 == 0) | (k1 == n1 // 2), 1.0, 2.0) / (n1 * n2)
    back = np.concatenate([cos_one * weight, -sin_one * weight], axis=0).T
    grid = np.arange(n2)
    angle_two = 2.0 * np.pi * ((grid[:, None] * grid[None, :]) % n2) / n2
    cos_two, sin_two = np.cos(angle_two), np.sin(angle_two)
    right = np.block([[cos_two, -sin_two], [sin_two, cos_two]])
    right_inv = np.block([[cos_two, sin_two], [-sin_two, cos_two]])
    angle_tw = 2.0 * np.pi * ((k1 * grid[None, :]) % (n1 * n2)) / (n1 * n2)
    bf = lambda a: np.asarray(a, np.float32).astype(jnp.bfloat16)
    return (
        bf(left),
        bf(back),
        bf(right),
        bf(right_inv),
        np.cos(angle_tw).astype(np.float32),
        np.sin(angle_tw).astype(np.float32),
    )


def features():
    positions = np.arange(SEQLEN)
    bands = np.arange(1, (PE - 1) // 2 + 1)
    angles = 2.0 * np.pi * ((bands[:, None] * positions[None, :]) % SEQLEN) / SEQLEN
    ramp = positions[None, :] / SEQLEN
    return np.concatenate([ramp, np.cos(angles), np.sin(angles)], axis=0).astype(np.float32)


def np_split(value, parts):
    pieces = []
    for _ in range(parts):
        piece = value.astype(jnp.bfloat16)
        pieces.append(piece)
        value = value - piece.astype(np.float32)
    return pieces


def feature_tables():
    table = np.zeros((PE_BLOCK, SEQLEN), np.float32)
    table[:PE] = features()
    table[PE] = 1.0
    pieces = np_split(table, 3)
    pad = np.zeros((2 * WIDTH - 3 * PE_BLOCK, SEQLEN), jnp.bfloat16)
    return np.concatenate(pieces + [pad], axis=0), pieces[0]


def poly_tables():
    top = math.pi**2 * 1.0001
    nodes = (np.cos(np.pi * (np.arange(64) + 0.5) / 64) + 1) * top / 2
    root = np.sqrt(nodes)
    cheb = np.polynomial.chebyshev.Chebyshev
    sin_fit = cheb.fit(nodes, math.sqrt(2) * np.sin(root / 2) / root, 4, domain=[0, top])
    cos_fit = cheb.fit(nodes, math.sqrt(2) * np.cos(root / 2), 4, domain=[0, top])
    to_poly = lambda c: [float(x) for x in c.convert(kind=np.polynomial.Polynomial).coef]
    return to_poly(sin_fit), to_poly(cos_fit)


SIN_COEF, COS_COEF = poly_tables()
TURN_HI = 6.28125
TURN_LO = float(np.float32(2 * math.pi - TURN_HI))


def sin_cos(value):
    turns = jnp.round(value * (0.5 / math.pi))
    rest = (value - turns * TURN_HI) - turns * TURN_LO
    square = rest * rest

    def horner(coefs):
        total = square * coefs[-1] + coefs[-2]
        for coef in coefs[-3::-1]:
            total = total * square + coef
        return total

    half = rest * horner(SIN_COEF)
    return half * horner(COS_COEF), 1.0 - half * half


def dot(left, right):
    return lax.dot_general(left, right, (((1,), (0,)), ((), ())), preferred_element_type=F32)


def dot_last(left, right):
    return lax.dot_general(left, right, (((1,), (1,)), ((), ())), preferred_element_type=F32)


def split_two(value):
    high = value.astype(BF16)
    return high, (value - high.astype(F32)).astype(BF16)


def forward_pair(signal, left, right, twid_cos, twid_sin):
    stacked = dot(left, signal)
    rows = []
    for j in range(2):
        cols = slice(j * RADIX, (j + 1) * RADIX)
        real_a, imag_a = stacked[:KROWS, cols], stacked[KROWS:, cols]
        real_b = (real_a * twid_cos + imag_a * twid_sin).astype(BF16)
        imag_b = (imag_a * twid_cos - real_a * twid_sin).astype(BF16)
        rows.append(jnp.concatenate([real_b, imag_b], axis=1))
    return dot(jnp.concatenate(rows, axis=0), right)


def inverse_pair(product, back, right_inv, twid_cos, twid_sin):
    section = dot(product, right_inv)
    cols = []
    for j in range(2):
        real_q = section[j * KROWS : (j + 1) * KROWS, :RADIX]
        imag_q = section[j * KROWS : (j + 1) * KROWS, RADIX:]
        real_r = (real_q * twid_cos - imag_q * twid_sin).astype(BF16)
        imag_r = (imag_q * twid_cos + real_q * twid_sin).astype(BF16)
        cols.append(jnp.concatenate([real_r, imag_r], axis=0))
    return dot(back, jnp.concatenate(cols, axis=1))


def spectral_product(left, right, sign_left, sign_right):
    left_re, left_im = left[:, :RADIX], left[:, RADIX:]
    right_re, right_im = right[:, :RADIX], right[:, RADIX:]
    cross = left_im * right_im
    real = left_re * right_re + cross if sign_left * sign_right < 0 else left_re * right_re - cross
    one, two = left_im * right_re, left_re * right_im
    if sign_left > 0:
        imag = one + two if sign_right > 0 else one - two
    else:
        imag = two - one
    return jnp.concatenate([real.astype(BF16), imag.astype(BF16)], axis=1)


def pack_kernel(v_hbm, x1_hbm, x2_hbm, cot_hbm, out_hbm, v, x1, x2, cot, sent, sems):
    loads = [
        pltpu.make_async_copy(src, dst, sems.at[i])
        for i, (src, dst) in enumerate(((v_hbm, v), (x1_hbm, x1), (x2_hbm, x2), (cot_hbm, cot)))
    ]
    for copy in loads:
        copy.start()
    for copy in loads:
        copy.wait()
    sent[:, :CHANNELS, :] = v[...]
    sent[:, CHANNELS : 2 * CHANNELS, :] = x1[...]
    sent[:, 2 * CHANNELS :, :] = (cot[...].astype(F32) * x2[...].astype(F32)).astype(BF16)
    last = pltpu.make_async_copy(sent, out_hbm, sems.at[4])
    last.start()
    last.wait()


def network_kernel(
    pe_ref, ramp_ref, left_ref, right_ref, tc_ref, ts_ref,
    pos_ref, pos_bias_ref, mid_ref, mid_bias_ref, out_ref, rate_ref,
    act_ref, cos_ref, spec_ref, own_ref, own_rate_ref,
    filt, square, wp, wm, wo, bias, decay,
):
    step = pl.program_id(0)

    @pl.when(step == 0)
    def _():
        rank = lax.axis_index(SEQ)
        lane = pl.multiple_of(rank // 8 * RADIX, RADIX)
        first = pl.multiple_of(rank % 8 * ROWS, ROWS)

        square[...] = jnp.zeros_like(square)
        for i in range(3):
            square[i * PE_BLOCK : i * PE_BLOCK + PE, :WIDTH] = pos_ref[...]
            square[i * PE_BLOCK + PE : i * PE_BLOCK + PE + 1, :WIDTH] = pos_bias_ref[...]
        wp[...] = jnp.concatenate(split_two(square[...].T[:WIDTH, :]), axis=0)

        square[...] = jnp.zeros_like(square)
        square[:WIDTH, :WIDTH] = mid_ref[...]
        own_ref[WIDTH:, :] = square[...].T[:WIDTH, :].astype(BF16)
        square[:WIDTH, WIDTH:] = mid_ref[...]
        wm[...] = jnp.concatenate(split_two(square[:WIDTH, :]), axis=0)

        square[:, :WIDTH] = jnp.broadcast_to(mid_bias_ref[...], (RADIX, WIDTH))
        bias[...] = square[...].T[:WIDTH, :]

        square[...] = jnp.broadcast_to(rate_ref[:, pl.ds(lane, RADIX)], (RADIX, RADIX)).T
        decay[...] = square[pl.ds(first, ROWS), :]
        own_rate_ref[...] = decay[...]

        block = out_ref[:, pl.ds(lane, RADIX)]
        square[...] = jnp.concatenate([block, block], axis=0).T
        mine = square[pl.ds(first, ROWS), :]
        wo[...] = jnp.concatenate(split_two(mine), axis=0)
        square[...] = jnp.zeros_like(square)
        square[:ROWS, :] = mine
        own_ref[:WIDTH, :] = square[...].T[:WIDTH, :].astype(BF16)

    span = 256
    parts = [slice(p * span, (p + 1) * span) for p in range(NET_CHUNK // span)]
    wide_bias = jnp.concatenate([bias[...]] * (span // RADIX), axis=1)
    wide_rate = jnp.concatenate([decay[...]] * (span // RADIX), axis=1)
    pres = []
    for cols in parts:
        both = dot(wp[...], pe_ref[:, cols])
        pres.append(both[:WIDTH] + both[WIDTH:])
    stacks = []
    for pre, cols in zip(pres, parts):
        act, slope = sin_cos(pre)
        pieces = split_two(act)
        act_ref[:WIDTH, cols] = pieces[0]
        cos_ref[:WIDTH, cols] = slope.astype(BF16)
        stacks.append(jnp.concatenate(pieces, axis=0))
    pres = []
    for stack in stacks:
        both = dot(wm[...], stack)
        pres.append(both[:WIDTH] + both[WIDTH:] + wide_bias)
    stacks = []
    for pre, cols in zip(pres, parts):
        act, slope = sin_cos(pre)
        pieces = split_two(act)
        act_ref[WIDTH:, cols] = pieces[0]
        cos_ref[WIDTH:, cols] = slope.astype(BF16)
        stacks.append(jnp.concatenate(pieces, axis=0))
    for part, (stack, cols) in enumerate(zip(stacks, parts)):
        both = dot(wo[...], stack)
        rows = (both[:ROWS] + both[ROWS:]) * jnp.exp(-wide_rate * ramp_ref[:, cols])
        for j in range(span // RADIX):
            base = pl.multiple_of(step * (NET_CHUNK // RADIX * ROWS) + (part * (span // RADIX) + j) * ROWS, ROWS)
            filt[pl.ds(base, ROWS), :] = rows[:, j * RADIX : (j + 1) * RADIX]

    @pl.when(step == SEQLEN // NET_CHUNK - 1)
    def _():
        for o in range(2):
            for pair in range(CHANNELS // 2):
                signal = jnp.concatenate(
                    [filt[pl.ds(2 * (2 * pair + j) + o, HALF_ROWS, stride=ROWS), :] for j in range(2)], axis=1
                ).astype(BF16)
                spec_ref[o, pair * 2 * KROWS : (pair + 1) * 2 * KROWS, :] = forward_pair(
                    signal, left_ref[...], right_ref[...], tc_ref[...], ts_ref[...]
                )


def chain_kernel(
    x_ref, left_ref, back_ref, right_ref, inv_ref, tc_ref, ts_ref, own_ref, rate_ref, ramp_ref,
    spec, act_hbm, cos_hbm, tail_hbm,
    y_ref, out_ref,
    xs, ys, sv, sg2, sz, sg1, conv, dz, dh, act, cos, acc, share, sems,
):
    copies = [
        pltpu.make_async_copy(cos_hbm, cos, sems.at[0]),
        pltpu.make_async_copy(act_hbm, act.at[pl.ds(0, 2 * WIDTH)], sems.at[1]),
        pltpu.make_async_copy(tail_hbm, act.at[pl.ds(2 * WIDTH, PE_BLOCK)], sems.at[2]),
    ]
    for copy in copies:
        copy.start()
    xs[...] = x_ref[...].astype(F32)
    tables_f = (left_ref[...], right_ref[...], tc_ref[...], ts_ref[...])
    tables_i = (back_ref[...], inv_ref[...], tc_ref[...], ts_ref[...])
    pairs = range(CHANNELS // 2)

    def signal(kind, pair):
        return jnp.concatenate(
            [xs[pl.ds(kind * CHANNELS + 2 * pair + j, HALF_ROWS, stride=DATA), :] for j in range(2)], axis=1
        )

    def rows(pair):
        return slice(pair * 2 * KROWS, (pair + 1) * 2 * KROWS)

    def lanes(pair):
        return slice(pair * 2 * RADIX, (pair + 1) * 2 * RADIX)

    def emit(kind, pair, value):
        for j in range(2):
            ys[pl.ds(kind * CHANNELS + 2 * pair + j, HALF_ROWS, stride=SEND), :] = value[
                :, j * RADIX : (j + 1) * RADIX
            ]

    def emit_filter(o, pair, value):
        for j in range(2):
            dh[pl.ds(2 * (2 * pair + j) + o, HALF_ROWS, stride=ROWS), :] = value[:, j * RADIX : (j + 1) * RADIX]

    for p in pairs:
        sv[rows(p), :] = forward_pair(signal(0, p).astype(BF16), *tables_f)
    for p in pairs:
        sg2[rows(p), :] = forward_pair(signal(2, p).astype(BF16), *tables_f)
    for p in pairs:
        conv[:, lanes(p)] = inverse_pair(spectral_product(spec[0, rows(p), :], sv[rows(p), :], 1, 1), *tables_i)
    for p in pairs:
        dz[:, lanes(p)] = inverse_pair(spectral_product(spec[1, rows(p), :], sg2[rows(p), :], -1, 1), *tables_i)
    for p in pairs:
        gated = (signal(1, p) * conv[:, lanes(p)]).astype(BF16)
        sz[rows(p), :] = forward_pair(gated, *tables_f)
    for p in pairs:
        emit(1, p, dz[:, lanes(p)] * conv[:, lanes(p)])
        grad = (dz[:, lanes(p)] * signal(1, p)).astype(BF16)
        sg1[rows(p), :] = forward_pair(grad, *tables_f)
    for p in pairs:
        emit_filter(1, p, inverse_pair(spectral_product(sg2[rows(p), :], sz[rows(p), :], 1, -1), *tables_i))
    for p in pairs:
        emit_filter(0, p, inverse_pair(spectral_product(sg1[rows(p), :], sv[rows(p), :], 1, -1), *tables_i))
    for p in pairs:
        emit(0, p, inverse_pair(spectral_product(spec[1, rows(p), :], sz[rows(p), :], 1, 1), *tables_i))
    for p in pairs:
        emit(2, p, inverse_pair(spectral_product(spec[0, rows(p), :], sg1[rows(p), :], -1, 1), *tables_i))
    for copy in copies:
        copy.wait()

    acc[...] = jnp.zeros_like(acc)
    per = CHUNK // RADIX
    wide_rate = jnp.concatenate([rate_ref[...]] * per, axis=1)
    for step in range(SEQLEN // CHUNK):
        cols = slice(step * CHUNK, (step + 1) * CHUNK)
        wide = jnp.concatenate([dh[(step * per + i) * ROWS : (step * per + i + 1) * ROWS, :] for i in range(per)], axis=1)
        grad = (wide * (jnp.exp(-wide_rate * ramp_ref[:, cols]) * (1.0 / SEQLEN))).astype(BF16)
        low_two = (dot(own_ref[:WIDTH, :ROWS], grad) * cos[WIDTH:, cols].astype(F32)).astype(BF16)
        low_one = (dot(own_ref[WIDTH:, :WIDTH], low_two) * cos[:WIDTH, cols].astype(F32)).astype(BF16)
        acc[...] += dot_last(act[:, cols], jnp.concatenate([low_two, low_one, grad], axis=0))
    out_ref[...] = acc[WIDTH : 2 * WIDTH, 2 * WIDTH :].T
    tail = 2 * WIDTH
    share[...] = jnp.zeros_like(share)
    share[:, :WIDTH] = acc[:WIDTH, :WIDTH]
    share[:PE_BLOCK, WIDTH:] = acc[tail:, WIDTH : 2 * WIDTH]
    share[PE_BLOCK : PE_BLOCK + 8, WIDTH:] = acc[tail + 32 :, :WIDTH]
    for i in range(HALF_ROWS):
        group = i % 8
        ys[i * SEND + DATA : (i + 1) * SEND, :] = share[group * SHARE : (group + 1) * SHARE, :]
    y_ref[...] = ys[...].astype(BF16)


def total_kernel(back_hbm, out_ref, shares, sem):
    copy = pltpu.make_async_copy(back_hbm.at[:, pl.ds(DATA, SHARE), :], shares, sem)
    copy.start()
    copy.wait()
    total = jnp.sum(shares[...].astype(F32), axis=0)
    out_ref[...] = jnp.broadcast_to(total[None], out_ref.shape)


def finish_kernel(back_ref, cot_ref, value_ref, first_ref, second_ref):
    value_ref[...] = back_ref[:, 2 * CHANNELS : DATA, :]
    first_ref[...] = back_ref[:, CHANNELS : 2 * CHANNELS, :]
    second_ref[...] = (cot_ref[...].astype(F32) * back_ref[:, :CHANNELS, :].astype(F32)).astype(BF16)


def inner_kernel(total_ref, pos_ref, pos_bias_ref, mid_ref, mid_bias_ref):
    mid_ref[...] = total_ref[...].T[:WIDTH, :]
    pos_ref[...] = total_ref[:PE, WIDTH:]
    pos_bias_ref[...] = total_ref[PE : PE + 1, WIDTH:]
    mid_bias_ref[...] = total_ref[PE_BLOCK + 1 : PE_BLOCK + 2, WIDTH:]


def full(shape):
    return pl.BlockSpec(shape, lambda i: (0,) * len(shape))


def params(limit=VMEM_BYTES):
    return pltpu.CompilerParams(vmem_limit_bytes=limit)


def pack(value, first, second, cot):
    anywhere = pl.BlockSpec(memory_space=pltpu.HBM)
    buffer = pltpu.VMEM(value.shape, BF16)
    return pl.pallas_call(
        pack_kernel,
        in_specs=[anywhere] * 4,
        out_specs=anywhere,
        out_shape=jax.ShapeDtypeStruct((value.shape[0], DATA, RADIX), BF16),
        scratch_shapes=[buffer] * 4 + [pltpu.VMEM((value.shape[0], DATA, RADIX), BF16), pltpu.SemaphoreType.DMA((5,))],
        compiler_params=params(),
        cost_estimate=pl.CostEstimate(flops=1 << 17, bytes_accessed=1 << 20, transcendentals=0),
    )(value, first, second, cot)


def network_forward(pos_weight, pos_bias, mid_weight, mid_bias, out_weight, decay_rates, tables, stack, ramp):
    left, back, right, right_inv, twid_cos, twid_sin = tables
    block = pl.BlockSpec((2 * WIDTH, NET_CHUNK), lambda i: (0, i))
    tabs = (left, right, twid_cos, twid_sin)
    args = (pos_weight.T, pos_bias[None, :], mid_weight, mid_bias[None, :], out_weight.T, decay_rates[None, :])
    outs = [
        jax.ShapeDtypeStruct((2 * WIDTH, SEQLEN), BF16),
        jax.ShapeDtypeStruct((2 * WIDTH, SEQLEN), BF16),
        jax.ShapeDtypeStruct((2, CHANNELS * KROWS, 2 * RADIX), F32),
        jax.ShapeDtypeStruct((2 * WIDTH, RADIX), BF16),
        jax.ShapeDtypeStruct((ROWS, RADIX), F32),
    ]
    return pl.pallas_call(
        network_kernel,
        grid=(SEQLEN // NET_CHUNK,),
        in_specs=[block, pl.BlockSpec((1, NET_CHUNK), lambda i: (0, i))]
        + [full(a.shape) for a in tabs]
        + [full(a.shape) for a in args],
        out_specs=[block] * 2 + [full(o.shape) for o in outs[2:]],
        out_shape=outs,
        scratch_shapes=[
            pltpu.VMEM((HALF_ROWS * ROWS, RADIX), F32),
            pltpu.VMEM((RADIX, RADIX), F32),
            pltpu.VMEM((2 * WIDTH, 2 * WIDTH), BF16),
            pltpu.VMEM((2 * WIDTH, 2 * WIDTH), BF16),
            pltpu.VMEM((2 * ROWS, 2 * WIDTH), BF16),
            pltpu.VMEM((WIDTH, RADIX), F32),
            pltpu.VMEM((ROWS, RADIX), F32),
        ],
        compiler_params=params(),
        cost_estimate=pl.CostEstimate(flops=1 << 30, bytes_accessed=10 << 20, transcendentals=1 << 20),
    )(stack, ramp, *tabs, *args)


def chain(x, net, tables, tail, ramp):
    act, cos, spec, own, own_rate = net
    left, back, right, right_inv, twid_cos, twid_sin = tables
    spectrum = pltpu.VMEM((CHANNELS * KROWS, 2 * RADIX), F32)
    wide = pltpu.VMEM((HALF_ROWS, CHANNELS * RADIX), F32)
    tall = 2 * WIDTH + PE_BLOCK
    anywhere = pl.BlockSpec(memory_space=pltpu.HBM)
    within = pl.BlockSpec(memory_space=pltpu.VMEM)
    return pl.pallas_call(
        chain_kernel,
        in_specs=[within] * 11 + [anywhere] * 3,
        out_specs=[within] * 2,
        out_shape=[
            jax.ShapeDtypeStruct((HALF_ROWS * SEND, RADIX), BF16),
            jax.ShapeDtypeStruct((ROWS, WIDTH), F32),
        ],
        scratch_shapes=[pltpu.VMEM(x.shape, F32), pltpu.VMEM((HALF_ROWS * SEND, RADIX), F32)]
        + [spectrum] * 4
        + [wide] * 2
        + [
            pltpu.VMEM((HALF_ROWS * ROWS, RADIX), F32),
            pltpu.VMEM((tall, SEQLEN), BF16),
            pltpu.VMEM((2 * WIDTH, SEQLEN), BF16),
            pltpu.VMEM((tall, 2 * WIDTH + ROWS), F32),
            pltpu.VMEM((WIDTH, RADIX), F32),
            pltpu.SemaphoreType.DMA((3,)),
        ],
        compiler_params=params(CHAIN_BYTES),
        cost_estimate=pl.CostEstimate(flops=3 << 30, bytes_accessed=8 << 20, transcendentals=1 << 17),
    )(x, left, back, right, right_inv, twid_cos, twid_sin, own, own_rate, ramp, spec, act, cos, tail)


def share_total(back, peers):
    return pl.pallas_call(
        total_kernel,
        in_specs=[pl.BlockSpec(memory_space=pltpu.HBM)],
        out_specs=pl.BlockSpec(memory_space=pltpu.VMEM),
        out_shape=jax.ShapeDtypeStruct((peers, SHARE, RADIX), F32),
        scratch_shapes=[pltpu.VMEM((back.shape[0], SHARE, RADIX), BF16), pltpu.SemaphoreType.DMA(())],
        compiler_params=params(),
        cost_estimate=pl.CostEstimate(flops=1 << 16, bytes_accessed=1 << 17, transcendentals=0),
    )(back)


def finish(back, cot):
    devices = cot.shape[0]
    steps = 2
    data = pl.BlockSpec((devices // steps, CHANNELS, RADIX), lambda i: (i, 0, 0))
    return pl.pallas_call(
        finish_kernel,
        grid=(steps,),
        in_specs=[pl.BlockSpec((devices // steps, SEND, RADIX), lambda i: (i, 0, 0)), data],
        out_specs=[data] * 3,
        out_shape=[jax.ShapeDtypeStruct(cot.shape, BF16)] * 3,
        compiler_params=params(),
        cost_estimate=pl.CostEstimate(flops=1 << 17, bytes_accessed=1 << 20, transcendentals=0),
    )(back, cot)


def inner_gradients(total):
    within = pl.BlockSpec(memory_space=pltpu.VMEM)
    return pl.pallas_call(
        inner_kernel,
        in_specs=[within],
        out_specs=[within] * 4,
        out_shape=[
            jax.ShapeDtypeStruct((PE, WIDTH), F32),
            jax.ShapeDtypeStruct((1, WIDTH), F32),
            jax.ShapeDtypeStruct((WIDTH, WIDTH), F32),
            jax.ShapeDtypeStruct((1, WIDTH), F32),
        ],
        compiler_params=params(2 << 20),
        cost_estimate=pl.CostEstimate(flops=1 << 13, bytes_accessed=1 << 16, transcendentals=0),
    )(total)


SEQ = ("z", "yhi", "ylo", "x")
NEAR = ("ylo", "x")


def on_device(
    value_branch, first_gate, second_gate, out_cotangent,
    pos_weight, pos_bias, mid_weight, mid_bias, out_weight, decay_rates,
):
    devices = lax.axis_size(SEQ)
    tables = dft_tables()
    stack, tail = feature_tables()
    ramp = (np.arange(SEQLEN) / SEQLEN).astype(np.float32)[None, :]
    blocks = (devices, CHANNELS, RADIX)
    cot = out_cotangent.reshape(blocks)
    sent = pack(value_branch.reshape(blocks), first_gate.reshape(blocks), second_gate.reshape(blocks), cot)
    x = lax.all_to_all(sent, SEQ, 0, 0, tiled=True)
    net = network_forward(
        pos_weight, pos_bias, mid_weight, mid_bias, out_weight, decay_rates, tables, stack, ramp
    )
    y, out_weight_grad = chain(x.reshape(HALF_ROWS * DATA, RADIX), net, tables, tail, ramp)
    back = lax.all_to_all(y.reshape(devices, SEND, RADIX), SEQ, 0, 0, tiled=True)
    total = share_total(back, lax.axis_size(NEAR))
    total = lax.all_to_all(total, NEAR, 0, 0, tiled=True)
    value_grad, first_grad, second_grad = finish(back, cot)
    pos_grad, pos_bias_grad, mid_grad, mid_bias_grad = inner_gradients(total.reshape(WIDTH, RADIX))
    shape = value_branch.shape
    return (
        value_grad.reshape(shape),
        first_grad.reshape(shape),
        second_grad.reshape(shape),
        pos_grad.T,
        pos_bias_grad[0],
        mid_grad,
        mid_bias_grad[0],
        out_weight_grad,
    )


def solution(mesh):
    grid = Mesh(mesh.devices.reshape(mesh.shape["dp"], 2, 4, 2, 4), ("dp",) + SEQ)
    part = P(None, ("dp",) + SEQ)
    in_specs = (part,) * 4 + (P(),) * 6
    out_specs = (part,) * 3 + (P("dp", None), P("dp"), P("dp", None), P("dp"), P(SEQ, "dp"))
    return jax.shard_map(on_device, mesh=grid, in_specs=in_specs, out_specs=out_specs, check_vma=False)
```

```python
import math

import jax
import jax.numpy as jnp
import numpy as np
from jax import lax
from jax.experimental import pallas as pl
from jax.experimental.pallas import tpu as pltpu
from jax.sharding import Mesh
from jax.sharding import PartitionSpec as P

F32 = jnp.float32
BF16 = jnp.bfloat16
RADIX = 128
HALF_ROWS = 64
SEQLEN = HALF_ROWS * RADIX
KROWS = 72
WIDTH = 64
PE = 33
PE_BLOCK = 40
NET_CHUNK = 2048
CHANNELS = 8
ROWS = 2 * CHANNELS
SHARE = 8
DATA = 3 * CHANNELS
SEND = DATA + SHARE
PACK_PARTS = 2
VMEM_BYTES = 64 << 20
CHAIN_BYTES = 64 << 20


def dft_tables():
    n1, n2 = 2 * HALF_ROWS, RADIX
    k1 = np.arange(KROWS)[:, None]
    live = (k1 <= n1 // 2).astype(np.float64)
    angle_one = 2.0 * np.pi * ((k1 * np.arange(n1 // 2)[None, :]) % n1) / n1
    cos_one = np.cos(angle_one) * live
    sin_one = np.sin(angle_one) * live
    left = np.concatenate([cos_one, -sin_one], axis=0)
    weight = np.where((k1 == 0) | (k1 == n1 // 2), 1.0, 2.0) / (n1 * n2)
    back = np.concatenate([cos_one * weight, -sin_one * weight], axis=0).T
    grid = np.arange(n2)
    angle_two = 2.0 * np.pi * ((grid[:, None] * grid[None, :]) % n2) / n2
    cos_two, sin_two = np.cos(angle_two), np.sin(angle_two)
    right = np.block([[cos_two, -sin_two], [sin_two, cos_two]])
    right_inv = np.block([[cos_two, sin_two], [-sin_two, cos_two]])
    angle_tw = 2.0 * np.pi * ((k1 * grid[None, :]) % (n1 * n2)) / (n1 * n2)
    bf = lambda a: np.asarray(a, np.float32).astype(jnp.bfloat16)
    return (
        bf(left),
        bf(back),
        bf(right),
        bf(right_inv),
        np.cos(angle_tw).astype(np.float32),
        np.sin(angle_tw).astype(np.float32),
    )


def features():
    positions = np.arange(SEQLEN)
    bands = np.arange(1, (PE - 1) // 2 + 1)
    angles = 2.0 * np.pi * ((bands[:, None] * positions[None, :]) % SEQLEN) / SEQLEN
    ramp = positions[None, :] / SEQLEN
    return np.concatenate([ramp, np.cos(angles), np.sin(angles)], axis=0).astype(np.float32)


def np_split(value, parts):
    pieces = []
    for _ in range(parts):
        piece = value.astype(jnp.bfloat16)
        pieces.append(piece)
        value = value - piece.astype(np.float32)
    return pieces


def feature_tables():
    table = np.zeros((PE_BLOCK, SEQLEN), np.float32)
    table[:PE] = features()
    table[PE] = 1.0
    pieces = np_split(table, 3)
    pad = np.zeros((2 * WIDTH - 3 * PE_BLOCK, SEQLEN), jnp.bfloat16)
    return np.concatenate(pieces + [pad], axis=0), pieces[0]


def poly_tables():
    top = math.pi**2 * 1.0001
    nodes = (np.cos(np.pi * (np.arange(64) + 0.5) / 64) + 1) * top / 2
    root = np.sqrt(nodes)
    cheb = np.polynomial.chebyshev.Chebyshev
    sin_fit = cheb.fit(nodes, math.sqrt(2) * np.sin(root / 2) / root, 4, domain=[0, top])
    cos_fit = cheb.fit(nodes, math.sqrt(2) * np.cos(root / 2), 4, domain=[0, top])
    to_poly = lambda c: [float(x) for x in c.convert(kind=np.polynomial.Polynomial).coef]
    return to_poly(sin_fit), to_poly(cos_fit)


SIN_COEF, COS_COEF = poly_tables()
TURN_HI = 6.28125
TURN_LO = float(np.float32(2 * math.pi - TURN_HI))


def sin_cos(value):
    turns = jnp.round(value * (0.5 / math.pi))
    rest = (value - turns * TURN_HI) - turns * TURN_LO
    square = rest * rest

    def horner(coefs):
        total = square * coefs[-1] + coefs[-2]
        for coef in coefs[-3::-1]:
            total = total * square + coef
        return total

    half = rest * horner(SIN_COEF)
    return half * horner(COS_COEF), 1.0 - half * half


def dot(left, right):
    return lax.dot_general(left, right, (((1,), (0,)), ((), ())), preferred_element_type=F32)


def dot_last(left, right):
    return lax.dot_general(left, right, (((1,), (1,)), ((), ())), preferred_element_type=F32)


def split_two(value):
    high = value.astype(BF16)
    return high, (value - high.astype(F32)).astype(BF16)


def forward_pair(signal, left, right, twid_cos, twid_sin):
    stacked = dot(left, signal)
    rows = []
    for j in range(2):
        cols = slice(j * RADIX, (j + 1) * RADIX)
        real_a, imag_a = stacked[:KROWS, cols], stacked[KROWS:, cols]
        real_b = real_a * twid_cos + imag_a * twid_sin
        imag_b = imag_a * twid_cos - real_a * twid_sin
        rows.append(jnp.concatenate([real_b, imag_b], axis=1))
    return dot(jnp.concatenate(rows, axis=0).astype(BF16), right)


def inverse_pair(product, back, right_inv, twid_cos, twid_sin):
    section = dot(product, right_inv)
    cols = []
    for j in range(2):
        real_q = section[j * KROWS : (j + 1) * KROWS, :RADIX]
        imag_q = section[j * KROWS : (j + 1) * KROWS, RADIX:]
        real_r = real_q * twid_cos - imag_q * twid_sin
        imag_r = imag_q * twid_cos + real_q * twid_sin
        cols.append(jnp.concatenate([real_r, imag_r], axis=0))
    return dot(back, jnp.concatenate(cols, axis=1).astype(BF16))


def spectral_product(left, right, sign_left, sign_right):
    left_re, left_im = left[:, :RADIX], left[:, RADIX:]
    right_re, right_im = right[:, :RADIX], right[:, RADIX:]
    cross = left_im * right_im
    real = left_re * right_re + cross if sign_left * sign_right < 0 else left_re * right_re - cross
    one, two = left_im * right_re, left_re * right_im
    if sign_left > 0:
        imag = one + two if sign_right > 0 else one - two
    else:
        imag = two - one
    return jnp.concatenate([real.astype(BF16), imag.astype(BF16)], axis=1)


def pack_kernel(v_hbm, x1_hbm, x2_hbm, cot_hbm, out_hbm, x2, cot, sent, sems):
    size = x2.shape[0] // PACK_PARTS
    spans = [pl.ds(i * size, size) for i in range(PACK_PARTS)]
    loads, stores = [], []
    for i, span in enumerate(spans):
        moves = (
            (v_hbm.at[span], sent.at[span, pl.ds(0, CHANNELS)]),
            (x1_hbm.at[span], sent.at[span, pl.ds(CHANNELS, CHANNELS)]),
            (x2_hbm.at[span], x2.at[span]),
            (cot_hbm.at[span], cot.at[span]),
        )
        loads.append([pltpu.make_async_copy(src, dst, sems.at[5 * i + j]) for j, (src, dst) in enumerate(moves)])
        for copy in loads[-1]:
            copy.start()
    for i, span in enumerate(spans):
        for copy in loads[i]:
            copy.wait()
        sent[span, 2 * CHANNELS :, :] = (cot[span].astype(F32) * x2[span].astype(F32)).astype(BF16)
        stores.append(pltpu.make_async_copy(sent.at[span], out_hbm.at[span], sems.at[5 * i + 4]))
        stores[-1].start()
    for copy in stores:
        copy.wait()


def network_kernel(
    pe_ref, ramp_ref, left_ref, right_ref, tc_ref, ts_ref,
    pos_ref, pos_bias_ref, mid_ref, mid_bias_ref, out_ref, rate_ref,
    act_ref, cos_ref, spec_ref, own_ref, own_rate_ref,
    filt, square, wp, wm, wo, bias, decay,
):
    step = pl.program_id(0)

    @pl.when(step == 0)
    def _():
        rank = lax.axis_index(SEQ)
        lane = pl.multiple_of(rank // 8 * RADIX, RADIX)
        first = pl.multiple_of(rank % 8 * ROWS, ROWS)

        square[...] = jnp.zeros_like(square)
        for i in range(3):
            square[i * PE_BLOCK : i * PE_BLOCK + PE, :WIDTH] = pos_ref[...]
            square[i * PE_BLOCK + PE : i * PE_BLOCK + PE + 1, :WIDTH] = pos_bias_ref[...]
        wp[...] = jnp.concatenate(split_two(square[...].T[:WIDTH, :]), axis=0)

        square[...] = jnp.zeros_like(square)
        square[:WIDTH, :WIDTH] = mid_ref[...]
        own_ref[WIDTH:, :] = square[...].T[:WIDTH, :].astype(BF16)
        square[:WIDTH, WIDTH:] = mid_ref[...]
        wm[...] = jnp.concatenate(split_two(square[:WIDTH, :]), axis=0)

        square[:, :WIDTH] = jnp.broadcast_to(mid_bias_ref[...], (RADIX, WIDTH))
        bias[...] = square[...].T[:WIDTH, :]

        square[...] = jnp.broadcast_to(rate_ref[:, pl.ds(lane, RADIX)], (RADIX, RADIX)).T
        decay[...] = square[pl.ds(first, ROWS), :]
        own_rate_ref[...] = decay[...]

        block = out_ref[:, pl.ds(lane, RADIX)]
        square[...] = jnp.concatenate([block, block], axis=0).T
        mine = square[pl.ds(first, ROWS), :]
        wo[...] = jnp.concatenate(split_two(mine), axis=0)
        square[...] = jnp.zeros_like(square)
        square[:ROWS, :] = mine
        own_ref[:WIDTH, :] = square[...].T[:WIDTH, :].astype(BF16)

    span = 256
    parts = [slice(p * span, (p + 1) * span) for p in range(NET_CHUNK // span)]
    wide_bias = jnp.concatenate([bias[...]] * (span // RADIX), axis=1)
    wide_rate = jnp.concatenate([decay[...]] * (span // RADIX), axis=1)
    pres = []
    for cols in parts:
        both = dot(wp[...], pe_ref[:, cols])
        pres.append(both[:WIDTH] + both[WIDTH:])
    stacks = []
    for pre, cols in zip(pres, parts):
        act, slope = sin_cos(pre)
        pieces = split_two(act)
        act_ref[:WIDTH, cols] = pieces[0]
        cos_ref[:WIDTH, cols] = slope.astype(BF16)
        stacks.append(jnp.concatenate(pieces, axis=0))
    pres = []
    for stack in stacks:
        both = dot(wm[...], stack)
        pres.append(both[:WIDTH] + both[WIDTH:] + wide_bias)
    stacks = []
    for pre, cols in zip(pres, parts):
        act, slope = sin_cos(pre)
        pieces = split_two(act)
        act_ref[WIDTH:, cols] = pieces[0]
        cos_ref[WIDTH:, cols] = slope.astype(BF16)
        stacks.append(jnp.concatenate(pieces, axis=0))
    for part, (stack, cols) in enumerate(zip(stacks, parts)):
        both = dot(wo[...], stack)
        rows = (both[:ROWS] + both[ROWS:]) * jnp.exp(-wide_rate * ramp_ref[:, cols])
        for j in range(span // RADIX):
            base = pl.multiple_of(step * (NET_CHUNK // RADIX * ROWS) + (part * (span // RADIX) + j) * ROWS, ROWS)
            filt[pl.ds(base, ROWS), :] = rows[:, j * RADIX : (j + 1) * RADIX]

    @pl.when(step == SEQLEN // NET_CHUNK - 1)
    def _():
        for o in range(2):
            for pair in range(CHANNELS // 2):
                signal = jnp.concatenate(
                    [filt[pl.ds(2 * (2 * pair + j) + o, HALF_ROWS, stride=ROWS), :] for j in range(2)], axis=1
                ).astype(BF16)
                spec_ref[o, pair * 2 * KROWS : (pair + 1) * 2 * KROWS, :] = forward_pair(
                    signal, left_ref[...], right_ref[...], tc_ref[...], ts_ref[...]
                )


def chain_kernel(
    x_hbm, left_hbm, back_hbm, right_hbm, inv_hbm, tc_hbm, ts_hbm, own_hbm, rate_hbm, ramp_hbm,
    spec_hbm, act_hbm, cos_hbm, tail_hbm,
    y_hbm, out_ref,
    x_ref, left_ref, back_ref, right_ref, inv_ref, tc_ref, ts_ref, own_ref, rate_ref, ramp_ref,
    xs, ys, sv, sg2, sz, sg1, conv, dz, dh, spec, act, cos, stat, acc, share, data, parts, sems,
):
    sources = (x_hbm, left_hbm, right_hbm, tc_hbm, ts_hbm, back_hbm, inv_hbm, own_hbm, rate_hbm, ramp_hbm)
    targets = (x_ref, left_ref, right_ref, tc_ref, ts_ref, back_ref, inv_ref, own_ref, rate_ref, ramp_ref)
    small = [pltpu.make_async_copy(s, d, sems.at[6 + i]) for i, (s, d) in enumerate(zip(sources, targets))]
    for copy in small:
        copy.start()
    first_load = pltpu.make_async_copy(spec_hbm, spec, sems.at[0])
    loads = [
        pltpu.make_async_copy(cos_hbm, cos, sems.at[1]),
        pltpu.make_async_copy(act_hbm, act.at[pl.ds(0, 2 * WIDTH)], sems.at[2]),
        pltpu.make_async_copy(tail_hbm, act.at[pl.ds(2 * WIDTH, PE_BLOCK)], sems.at[3]),
    ]
    first_load.start()
    for copy in loads:
        copy.start()
    for copy in small[:5]:
        copy.wait()
    xs[...] = x_ref[...].astype(F32)
    tables_f = (left_ref[...], right_ref[...], tc_ref[...], ts_ref[...])
    pairs = range(CHANNELS // 2)

    def signal(kind, pair):
        return jnp.concatenate(
            [xs[pl.ds(kind * CHANNELS + 2 * pair + j, HALF_ROWS, stride=DATA), :] for j in range(2)], axis=1
        )

    def rows(pair):
        return slice(pair * 2 * KROWS, (pair + 1) * 2 * KROWS)

    def lanes(pair):
        return slice(pair * 2 * RADIX, (pair + 1) * 2 * RADIX)

    def emit(kind, pair, value):
        for j in range(2):
            ys[pl.ds(kind * CHANNELS + 2 * pair + j, HALF_ROWS, stride=DATA), :] = value[
                :, j * RADIX : (j + 1) * RADIX
            ]

    def emit_filter(o, pair, value):
        for j in range(2):
            dh[pl.ds(2 * (2 * pair + j) + o, HALF_ROWS, stride=ROWS), :] = value[:, j * RADIX : (j + 1) * RADIX]

    for p in pairs:
        sv[rows(p), :] = forward_pair(signal(0, p).astype(BF16), *tables_f)
    for p in pairs:
        sg2[rows(p), :] = forward_pair(signal(2, p).astype(BF16), *tables_f)
    first_load.wait()
    for copy in small[5:]:
        copy.wait()
    tables_i = (back_ref[...], inv_ref[...], tc_ref[...], ts_ref[...])
    for p in pairs:
        conv[:, lanes(p)] = inverse_pair(spectral_product(spec[0, rows(p), :], sv[rows(p), :], 1, 1), *tables_i)
    for p in pairs:
        dz[:, lanes(p)] = inverse_pair(spectral_product(spec[1, rows(p), :], sg2[rows(p), :], -1, 1), *tables_i)
    for p in pairs:
        gated = (signal(1, p) * conv[:, lanes(p)]).astype(BF16)
        sz[rows(p), :] = forward_pair(gated, *tables_f)
    for p in pairs:
        emit(1, p, dz[:, lanes(p)] * conv[:, lanes(p)])
        grad = (dz[:, lanes(p)] * signal(1, p)).astype(BF16)
        sg1[rows(p), :] = forward_pair(grad, *tables_f)
    for p in pairs:
        emit_filter(1, p, inverse_pair(spectral_product(sg2[rows(p), :], sz[rows(p), :], 1, -1), *tables_i))
    for p in pairs:
        emit_filter(0, p, inverse_pair(spectral_product(sg1[rows(p), :], sv[rows(p), :], 1, -1), *tables_i))
    for p in pairs:
        emit(0, p, inverse_pair(spectral_product(spec[1, rows(p), :], sz[rows(p), :], 1, 1), *tables_i))
    for p in pairs:
        emit(2, p, inverse_pair(spectral_product(spec[0, rows(p), :], sg1[rows(p), :], -1, 1), *tables_i))
    for i in range(HALF_ROWS):
        data[i] = ys[i * DATA : (i + 1) * DATA, :].astype(BF16)
    stores = [pltpu.make_async_copy(data, y_hbm.at[:, pl.ds(0, DATA), :], sems.at[4])]
    stores[0].start()

    span = 256
    columns = [slice(i * span, (i + 1) * span) for i in range(SEQLEN // span)]
    wide_rate = jnp.concatenate([rate_ref[...]] * (span // RADIX), axis=1)
    for cols in columns:
        first = cols.start // RADIX
        wide = jnp.concatenate([dh[(first + i) * ROWS : (first + i + 1) * ROWS, :] for i in range(span // RADIX)], axis=1)
        grad = wide * (jnp.exp(-wide_rate * ramp_ref[:, cols]) * (1.0 / SEQLEN))
        stat[2 * WIDTH :, cols] = grad.astype(BF16)
    for copy in loads:
        copy.wait()
    for cols in columns:
        stat[:WIDTH, cols] = (dot(own_ref[:WIDTH, :ROWS], stat[2 * WIDTH :, cols]) * cos[WIDTH:, cols].astype(F32)).astype(BF16)
    for cols in columns:
        stat[WIDTH : 2 * WIDTH, cols] = (
            dot(own_ref[WIDTH:, :WIDTH], stat[:WIDTH, cols]) * cos[:WIDTH, cols].astype(F32)
        ).astype(BF16)
    acc[...] = dot_last(act[...], stat[...])
    out_ref[...] = acc[WIDTH : 2 * WIDTH, 2 * WIDTH :].T
    tail = 2 * WIDTH
    share[...] = jnp.zeros_like(share)
    share[:, :WIDTH] = acc[:WIDTH, :WIDTH]
    share[:PE_BLOCK, WIDTH:] = acc[tail:, WIDTH : 2 * WIDTH]
    share[PE_BLOCK : PE_BLOCK + 8, WIDTH:] = acc[tail + 32 :, :WIDTH]
    for i in range(HALF_ROWS):
        group = i % 8
        parts[i] = share[group * SHARE : (group + 1) * SHARE, :].astype(BF16)
    stores.append(pltpu.make_async_copy(parts, y_hbm.at[:, pl.ds(DATA, SHARE), :], sems.at[5]))
    stores[1].start()
    for copy in stores:
        copy.wait()


def total_kernel(back_hbm, out_ref, shares, sem):
    copy = pltpu.make_async_copy(back_hbm.at[:, pl.ds(DATA, SHARE), :], shares, sem)
    copy.start()
    copy.wait()
    total = jnp.sum(shares[...].astype(F32), axis=0)
    out_ref[...] = jnp.broadcast_to(total[None], out_ref.shape)


def finish_kernel(back_ref, cot_ref, value_ref, first_ref, second_ref):
    value_ref[...] = back_ref[:, 2 * CHANNELS : DATA, :]
    first_ref[...] = back_ref[:, CHANNELS : 2 * CHANNELS, :]
    second_ref[...] = (cot_ref[...].astype(F32) * back_ref[:, :CHANNELS, :].astype(F32)).astype(BF16)


def inner_kernel(total_ref, pos_ref, pos_bias_ref, mid_ref, mid_bias_ref):
    mid_ref[...] = total_ref[...].T[:WIDTH, :]
    pos_ref[...] = total_ref[:PE, WIDTH:]
    pos_bias_ref[...] = total_ref[PE : PE + 1, WIDTH:]
    mid_bias_ref[...] = total_ref[PE_BLOCK + 1 : PE_BLOCK + 2, WIDTH:]


def full(shape):
    return pl.BlockSpec(shape, lambda i: (0,) * len(shape))


def params(limit=VMEM_BYTES):
    return pltpu.CompilerParams(vmem_limit_bytes=limit)


def pack(value, first, second, cot):
    anywhere = pl.BlockSpec(memory_space=pltpu.HBM)
    buffer = pltpu.VMEM(value.shape, BF16)
    return pl.pallas_call(
        pack_kernel,
        in_specs=[anywhere] * 4,
        out_specs=anywhere,
        out_shape=jax.ShapeDtypeStruct((value.shape[0], DATA, RADIX), BF16),
        scratch_shapes=[buffer] * 2
        + [pltpu.VMEM((value.shape[0], DATA, RADIX), BF16), pltpu.SemaphoreType.DMA((5 * PACK_PARTS,))],
        compiler_params=params(),
        cost_estimate=pl.CostEstimate(flops=1 << 17, bytes_accessed=1 << 20, transcendentals=0),
    )(value, first, second, cot)


def network_forward(pos_weight, pos_bias, mid_weight, mid_bias, out_weight, decay_rates, tables, stack, ramp):
    left, back, right, right_inv, twid_cos, twid_sin = tables
    block = pl.BlockSpec((2 * WIDTH, NET_CHUNK), lambda i: (0, i))
    tabs = (left, right, twid_cos, twid_sin)
    args = (pos_weight.T, pos_bias[None, :], mid_weight, mid_bias[None, :], out_weight.T, decay_rates[None, :])
    outs = [
        jax.ShapeDtypeStruct((2 * WIDTH, SEQLEN), BF16),
        jax.ShapeDtypeStruct((2 * WIDTH, SEQLEN), BF16),
        jax.ShapeDtypeStruct((2, CHANNELS * KROWS, 2 * RADIX), F32),
        jax.ShapeDtypeStruct((2 * WIDTH, RADIX), BF16),
        jax.ShapeDtypeStruct((ROWS, RADIX), F32),
    ]
    return pl.pallas_call(
        network_kernel,
        grid=(SEQLEN // NET_CHUNK,),
        in_specs=[block, pl.BlockSpec((1, NET_CHUNK), lambda i: (0, i))]
        + [full(a.shape) for a in tabs]
        + [full(a.shape) for a in args],
        out_specs=[block] * 2 + [full(o.shape) for o in outs[2:]],
        out_shape=outs,
        scratch_shapes=[
            pltpu.VMEM((HALF_ROWS * ROWS, RADIX), F32),
            pltpu.VMEM((RADIX, RADIX), F32),
            pltpu.VMEM((2 * WIDTH, 2 * WIDTH), BF16),
            pltpu.VMEM((2 * WIDTH, 2 * WIDTH), BF16),
            pltpu.VMEM((2 * ROWS, 2 * WIDTH), BF16),
            pltpu.VMEM((WIDTH, RADIX), F32),
            pltpu.VMEM((ROWS, RADIX), F32),
        ],
        compiler_params=params(),
        cost_estimate=pl.CostEstimate(flops=1 << 30, bytes_accessed=10 << 20, transcendentals=1 << 20),
    )(stack, ramp, *tabs, *args)


def chain(x, net, tables, tail, ramp):
    act, cos, spec, own, own_rate = net
    left, back, right, right_inv, twid_cos, twid_sin = tables
    spectrum = pltpu.VMEM((CHANNELS * KROWS, 2 * RADIX), F32)
    wide = pltpu.VMEM((HALF_ROWS, CHANNELS * RADIX), F32)
    tall = 2 * WIDTH + PE_BLOCK
    small = (x, left, back, right, right_inv, twid_cos, twid_sin, own, own_rate, ramp)
    anywhere = pl.BlockSpec(memory_space=pltpu.HBM)
    within = pl.BlockSpec(memory_space=pltpu.VMEM)
    return pl.pallas_call(
        chain_kernel,
        in_specs=[anywhere] * 14,
        out_specs=[anywhere, within],
        out_shape=[
            jax.ShapeDtypeStruct((HALF_ROWS, SEND, RADIX), BF16),
            jax.ShapeDtypeStruct((ROWS, WIDTH), F32),
        ],
        scratch_shapes=[pltpu.VMEM(a.shape, a.dtype) for a in small]
        + [pltpu.VMEM(x.shape, F32)] * 2
        + [spectrum] * 4
        + [wide] * 2
        + [
            pltpu.VMEM((HALF_ROWS * ROWS, RADIX), F32),
            pltpu.VMEM(spec.shape, F32),
            pltpu.VMEM((tall, SEQLEN), BF16),
            pltpu.VMEM((2 * WIDTH, SEQLEN), BF16),
            pltpu.VMEM((2 * WIDTH + ROWS, SEQLEN), BF16),
            pltpu.VMEM((tall, 2 * WIDTH + ROWS), F32),
            pltpu.VMEM((WIDTH, RADIX), F32),
            pltpu.VMEM((HALF_ROWS, DATA, RADIX), BF16),
            pltpu.VMEM((HALF_ROWS, SHARE, RADIX), BF16),
            pltpu.SemaphoreType.DMA((6 + len(small),)),
        ],
        compiler_params=params(CHAIN_BYTES),
        cost_estimate=pl.CostEstimate(flops=3 << 30, bytes_accessed=8 << 20, transcendentals=1 << 17),
    )(*small, spec, act, cos, tail)


def share_total(back, peers):
    return pl.pallas_call(
        total_kernel,
        in_specs=[pl.BlockSpec(memory_space=pltpu.HBM)],
        out_specs=pl.BlockSpec(memory_space=pltpu.VMEM),
        out_shape=jax.ShapeDtypeStruct((peers, SHARE, RADIX), F32),
        scratch_shapes=[pltpu.VMEM((back.shape[0], SHARE, RADIX), BF16), pltpu.SemaphoreType.DMA(())],
        compiler_params=params(),
        cost_estimate=pl.CostEstimate(flops=1 << 16, bytes_accessed=1 << 17, transcendentals=0),
    )(back)


def finish(back, cot):
    devices = cot.shape[0]
    steps = 2
    data = pl.BlockSpec((devices // steps, CHANNELS, RADIX), lambda i: (i, 0, 0))
    return pl.pallas_call(
        finish_kernel,
        grid=(steps,),
        in_specs=[pl.BlockSpec((devices // steps, SEND, RADIX), lambda i: (i, 0, 0)), data],
        out_specs=[data] * 3,
        out_shape=[jax.ShapeDtypeStruct(cot.shape, BF16)] * 3,
        compiler_params=params(),
        cost_estimate=pl.CostEstimate(flops=1 << 17, bytes_accessed=1 << 20, transcendentals=0),
    )(back, cot)


def inner_gradients(total):
    within = pl.BlockSpec(memory_space=pltpu.VMEM)
    return pl.pallas_call(
        inner_kernel,
        in_specs=[within],
        out_specs=[within] * 4,
        out_shape=[
            jax.ShapeDtypeStruct((PE, WIDTH), F32),
            jax.ShapeDtypeStruct((1, WIDTH), F32),
            jax.ShapeDtypeStruct((WIDTH, WIDTH), F32),
            jax.ShapeDtypeStruct((1, WIDTH), F32),
        ],
        compiler_params=params(2 << 20),
        cost_estimate=pl.CostEstimate(flops=1 << 13, bytes_accessed=1 << 16, transcendentals=0),
    )(total)


SEQ = ("z", "yhi", "ylo", "x")
NEAR = ("ylo", "x")


def on_device(
    value_branch, first_gate, second_gate, out_cotangent,
    pos_weight, pos_bias, mid_weight, mid_bias, out_weight, decay_rates,
):
    devices = lax.axis_size(SEQ)
    tables = dft_tables()
    stack, tail = feature_tables()
    ramp = (np.arange(SEQLEN) / SEQLEN).astype(np.float32)[None, :]
    blocks = (devices, CHANNELS, RADIX)
    cot = out_cotangent.reshape(blocks)
    sent = pack(value_branch.reshape(blocks), first_gate.reshape(blocks), second_gate.reshape(blocks), cot)
    x = lax.all_to_all(sent, SEQ, 0, 0, tiled=True)
    net = network_forward(
        pos_weight, pos_bias, mid_weight, mid_bias, out_weight, decay_rates, tables, stack, ramp
    )
    y, out_weight_grad = chain(x.reshape(HALF_ROWS * DATA, RADIX), net, tables, tail, ramp)
    back = lax.all_to_all(y, SEQ, 0, 0, tiled=True)
    total = share_total(back, lax.axis_size(NEAR))
    total = lax.all_to_all(total, NEAR, 0, 0, tiled=True)
    value_grad, first_grad, second_grad = finish(back, cot)
    pos_grad, pos_bias_grad, mid_grad, mid_bias_grad = inner_gradients(total.reshape(WIDTH, RADIX))
    shape = value_branch.shape
    return (
        value_grad.reshape(shape),
        first_grad.reshape(shape),
        second_grad.reshape(shape),
        pos_grad.T,
        pos_bias_grad[0],
        mid_grad,
        mid_bias_grad[0],
        out_weight_grad,
    )


def solution(mesh):
    grid = Mesh(mesh.devices.reshape(mesh.shape["dp"], 2, 4, 2, 4), ("dp",) + SEQ)
    part = P(None, ("dp",) + SEQ)
    in_specs = (part,) * 4 + (P(),) * 6
    out_specs = (part,) * 3 + (P("dp", None), P("dp"), P("dp", None), P("dp"), P(SEQ, "dp"))
    return jax.shard_map(on_device, mesh=grid, in_specs=in_specs, out_specs=out_specs, check_vma=False)
```

```python
import math

import jax
import jax.numpy as jnp
import numpy as np
from jax import lax
from jax.experimental import pallas as pl
from jax.experimental.pallas import tpu as pltpu
from jax.sharding import Mesh
from jax.sharding import PartitionSpec as P

F32 = jnp.float32
BF16 = jnp.bfloat16
RADIX = 128
HALF_ROWS = 64
SEQLEN = HALF_ROWS * RADIX
KROWS = 72
WIDTH = 64
PE = 33
PE_BLOCK = 40
NET_CHUNK = 2048
CHANNELS = 8
ROWS = 2 * CHANNELS
SHARE = 8
DATA = 3 * CHANNELS
SEND = DATA + SHARE
PEERS = 8
PACK_PARTS = 2
VMEM_BYTES = 64 << 20
CHAIN_BYTES = 64 << 20


def dft_tables():
    n1, n2 = 2 * HALF_ROWS, RADIX
    k1 = np.arange(KROWS)[:, None]
    live = (k1 <= n1 // 2).astype(np.float64)
    angle_one = 2.0 * np.pi * ((k1 * np.arange(n1 // 2)[None, :]) % n1) / n1
    cos_one = np.cos(angle_one) * live
    sin_one = np.sin(angle_one) * live
    left = np.concatenate([cos_one, -sin_one], axis=0)
    weight = np.where((k1 == 0) | (k1 == n1 // 2), 1.0, 2.0) / (n1 * n2)
    back = np.concatenate([cos_one * weight, -sin_one * weight], axis=0).T
    grid = np.arange(n2)
    angle_two = 2.0 * np.pi * ((grid[:, None] * grid[None, :]) % n2) / n2
    cos_two, sin_two = np.cos(angle_two), np.sin(angle_two)
    right = np.block([[cos_two, -sin_two], [sin_two, cos_two]])
    right_inv = np.block([[cos_two, sin_two], [-sin_two, cos_two]])
    angle_tw = 2.0 * np.pi * ((k1 * grid[None, :]) % (n1 * n2)) / (n1 * n2)
    bf = lambda a: np.asarray(a, np.float32).astype(jnp.bfloat16)
    return (
        bf(left),
        bf(back),
        bf(right),
        bf(right_inv),
        np.cos(angle_tw).astype(np.float32),
        np.sin(angle_tw).astype(np.float32),
    )


def features():
    positions = np.arange(SEQLEN)
    bands = np.arange(1, (PE - 1) // 2 + 1)
    angles = 2.0 * np.pi * ((bands[:, None] * positions[None, :]) % SEQLEN) / SEQLEN
    ramp = positions[None, :] / SEQLEN
    return np.concatenate([ramp, np.cos(angles), np.sin(angles)], axis=0).astype(np.float32)


def np_split(value, parts):
    pieces = []
    for _ in range(parts):
        piece = value.astype(jnp.bfloat16)
        pieces.append(piece)
        value = value - piece.astype(np.float32)
    return pieces


def feature_tables():
    table = np.zeros((PE_BLOCK, SEQLEN), np.float32)
    table[:PE] = features()
    table[PE] = 1.0
    pieces = np_split(table, 3)
    pad = np.zeros((2 * WIDTH - 3 * PE_BLOCK, SEQLEN), jnp.bfloat16)
    return np.concatenate(pieces + [pad], axis=0), pieces[0]


def poly_tables():
    top = math.pi**2 * 1.0001
    nodes = (np.cos(np.pi * (np.arange(64) + 0.5) / 64) + 1) * top / 2
    root = np.sqrt(nodes)
    cheb = np.polynomial.chebyshev.Chebyshev
    sin_fit = cheb.fit(nodes, math.sqrt(2) * np.sin(root / 2) / root, 4, domain=[0, top])
    cos_fit = cheb.fit(nodes, math.sqrt(2) * np.cos(root / 2), 4, domain=[0, top])
    to_poly = lambda c: [float(x) for x in c.convert(kind=np.polynomial.Polynomial).coef]
    return to_poly(sin_fit), to_poly(cos_fit)


SIN_COEF, COS_COEF = poly_tables()
TURN_HI = 6.28125
TURN_LO = float(np.float32(2 * math.pi - TURN_HI))


def sin_cos(value):
    turns = jnp.round(value * (0.5 / math.pi))
    rest = (value - turns * TURN_HI) - turns * TURN_LO
    square = rest * rest

    def horner(coefs):
        total = square * coefs[-1] + coefs[-2]
        for coef in coefs[-3::-1]:
            total = total * square + coef
        return total

    half = rest * horner(SIN_COEF)
    return half * horner(COS_COEF), 1.0 - half * half


def dot(left, right):
    return lax.dot_general(left, right, (((1,), (0,)), ((), ())), preferred_element_type=F32)


def dot_last(left, right):
    return lax.dot_general(left, right, (((1,), (1,)), ((), ())), preferred_element_type=F32)


def split_two(value):
    high = value.astype(BF16)
    return high, (value - high.astype(F32)).astype(BF16)


def forward_pair(signal, left, right, twid_cos, twid_sin):
    stacked = dot(left, signal)
    rows = []
    for j in range(2):
        cols = slice(j * RADIX, (j + 1) * RADIX)
        real_a, imag_a = stacked[:KROWS, cols], stacked[KROWS:, cols]
        real_b = real_a * twid_cos + imag_a * twid_sin
        imag_b = imag_a * twid_cos - real_a * twid_sin
        rows.append(jnp.concatenate([real_b, imag_b], axis=1))
    return dot(jnp.concatenate(rows, axis=0).astype(BF16), right)


def inverse_pair(product, back, right_inv, twid_cos, twid_sin):
    section = dot(product, right_inv)
    cols = []
    for j in range(2):
        real_q = section[j * KROWS : (j + 1) * KROWS, :RADIX]
        imag_q = section[j * KROWS : (j + 1) * KROWS, RADIX:]
        real_r = real_q * twid_cos - imag_q * twid_sin
        imag_r = imag_q * twid_cos + real_q * twid_sin
        cols.append(jnp.concatenate([real_r, imag_r], axis=0))
    return dot(back, jnp.concatenate(cols, axis=1).astype(BF16))


def spectral_product(left, right, sign_left, sign_right):
    left_re, left_im = left[:, :RADIX], left[:, RADIX:]
    right_re, right_im = right[:, :RADIX], right[:, RADIX:]
    cross = left_im * right_im
    real = left_re * right_re + cross if sign_left * sign_right < 0 else left_re * right_re - cross
    one, two = left_im * right_re, left_re * right_im
    if sign_left > 0:
        imag = one + two if sign_right > 0 else one - two
    else:
        imag = two - one
    return jnp.concatenate([real.astype(BF16), imag.astype(BF16)], axis=1)


def pack_kernel(v_hbm, x1_hbm, x2_hbm, cot_hbm, out_hbm, x2, cot, sent, sems):
    size = x2.shape[0] // PACK_PARTS
    spans = [pl.ds(i * size, size) for i in range(PACK_PARTS)]
    loads, stores = [], []
    for i, span in enumerate(spans):
        moves = (
            (v_hbm.at[span], sent.at[span, pl.ds(0, CHANNELS)]),
            (x1_hbm.at[span], sent.at[span, pl.ds(CHANNELS, CHANNELS)]),
            (x2_hbm.at[span], x2.at[span]),
            (cot_hbm.at[span], cot.at[span]),
        )
        loads.append([pltpu.make_async_copy(src, dst, sems.at[5 * i + j]) for j, (src, dst) in enumerate(moves)])
        for copy in loads[-1]:
            copy.start()
    for i, span in enumerate(spans):
        for copy in loads[i]:
            copy.wait()
        sent[span, 2 * CHANNELS :, :] = (cot[span].astype(F32) * x2[span].astype(F32)).astype(BF16)
        stores.append(pltpu.make_async_copy(sent.at[span], out_hbm.at[span], sems.at[5 * i + 4]))
        stores[-1].start()
    for copy in stores:
        copy.wait()


def network_kernel(
    pe_ref, ramp_ref, left_ref, right_ref, tc_ref, ts_ref,
    pos_ref, pos_bias_ref, mid_ref, mid_bias_ref, out_ref, rate_ref,
    act_ref, cos_ref, spec_ref, own_ref, own_rate_ref,
    filt, square, wp, wm, wo, bias, decay,
):
    step = pl.program_id(0)

    @pl.when(step == 0)
    def _():
        rank = lax.axis_index(SEQ)
        lane = pl.multiple_of(rank // 8 * RADIX, RADIX)
        first = pl.multiple_of(rank % 8 * ROWS, ROWS)

        square[...] = jnp.zeros_like(square)
        for i in range(3):
            square[i * PE_BLOCK : i * PE_BLOCK + PE, :WIDTH] = pos_ref[...]
            square[i * PE_BLOCK + PE : i * PE_BLOCK + PE + 1, :WIDTH] = pos_bias_ref[...]
        wp[...] = jnp.concatenate(split_two(square[...].T[:WIDTH, :]), axis=0)

        square[...] = jnp.zeros_like(square)
        square[:WIDTH, :WIDTH] = mid_ref[...]
        own_ref[WIDTH:, :] = square[...].T[:WIDTH, :].astype(BF16)
        square[:WIDTH, WIDTH:] = mid_ref[...]
        wm[...] = jnp.concatenate(split_two(square[:WIDTH, :]), axis=0)

        square[:, :WIDTH] = jnp.broadcast_to(mid_bias_ref[...], (RADIX, WIDTH))
        bias[...] = square[...].T[:WIDTH, :]

        square[...] = jnp.broadcast_to(rate_ref[:, pl.ds(lane, RADIX)], (RADIX, RADIX)).T
        decay[...] = square[pl.ds(first, ROWS), :]
        own_rate_ref[...] = decay[...]

        block = out_ref[:, pl.ds(lane, RADIX)]
        square[...] = jnp.concatenate([block, block], axis=0).T
        mine = square[pl.ds(first, ROWS), :]
        wo[...] = jnp.concatenate(split_two(mine), axis=0)
        square[...] = jnp.zeros_like(square)
        square[:ROWS, :] = mine
        own_ref[:WIDTH, :] = square[...].T[:WIDTH, :].astype(BF16)

    span = 256
    parts = [slice(p * span, (p + 1) * span) for p in range(NET_CHUNK // span)]
    wide_bias = jnp.concatenate([bias[...]] * (span // RADIX), axis=1)
    wide_rate = jnp.concatenate([decay[...]] * (span // RADIX), axis=1)
    pres = []
    for cols in parts:
        both = dot(wp[...], pe_ref[:, cols])
        pres.append(both[:WIDTH] + both[WIDTH:])
    stacks = []
    for pre, cols in zip(pres, parts):
        act, slope = sin_cos(pre)
        pieces = split_two(act)
        act_ref[:WIDTH, cols] = pieces[0]
        cos_ref[:WIDTH, cols] = slope.astype(BF16)
        stacks.append(jnp.concatenate(pieces, axis=0))
    pres = []
    for stack in stacks:
        both = dot(wm[...], stack)
        pres.append(both[:WIDTH] + both[WIDTH:] + wide_bias)
    stacks = []
    for pre, cols in zip(pres, parts):
        act, slope = sin_cos(pre)
        pieces = split_two(act)
        act_ref[WIDTH:, cols] = pieces[0]
        cos_ref[WIDTH:, cols] = slope.astype(BF16)
        stacks.append(jnp.concatenate(pieces, axis=0))
    for part, (stack, cols) in enumerate(zip(stacks, parts)):
        both = dot(wo[...], stack)
        rows = (both[:ROWS] + both[ROWS:]) * jnp.exp(-wide_rate * ramp_ref[:, cols])
        for j in range(span // RADIX):
            base = pl.multiple_of(step * (NET_CHUNK // RADIX * ROWS) + (part * (span // RADIX) + j) * ROWS, ROWS)
            filt[pl.ds(base, ROWS), :] = rows[:, j * RADIX : (j + 1) * RADIX]

    @pl.when(step == SEQLEN // NET_CHUNK - 1)
    def _():
        for o in range(2):
            for pair in range(CHANNELS // 2):
                signal = jnp.concatenate(
                    [filt[pl.ds(2 * (2 * pair + j) + o, HALF_ROWS, stride=ROWS), :] for j in range(2)], axis=1
                ).astype(BF16)
                spec_ref[o, pair * 2 * KROWS : (pair + 1) * 2 * KROWS, :] = forward_pair(
                    signal, left_ref[...], right_ref[...], tc_ref[...], ts_ref[...]
                )


def chain_kernel(
    x_hbm, left_hbm, back_hbm, right_hbm, inv_hbm, tc_hbm, ts_hbm, own_hbm, rate_hbm, ramp_hbm,
    spec_hbm, act_hbm, cos_hbm, tail_hbm,
    share_ref, out_ref, sz_hbm, sg1_hbm, prod_hbm,
    x_ref, left_ref, back_ref, right_ref, inv_ref, tc_ref, ts_ref, own_ref, rate_ref, ramp_ref,
    xs, sv, sg2, sz, sg1, conv, dz, prod, dh, spec, act, cos, stat, acc, sems,
):
    sources = (x_hbm, left_hbm, right_hbm, tc_hbm, ts_hbm, back_hbm, inv_hbm, own_hbm, rate_hbm, ramp_hbm)
    targets = (x_ref, left_ref, right_ref, tc_ref, ts_ref, back_ref, inv_ref, own_ref, rate_ref, ramp_ref)
    small = [pltpu.make_async_copy(s, d, sems.at[7 + i]) for i, (s, d) in enumerate(zip(sources, targets))]
    for copy in small:
        copy.start()
    first_load = pltpu.make_async_copy(spec_hbm, spec, sems.at[0])
    loads = [
        pltpu.make_async_copy(cos_hbm, cos, sems.at[1]),
        pltpu.make_async_copy(act_hbm, act.at[pl.ds(0, 2 * WIDTH)], sems.at[2]),
        pltpu.make_async_copy(tail_hbm, act.at[pl.ds(2 * WIDTH, PE_BLOCK)], sems.at[3]),
    ]
    first_load.start()
    for copy in loads:
        copy.start()
    for copy in small[:5]:
        copy.wait()
    xs[...] = x_ref[...].astype(F32)
    tables_f = (left_ref[...], right_ref[...], tc_ref[...], ts_ref[...])
    pairs = range(CHANNELS // 2)

    def signal(kind, pair):
        return jnp.concatenate(
            [xs[pl.ds(kind * CHANNELS + 2 * pair + j, HALF_ROWS, stride=DATA), :] for j in range(2)], axis=1
        )

    def rows(pair):
        return slice(pair * 2 * KROWS, (pair + 1) * 2 * KROWS)

    def lanes(pair):
        return slice(pair * 2 * RADIX, (pair + 1) * 2 * RADIX)

    def emit_filter(o, pair, value):
        for j in range(2):
            dh[pl.ds(2 * (2 * pair + j) + o, HALF_ROWS, stride=ROWS), :] = value[:, j * RADIX : (j + 1) * RADIX]

    for p in pairs:
        sv[rows(p), :] = forward_pair(signal(0, p).astype(BF16), *tables_f)
    for p in pairs:
        sg2[rows(p), :] = forward_pair(signal(2, p).astype(BF16), *tables_f)
    first_load.wait()
    for copy in small[5:]:
        copy.wait()
    tables_i = (back_ref[...], inv_ref[...], tc_ref[...], ts_ref[...])
    for p in pairs:
        conv[:, lanes(p)] = inverse_pair(spectral_product(spec[0, rows(p), :], sv[rows(p), :], 1, 1), *tables_i)
    for p in pairs:
        dz[:, lanes(p)] = inverse_pair(spectral_product(spec[1, rows(p), :], sg2[rows(p), :], -1, 1), *tables_i)
    for p in pairs:
        gated = (signal(1, p) * conv[:, lanes(p)]).astype(BF16)
        sz[rows(p), :] = forward_pair(gated, *tables_f)
    for p in pairs:
        prod[:, lanes(p)] = (dz[:, lanes(p)] * conv[:, lanes(p)]).astype(BF16)
        grad = (dz[:, lanes(p)] * signal(1, p)).astype(BF16)
        sg1[rows(p), :] = forward_pair(grad, *tables_f)
    stores = [
        pltpu.make_async_copy(sz, sz_hbm, sems.at[4]),
        pltpu.make_async_copy(sg1, sg1_hbm, sems.at[5]),
        pltpu.make_async_copy(prod, prod_hbm, sems.at[6]),
    ]
    for copy in stores:
        copy.start()
    for p in pairs:
        emit_filter(1, p, inverse_pair(spectral_product(sg2[rows(p), :], sz[rows(p), :], 1, -1), *tables_i))
    for p in pairs:
        emit_filter(0, p, inverse_pair(spectral_product(sg1[rows(p), :], sv[rows(p), :], 1, -1), *tables_i))

    span = 256
    columns = [slice(i * span, (i + 1) * span) for i in range(SEQLEN // span)]
    wide_rate = jnp.concatenate([rate_ref[...]] * (span // RADIX), axis=1)
    for cols in columns:
        first = cols.start // RADIX
        wide = jnp.concatenate([dh[(first + i) * ROWS : (first + i + 1) * ROWS, :] for i in range(span // RADIX)], axis=1)
        grad = wide * (jnp.exp(-wide_rate * ramp_ref[:, cols]) * (1.0 / SEQLEN))
        stat[2 * WIDTH :, cols] = grad.astype(BF16)
    for copy in loads:
        copy.wait()
    for cols in columns:
        stat[:WIDTH, cols] = (dot(own_ref[:WIDTH, :ROWS], stat[2 * WIDTH :, cols]) * cos[WIDTH:, cols].astype(F32)).astype(BF16)
    for cols in columns:
        stat[WIDTH : 2 * WIDTH, cols] = (
            dot(own_ref[WIDTH:, :WIDTH], stat[:WIDTH, cols]) * cos[:WIDTH, cols].astype(F32)
        ).astype(BF16)
    acc[...] = dot_last(act[...], stat[...])
    out_ref[...] = acc[WIDTH : 2 * WIDTH, 2 * WIDTH :].T
    tail = 2 * WIDTH
    share_ref[...] = jnp.zeros_like(share_ref)
    share_ref[:, :WIDTH] = acc[:WIDTH, :WIDTH]
    share_ref[:PE_BLOCK, WIDTH:] = acc[tail:, WIDTH : 2 * WIDTH]
    share_ref[PE_BLOCK : PE_BLOCK + 8, WIDTH:] = acc[tail + 32 :, :WIDTH]
    for copy in stores:
        copy.wait()


def output_kernel(
    spec_hbm, sz_hbm, sg1_hbm, prod_hbm, back_hbm, inv_hbm, tc_hbm, ts_hbm,
    y_hbm,
    spec, sz, sg1, prod, back_ref, inv_ref, tc_ref, ts_ref, ys, data, sems,
):
    sources = (spec_hbm, sz_hbm, sg1_hbm, prod_hbm, back_hbm, inv_hbm, tc_hbm, ts_hbm)
    targets = (spec, sz, sg1, prod, back_ref, inv_ref, tc_ref, ts_ref)
    loads = [pltpu.make_async_copy(s, d, sems.at[i]) for i, (s, d) in enumerate(zip(sources, targets))]
    for copy in loads:
        copy.start()
    for copy in loads:
        copy.wait()
    tables_i = (back_ref[...], inv_ref[...], tc_ref[...], ts_ref[...])

    def emit(kind, pair, value):
        for j in range(2):
            ys[pl.ds(kind * CHANNELS + 2 * pair + j, HALF_ROWS, stride=DATA), :] = value[
                :, j * RADIX : (j + 1) * RADIX
            ]

    for p in range(CHANNELS // 2):
        rows = slice(p * 2 * KROWS, (p + 1) * 2 * KROWS)
        emit(0, p, inverse_pair(spectral_product(spec[1, rows, :], sz[rows, :], 1, 1), *tables_i))
    for p in range(CHANNELS // 2):
        rows = slice(p * 2 * KROWS, (p + 1) * 2 * KROWS)
        emit(2, p, inverse_pair(spectral_product(spec[0, rows, :], sg1[rows, :], -1, 1), *tables_i))
        emit(1, p, prod[:, p * 2 * RADIX : (p + 1) * 2 * RADIX].astype(F32))
    for i in range(HALF_ROWS):
        data[i] = ys[i * DATA : (i + 1) * DATA, :].astype(BF16)
    last = pltpu.make_async_copy(data, y_hbm.at[:, pl.ds(0, DATA), :], sems.at[8])
    last.start()
    last.wait()


def total_kernel(y_in, near_ref, y_out, parts, sem):
    total = jnp.sum(near_ref[...], axis=0).astype(BF16)
    parts[...] = jnp.broadcast_to(total[None], parts.shape)
    copy = pltpu.make_async_copy(parts, y_out.at[:, pl.ds(DATA, SHARE), :], sem)
    copy.start()
    copy.wait()


def finish_kernel(back_ref, cot_ref, value_ref, first_ref, second_ref, pos_ref, pos_bias_ref, mid_ref, mid_bias_ref, total):
    step = pl.program_id(0)
    value_ref[...] = back_ref[:, 2 * CHANNELS : DATA, :]
    first_ref[...] = back_ref[:, CHANNELS : 2 * CHANNELS, :]
    second_ref[...] = (cot_ref[...].astype(F32) * back_ref[:, :CHANNELS, :].astype(F32)).astype(BF16)
    part = jnp.zeros(total.shape, F32)
    for i in range(back_ref.shape[0] // PEERS):
        part = part + back_ref[i * PEERS : (i + 1) * PEERS, DATA:, :].astype(F32)

    @pl.when(step == 0)
    def _():
        total[...] = part

    @pl.when(step > 0)
    def _():
        total[...] += part

    @pl.when(step == pl.num_programs(0) - 1)
    def _():
        whole = jnp.concatenate([total[j] for j in range(PEERS)], axis=0)
        mid_ref[...] = whole.T[:WIDTH, :]
        pos_ref[...] = whole[:PE, WIDTH:]
        pos_bias_ref[...] = whole[PE : PE + 1, WIDTH:]
        mid_bias_ref[...] = whole[PE_BLOCK + 1 : PE_BLOCK + 2, WIDTH:]


def full(shape):
    return pl.BlockSpec(shape, lambda i: (0,) * len(shape))


def params(limit=VMEM_BYTES):
    return pltpu.CompilerParams(vmem_limit_bytes=limit)


def pack(value, first, second, cot):
    anywhere = pl.BlockSpec(memory_space=pltpu.HBM)
    buffer = pltpu.VMEM(value.shape, BF16)
    return pl.pallas_call(
        pack_kernel,
        in_specs=[anywhere] * 4,
        out_specs=anywhere,
        out_shape=jax.ShapeDtypeStruct((value.shape[0], DATA, RADIX), BF16),
        scratch_shapes=[buffer] * 2
        + [pltpu.VMEM((value.shape[0], DATA, RADIX), BF16), pltpu.SemaphoreType.DMA((5 * PACK_PARTS,))],
        compiler_params=params(),
        cost_estimate=pl.CostEstimate(flops=1 << 17, bytes_accessed=1 << 20, transcendentals=0),
    )(value, first, second, cot)


def network_forward(pos_weight, pos_bias, mid_weight, mid_bias, out_weight, decay_rates, tables, stack, ramp):
    left, back, right, right_inv, twid_cos, twid_sin = tables
    block = pl.BlockSpec((2 * WIDTH, NET_CHUNK), lambda i: (0, i))
    tabs = (left, right, twid_cos, twid_sin)
    args = (pos_weight.T, pos_bias[None, :], mid_weight, mid_bias[None, :], out_weight.T, decay_rates[None, :])
    outs = [
        jax.ShapeDtypeStruct((2 * WIDTH, SEQLEN), BF16),
        jax.ShapeDtypeStruct((2 * WIDTH, SEQLEN), BF16),
        jax.ShapeDtypeStruct((2, CHANNELS * KROWS, 2 * RADIX), F32),
        jax.ShapeDtypeStruct((2 * WIDTH, RADIX), BF16),
        jax.ShapeDtypeStruct((ROWS, RADIX), F32),
    ]
    return pl.pallas_call(
        network_kernel,
        grid=(SEQLEN // NET_CHUNK,),
        in_specs=[block, pl.BlockSpec((1, NET_CHUNK), lambda i: (0, i))]
        + [full(a.shape) for a in tabs]
        + [full(a.shape) for a in args],
        out_specs=[block] * 2 + [full(o.shape) for o in outs[2:]],
        out_shape=outs,
        scratch_shapes=[
            pltpu.VMEM((HALF_ROWS * ROWS, RADIX), F32),
            pltpu.VMEM((RADIX, RADIX), F32),
            pltpu.VMEM((2 * WIDTH, 2 * WIDTH), BF16),
            pltpu.VMEM((2 * WIDTH, 2 * WIDTH), BF16),
            pltpu.VMEM((2 * ROWS, 2 * WIDTH), BF16),
            pltpu.VMEM((WIDTH, RADIX), F32),
            pltpu.VMEM((ROWS, RADIX), F32),
        ],
        compiler_params=params(),
        cost_estimate=pl.CostEstimate(flops=1 << 30, bytes_accessed=10 << 20, transcendentals=1 << 20),
    )(stack, ramp, *tabs, *args)


def chain(x, net, tables, tail, ramp):
    act, cos, spec, own, own_rate = net
    left, back, right, right_inv, twid_cos, twid_sin = tables
    spectrum = pltpu.VMEM((CHANNELS * KROWS, 2 * RADIX), F32)
    wide = pltpu.VMEM((HALF_ROWS, CHANNELS * RADIX), F32)
    tall = 2 * WIDTH + PE_BLOCK
    small = (x, left, back, right, right_inv, twid_cos, twid_sin, own, own_rate, ramp)
    anywhere = pl.BlockSpec(memory_space=pltpu.HBM)
    within = pl.BlockSpec(memory_space=pltpu.VMEM)
    return pl.pallas_call(
        chain_kernel,
        in_specs=[anywhere] * 14,
        out_specs=[within] * 2 + [anywhere] * 3,
        out_shape=[
            jax.ShapeDtypeStruct((WIDTH, RADIX), F32),
            jax.ShapeDtypeStruct((ROWS, WIDTH), F32),
            jax.ShapeDtypeStruct((CHANNELS * KROWS, 2 * RADIX), F32),
            jax.ShapeDtypeStruct((CHANNELS * KROWS, 2 * RADIX), F32),
            jax.ShapeDtypeStruct((HALF_ROWS, CHANNELS * RADIX), BF16),
        ],
        scratch_shapes=[pltpu.VMEM(a.shape, a.dtype) for a in small]
        + [pltpu.VMEM(x.shape, F32)]
        + [spectrum] * 4
        + [wide] * 2
        + [
            pltpu.VMEM((HALF_ROWS, CHANNELS * RADIX), BF16),
            pltpu.VMEM((HALF_ROWS * ROWS, RADIX), F32),
            pltpu.VMEM(spec.shape, F32),
            pltpu.VMEM((tall, SEQLEN), BF16),
            pltpu.VMEM((2 * WIDTH, SEQLEN), BF16),
            pltpu.VMEM((2 * WIDTH + ROWS, SEQLEN), BF16),
            pltpu.VMEM((tall, 2 * WIDTH + ROWS), F32),
            pltpu.SemaphoreType.DMA((7 + len(small),)),
        ],
        compiler_params=params(CHAIN_BYTES),
        cost_estimate=pl.CostEstimate(flops=3 << 30, bytes_accessed=8 << 20, transcendentals=1 << 17),
    )(*small, spec, act, cos, tail)


def outputs(spec, sz, sg1, prod, tables):
    left, back, right, right_inv, twid_cos, twid_sin = tables
    anywhere = pl.BlockSpec(memory_space=pltpu.HBM)
    args = (spec, sz, sg1, prod, back, right_inv, twid_cos, twid_sin)
    return pl.pallas_call(
        output_kernel,
        in_specs=[anywhere] * len(args),
        out_specs=anywhere,
        out_shape=jax.ShapeDtypeStruct((HALF_ROWS, SEND, RADIX), BF16),
        scratch_shapes=[pltpu.VMEM(a.shape, a.dtype) for a in args]
        + [
            pltpu.VMEM((HALF_ROWS * DATA, RADIX), F32),
            pltpu.VMEM((HALF_ROWS, DATA, RADIX), BF16),
            pltpu.SemaphoreType.DMA((len(args) + 1,)),
        ],
        compiler_params=params(),
        cost_estimate=pl.CostEstimate(flops=1 << 29, bytes_accessed=4 << 20, transcendentals=0),
    )(*args)


def add_total(y, near):
    anywhere = pl.BlockSpec(memory_space=pltpu.HBM)
    return pl.pallas_call(
        total_kernel,
        in_specs=[anywhere, pl.BlockSpec(memory_space=pltpu.VMEM)],
        out_specs=anywhere,
        out_shape=jax.ShapeDtypeStruct(y.shape, BF16),
        input_output_aliases={0: 0},
        scratch_shapes=[pltpu.VMEM((y.shape[0], SHARE, RADIX), BF16), pltpu.SemaphoreType.DMA(())],
        compiler_params=params(),
        cost_estimate=pl.CostEstimate(flops=1 << 16, bytes_accessed=1 << 17, transcendentals=0),
    )(y, near)


def finish(back, cot):
    devices = cot.shape[0]
    steps = 2
    data = pl.BlockSpec((devices // steps, CHANNELS, RADIX), lambda i: (i, 0, 0))
    outs = [jax.ShapeDtypeStruct(cot.shape, BF16)] * 3 + [
        jax.ShapeDtypeStruct((PE, WIDTH), F32),
        jax.ShapeDtypeStruct((1, WIDTH), F32),
        jax.ShapeDtypeStruct((WIDTH, WIDTH), F32),
        jax.ShapeDtypeStruct((1, WIDTH), F32),
    ]
    return pl.pallas_call(
        finish_kernel,
        grid=(steps,),
        in_specs=[pl.BlockSpec((devices // steps, SEND, RADIX), lambda i: (i, 0, 0)), data],
        out_specs=[data] * 3 + [full(o.shape) for o in outs[3:]],
        out_shape=outs,
        scratch_shapes=[pltpu.VMEM((PEERS, SHARE, RADIX), F32)],
        compiler_params=params(),
        cost_estimate=pl.CostEstimate(flops=1 << 20, bytes_accessed=1 << 20, transcendentals=0),
    )(back, cot)


SEQ = ("z", "yhi", "ylo", "x")
NEAR = ("ylo", "x")


def on_device(
    value_branch, first_gate, second_gate, out_cotangent,
    pos_weight, pos_bias, mid_weight, mid_bias, out_weight, decay_rates,
):
    devices = lax.axis_size(SEQ)
    tables = dft_tables()
    stack, tail = feature_tables()
    ramp = (np.arange(SEQLEN) / SEQLEN).astype(np.float32)[None, :]
    blocks = (devices, CHANNELS, RADIX)
    cot = out_cotangent.reshape(blocks)
    sent = pack(value_branch.reshape(blocks), first_gate.reshape(blocks), second_gate.reshape(blocks), cot)
    x = lax.all_to_all(sent, SEQ, 0, 0, tiled=True)
    net = network_forward(
        pos_weight, pos_bias, mid_weight, mid_bias, out_weight, decay_rates, tables, stack, ramp
    )
    share, out_weight_grad, sz, sg1, prod = chain(x.reshape(HALF_ROWS * DATA, RADIX), net, tables, tail, ramp)
    near = lax.all_to_all(share.reshape(PEERS, SHARE, RADIX), NEAR, 0, 0, tiled=True)
    y = outputs(net[2], sz, sg1, prod, tables)
    back = lax.all_to_all(add_total(y, near), SEQ, 0, 0, tiled=True)
    value_grad, first_grad, second_grad, pos_grad, pos_bias_grad, mid_grad, mid_bias_grad = finish(back, cot)
    shape = value_branch.shape
    return (
        value_grad.reshape(shape),
        first_grad.reshape(shape),
        second_grad.reshape(shape),
        pos_grad.T,
        pos_bias_grad[0],
        mid_grad,
        mid_bias_grad[0],
        out_weight_grad,
    )


def solution(mesh):
    grid = Mesh(mesh.devices.reshape(mesh.shape["dp"], 2, 4, 2, 4), ("dp",) + SEQ)
    part = P(None, ("dp",) + SEQ)
    in_specs = (part,) * 4 + (P(),) * 6
    out_specs = (part,) * 3 + (P("dp", None), P("dp"), P("dp", None), P("dp"), P(SEQ, "dp"))
    return jax.shard_map(on_device, mesh=grid, in_specs=in_specs, out_specs=out_specs, check_vma=False)
```

```python
import math

import jax
import jax.numpy as jnp
import numpy as np
from jax import lax
from jax.experimental import pallas as pl
from jax.experimental.pallas import tpu as pltpu
from jax.sharding import Mesh
from jax.sharding import PartitionSpec as P

F32 = jnp.float32
BF16 = jnp.bfloat16
RADIX = 128
HALF_ROWS = 64
SEQLEN = HALF_ROWS * RADIX
KROWS = 72
WIDTH = 64
PE = 33
PE_BLOCK = 40
NET_CHUNK = 8192
CHANNELS = 8
ROWS = 2 * CHANNELS
SHARE = 8
DATA = 3 * CHANNELS
SEND = DATA + SHARE
PEERS = 8
PACK_PARTS = 2
ADD_BYTES = 64 << 20
FIN_BYTES = 64 << 20
VMEM_BYTES = 64 << 20
CHAIN_BYTES = 64 << 20


def dft_tables():
    n1, n2 = 2 * HALF_ROWS, RADIX
    k1 = np.arange(KROWS)[:, None]
    live = (k1 <= n1 // 2).astype(np.float64)
    angle_one = 2.0 * np.pi * ((k1 * np.arange(n1 // 2)[None, :]) % n1) / n1
    cos_one = np.cos(angle_one) * live
    sin_one = np.sin(angle_one) * live
    left = np.concatenate([cos_one, -sin_one], axis=0)
    weight = np.where((k1 == 0) | (k1 == n1 // 2), 1.0, 2.0) / (n1 * n2)
    back = np.concatenate([cos_one * weight, -sin_one * weight], axis=0).T
    grid = np.arange(n2)
    angle_two = 2.0 * np.pi * ((grid[:, None] * grid[None, :]) % n2) / n2
    cos_two, sin_two = np.cos(angle_two), np.sin(angle_two)
    right = np.block([[cos_two, -sin_two], [sin_two, cos_two]])
    right_inv = np.block([[cos_two, sin_two], [-sin_two, cos_two]])
    angle_tw = 2.0 * np.pi * ((k1 * grid[None, :]) % (n1 * n2)) / (n1 * n2)
    bf = lambda a: np.asarray(a, np.float32).astype(jnp.bfloat16)
    return (
        bf(left),
        bf(back),
        bf(right),
        bf(right_inv),
        np.cos(angle_tw).astype(np.float32),
        np.sin(angle_tw).astype(np.float32),
    )


def features():
    positions = np.arange(SEQLEN)
    bands = np.arange(1, (PE - 1) // 2 + 1)
    angles = 2.0 * np.pi * ((bands[:, None] * positions[None, :]) % SEQLEN) / SEQLEN
    ramp = positions[None, :] / SEQLEN
    return np.concatenate([ramp, np.cos(angles), np.sin(angles)], axis=0).astype(np.float32)


def np_split(value, parts):
    pieces = []
    for _ in range(parts):
        piece = value.astype(jnp.bfloat16)
        pieces.append(piece)
        value = value - piece.astype(np.float32)
    return pieces


def feature_tables():
    table = np.zeros((PE_BLOCK, SEQLEN), np.float32)
    table[:PE] = features()
    table[PE] = 1.0
    pieces = np_split(table, 3)
    pad = np.zeros((2 * WIDTH - 3 * PE_BLOCK, SEQLEN), jnp.bfloat16)
    return np.concatenate(pieces + [pad], axis=0), pieces[0]


def poly_tables():
    top = math.pi**2 * 1.0001
    nodes = (np.cos(np.pi * (np.arange(64) + 0.5) / 64) + 1) * top / 2
    root = np.sqrt(nodes)
    cheb = np.polynomial.chebyshev.Chebyshev
    sin_fit = cheb.fit(nodes, math.sqrt(2) * np.sin(root / 2) / root, 4, domain=[0, top])
    cos_fit = cheb.fit(nodes, math.sqrt(2) * np.cos(root / 2), 4, domain=[0, top])
    to_poly = lambda c: [float(x) for x in c.convert(kind=np.polynomial.Polynomial).coef]
    return to_poly(sin_fit), to_poly(cos_fit)


SIN_COEF, COS_COEF = poly_tables()
TURN_HI = 6.28125
TURN_LO = float(np.float32(2 * math.pi - TURN_HI))


def sin_cos(value):
    turns = jnp.round(value * (0.5 / math.pi))
    rest = (value - turns * TURN_HI) - turns * TURN_LO
    square = rest * rest

    def horner(coefs):
        total = square * coefs[-1] + coefs[-2]
        for coef in coefs[-3::-1]:
            total = total * square + coef
        return total

    half = rest * horner(SIN_COEF)
    return half * horner(COS_COEF), 1.0 - half * half


def dot(left, right):
    return lax.dot_general(left, right, (((1,), (0,)), ((), ())), preferred_element_type=F32)


def dot_last(left, right):
    return lax.dot_general(left, right, (((1,), (1,)), ((), ())), preferred_element_type=F32)


def split_two(value):
    high = value.astype(BF16)
    return high, (value - high.astype(F32)).astype(BF16)


def forward_pair(signal, left, right, twid_cos, twid_sin):
    stacked = dot(left, signal)
    rows = []
    for j in range(2):
        cols = slice(j * RADIX, (j + 1) * RADIX)
        real_a, imag_a = stacked[:KROWS, cols], stacked[KROWS:, cols]
        real_b = real_a * twid_cos + imag_a * twid_sin
        imag_b = imag_a * twid_cos - real_a * twid_sin
        rows.append(jnp.concatenate([real_b, imag_b], axis=1))
    return dot(jnp.concatenate(rows, axis=0).astype(BF16), right)


def inverse_pair(product, back, right_inv, twid_cos, twid_sin):
    section = dot(product, right_inv)
    cols = []
    for j in range(2):
        real_q = section[j * KROWS : (j + 1) * KROWS, :RADIX]
        imag_q = section[j * KROWS : (j + 1) * KROWS, RADIX:]
        real_r = real_q * twid_cos - imag_q * twid_sin
        imag_r = imag_q * twid_cos + real_q * twid_sin
        cols.append(jnp.concatenate([real_r, imag_r], axis=0))
    return dot(back, jnp.concatenate(cols, axis=1).astype(BF16))


def spectral_product(left, right, sign_left, sign_right):
    left_re, left_im = left[:, :RADIX], left[:, RADIX:]
    right_re, right_im = right[:, :RADIX], right[:, RADIX:]
    cross = left_im * right_im
    real = left_re * right_re + cross if sign_left * sign_right < 0 else left_re * right_re - cross
    one, two = left_im * right_re, left_re * right_im
    if sign_left > 0:
        imag = one + two if sign_right > 0 else one - two
    else:
        imag = two - one
    return jnp.concatenate([real.astype(BF16), imag.astype(BF16)], axis=1)


def pack_kernel(v_hbm, x1_hbm, x2_hbm, cot_hbm, out_hbm, x2, cot, sent, sems):
    size = x2.shape[0] // PACK_PARTS
    spans = [pl.ds(i * size, size) for i in range(PACK_PARTS)]
    loads, stores = [], []
    for i, span in enumerate(spans):
        moves = (
            (v_hbm.at[span], sent.at[span, pl.ds(0, CHANNELS)]),
            (x1_hbm.at[span], sent.at[span, pl.ds(CHANNELS, CHANNELS)]),
            (x2_hbm.at[span], x2.at[span]),
            (cot_hbm.at[span], cot.at[span]),
        )
        loads.append([pltpu.make_async_copy(src, dst, sems.at[5 * i + j]) for j, (src, dst) in enumerate(moves)])
        for copy in loads[-1]:
            copy.start()
    for i, span in enumerate(spans):
        for copy in loads[i]:
            copy.wait()
        sent[span, 2 * CHANNELS :, :] = (cot[span].astype(F32) * x2[span].astype(F32)).astype(BF16)
        stores.append(pltpu.make_async_copy(sent.at[span], out_hbm.at[span], sems.at[5 * i + 4]))
        stores[-1].start()
    for copy in stores:
        copy.wait()


def network_kernel(
    pe_ref, ramp_ref, left_ref, right_ref, tc_ref, ts_ref,
    pos_ref, pos_bias_ref, mid_ref, mid_bias_ref, out_ref, rate_ref,
    act_ref, cos_ref, spec_ref, own_ref, own_rate_ref,
    filt, square, wp, wm, wo, bias, decay,
):
    step = pl.program_id(0)

    @pl.when(step == 0)
    def _():
        rank = lax.axis_index(SEQ)
        lane = pl.multiple_of(rank // 8 * RADIX, RADIX)
        first = pl.multiple_of(rank % 8 * ROWS, ROWS)

        square[...] = jnp.zeros_like(square)
        for i in range(3):
            square[i * PE_BLOCK : i * PE_BLOCK + PE, :WIDTH] = pos_ref[...]
            square[i * PE_BLOCK + PE : i * PE_BLOCK + PE + 1, :WIDTH] = pos_bias_ref[...]
        wp[...] = jnp.concatenate(split_two(square[...].T[:WIDTH, :]), axis=0)

        square[...] = jnp.zeros_like(square)
        square[:WIDTH, :WIDTH] = mid_ref[...]
        own_ref[WIDTH:, :] = square[...].T[:WIDTH, :].astype(BF16)
        square[:WIDTH, WIDTH:] = mid_ref[...]
        wm[...] = jnp.concatenate(split_two(square[:WIDTH, :]), axis=0)

        square[:, :WIDTH] = jnp.broadcast_to(mid_bias_ref[...], (RADIX, WIDTH))
        bias[...] = square[...].T[:WIDTH, :]

        square[...] = jnp.broadcast_to(rate_ref[:, pl.ds(lane, RADIX)], (RADIX, RADIX)).T
        decay[...] = square[pl.ds(first, ROWS), :]
        own_rate_ref[...] = decay[...]

        block = out_ref[:, pl.ds(lane, RADIX)]
        square[...] = jnp.concatenate([block, block], axis=0).T
        mine = square[pl.ds(first, ROWS), :]
        wo[...] = jnp.concatenate(split_two(mine), axis=0)
        square[...] = jnp.zeros_like(square)
        square[:ROWS, :] = mine
        own_ref[:WIDTH, :] = square[...].T[:WIDTH, :].astype(BF16)

    span = 256
    parts = [slice(p * span, (p + 1) * span) for p in range(NET_CHUNK // span)]
    wide_bias = jnp.concatenate([bias[...]] * (span // RADIX), axis=1)
    wide_rate = jnp.concatenate([decay[...]] * (span // RADIX), axis=1)
    pres = []
    for cols in parts:
        both = dot(wp[...], pe_ref[:, cols])
        pres.append(both[:WIDTH] + both[WIDTH:])
    stacks = []
    for pre, cols in zip(pres, parts):
        act, slope = sin_cos(pre)
        pieces = split_two(act)
        act_ref[:WIDTH, cols] = pieces[0]
        cos_ref[:WIDTH, cols] = slope.astype(BF16)
        stacks.append(jnp.concatenate(pieces, axis=0))
    pres = []
    for stack in stacks:
        both = dot(wm[...], stack)
        pres.append(both[:WIDTH] + both[WIDTH:] + wide_bias)
    stacks = []
    for pre, cols in zip(pres, parts):
        act, slope = sin_cos(pre)
        pieces = split_two(act)
        act_ref[WIDTH:, cols] = pieces[0]
        cos_ref[WIDTH:, cols] = slope.astype(BF16)
        stacks.append(jnp.concatenate(pieces, axis=0))
    for part, (stack, cols) in enumerate(zip(stacks, parts)):
        both = dot(wo[...], stack)
        rows = (both[:ROWS] + both[ROWS:]) * jnp.exp(-wide_rate * ramp_ref[:, cols])
        for j in range(span // RADIX):
            base = pl.multiple_of(step * (NET_CHUNK // RADIX * ROWS) + (part * (span // RADIX) + j) * ROWS, ROWS)
            filt[pl.ds(base, ROWS), :] = rows[:, j * RADIX : (j + 1) * RADIX]

    @pl.when(step == SEQLEN // NET_CHUNK - 1)
    def _():
        for o in range(2):
            for pair in range(CHANNELS // 2):
                signal = jnp.concatenate(
                    [filt[pl.ds(2 * (2 * pair + j) + o, HALF_ROWS, stride=ROWS), :] for j in range(2)], axis=1
                ).astype(BF16)
                spec_ref[o, pair * 2 * KROWS : (pair + 1) * 2 * KROWS, :] = forward_pair(
                    signal, left_ref[...], right_ref[...], tc_ref[...], ts_ref[...]
                )


def chain_kernel(
    x_hbm, left_hbm, back_hbm, right_hbm, inv_hbm, tc_hbm, ts_hbm, own_hbm, rate_hbm, ramp_hbm,
    spec_hbm, act_hbm, cos_hbm, tail_hbm,
    share_ref, out_ref, sz_hbm, sg1_hbm, prod_hbm,
    x_ref, left_ref, back_ref, right_ref, inv_ref, tc_ref, ts_ref, own_ref, rate_ref, ramp_ref,
    xs, sv, sg2, sz, sg1, conv, dz, prod, dh, spec, act, cos, stat, acc, sems,
):
    sources = (x_hbm, left_hbm, right_hbm, tc_hbm, ts_hbm, back_hbm, inv_hbm, own_hbm, rate_hbm, ramp_hbm)
    targets = (x_ref, left_ref, right_ref, tc_ref, ts_ref, back_ref, inv_ref, own_ref, rate_ref, ramp_ref)
    small = [pltpu.make_async_copy(s, d, sems.at[7 + i]) for i, (s, d) in enumerate(zip(sources, targets))]
    for copy in small:
        copy.start()
    first_load = pltpu.make_async_copy(spec_hbm, spec, sems.at[0])
    loads = [
        pltpu.make_async_copy(cos_hbm, cos, sems.at[1]),
        pltpu.make_async_copy(act_hbm, act.at[pl.ds(0, 2 * WIDTH)], sems.at[2]),
        pltpu.make_async_copy(tail_hbm, act.at[pl.ds(2 * WIDTH, PE_BLOCK)], sems.at[3]),
    ]
    first_load.start()
    for copy in loads:
        copy.start()
    for copy in small[:5]:
        copy.wait()
    xs[...] = x_ref[...].astype(F32)
    tables_f = (left_ref[...], right_ref[...], tc_ref[...], ts_ref[...])
    pairs = range(CHANNELS // 2)

    def signal(kind, pair):
        return jnp.concatenate(
            [xs[pl.ds(kind * CHANNELS + 2 * pair + j, HALF_ROWS, stride=DATA), :] for j in range(2)], axis=1
        )

    def rows(pair):
        return slice(pair * 2 * KROWS, (pair + 1) * 2 * KROWS)

    def lanes(pair):
        return slice(pair * 2 * RADIX, (pair + 1) * 2 * RADIX)

    def emit_filter(o, pair, value):
        for j in range(2):
            dh[pl.ds(2 * (2 * pair + j) + o, HALF_ROWS, stride=ROWS), :] = value[:, j * RADIX : (j + 1) * RADIX]

    for p in pairs:
        sv[rows(p), :] = forward_pair(signal(0, p).astype(BF16), *tables_f)
    for p in pairs:
        sg2[rows(p), :] = forward_pair(signal(2, p).astype(BF16), *tables_f)
    first_load.wait()
    for copy in small[5:]:
        copy.wait()
    tables_i = (back_ref[...], inv_ref[...], tc_ref[...], ts_ref[...])
    for p in pairs:
        conv[:, lanes(p)] = inverse_pair(spectral_product(spec[0, rows(p), :], sv[rows(p), :], 1, 1), *tables_i)
    for p in pairs:
        dz[:, lanes(p)] = inverse_pair(spectral_product(spec[1, rows(p), :], sg2[rows(p), :], -1, 1), *tables_i)
    for p in pairs:
        gated = (signal(1, p) * conv[:, lanes(p)]).astype(BF16)
        sz[rows(p), :] = forward_pair(gated, *tables_f)
    for p in pairs:
        prod[:, lanes(p)] = (dz[:, lanes(p)] * conv[:, lanes(p)]).astype(BF16)
        grad = (dz[:, lanes(p)] * signal(1, p)).astype(BF16)
        sg1[rows(p), :] = forward_pair(grad, *tables_f)
    stores = [
        pltpu.make_async_copy(sz, sz_hbm, sems.at[4]),
        pltpu.make_async_copy(sg1, sg1_hbm, sems.at[5]),
        pltpu.make_async_copy(prod, prod_hbm, sems.at[6]),
    ]
    for copy in stores:
        copy.start()
    for p in pairs:
        emit_filter(1, p, inverse_pair(spectral_product(sg2[rows(p), :], sz[rows(p), :], 1, -1), *tables_i))
    for p in pairs:
        emit_filter(0, p, inverse_pair(spectral_product(sg1[rows(p), :], sv[rows(p), :], 1, -1), *tables_i))

    span = 256
    columns = [slice(i * span, (i + 1) * span) for i in range(SEQLEN // span)]
    wide_rate = jnp.concatenate([rate_ref[...]] * (span // RADIX), axis=1)
    for cols in columns:
        first = cols.start // RADIX
        wide = jnp.concatenate([dh[(first + i) * ROWS : (first + i + 1) * ROWS, :] for i in range(span // RADIX)], axis=1)
        grad = wide * (jnp.exp(-wide_rate * ramp_ref[:, cols]) * (1.0 / SEQLEN))
        stat[2 * WIDTH :, cols] = grad.astype(BF16)
    for copy in loads:
        copy.wait()
    for cols in columns:
        stat[:WIDTH, cols] = (dot(own_ref[:WIDTH, :ROWS], stat[2 * WIDTH :, cols]) * cos[WIDTH:, cols].astype(F32)).astype(BF16)
    for cols in columns:
        stat[WIDTH : 2 * WIDTH, cols] = (
            dot(own_ref[WIDTH:, :WIDTH], stat[:WIDTH, cols]) * cos[:WIDTH, cols].astype(F32)
        ).astype(BF16)
    acc[...] = dot_last(act[...], stat[...])
    out_ref[...] = acc[WIDTH : 2 * WIDTH, 2 * WIDTH :].T
    tail = 2 * WIDTH
    share_ref[...] = jnp.zeros_like(share_ref)
    share_ref[:, :WIDTH] = acc[:WIDTH, :WIDTH]
    share_ref[:PE_BLOCK, WIDTH:] = acc[tail:, WIDTH : 2 * WIDTH]
    share_ref[PE_BLOCK : PE_BLOCK + 8, WIDTH:] = acc[tail + 32 :, :WIDTH]
    for copy in stores:
        copy.wait()


def output_kernel(
    spec_hbm, sz_hbm, sg1_hbm, prod_hbm, back_hbm, inv_hbm, tc_hbm, ts_hbm,
    y_hbm,
    spec, sz, sg1, prod, back_ref, inv_ref, tc_ref, ts_ref, ys, data, sems,
):
    sources = (spec_hbm.at[1], sz_hbm, inv_hbm, tc_hbm, ts_hbm, back_hbm, spec_hbm.at[0], sg1_hbm, prod_hbm)
    targets = (spec.at[1], sz, inv_ref, tc_ref, ts_ref, back_ref, spec.at[0], sg1, prod)
    loads = [pltpu.make_async_copy(s, d, sems.at[i]) for i, (s, d) in enumerate(zip(sources, targets))]
    for copy in loads:
        copy.start()
    for copy in loads[:6]:
        copy.wait()
    tables_i = (back_ref[...], inv_ref[...], tc_ref[...], ts_ref[...])

    def emit(kind, pair, value):
        for j in range(2):
            ys[pl.ds(kind * CHANNELS + 2 * pair + j, HALF_ROWS, stride=DATA), :] = value[
                :, j * RADIX : (j + 1) * RADIX
            ]

    for p in range(CHANNELS // 2):
        rows = slice(p * 2 * KROWS, (p + 1) * 2 * KROWS)
        emit(0, p, inverse_pair(spectral_product(spec[1, rows, :], sz[rows, :], 1, 1), *tables_i))
    for copy in loads[6:]:
        copy.wait()
    for p in range(CHANNELS // 2):
        rows = slice(p * 2 * KROWS, (p + 1) * 2 * KROWS)
        emit(2, p, inverse_pair(spectral_product(spec[0, rows, :], sg1[rows, :], -1, 1), *tables_i))
        emit(1, p, prod[:, p * 2 * RADIX : (p + 1) * 2 * RADIX].astype(F32))
    for i in range(HALF_ROWS):
        data[i] = ys[i * DATA : (i + 1) * DATA, :].astype(BF16)
    last = pltpu.make_async_copy(data, y_hbm.at[:, pl.ds(0, DATA), :], sems.at[9])
    last.start()
    last.wait()


def total_kernel(y_in, near_ref, y_out, parts, sem):
    total = jnp.sum(near_ref[...], axis=0).astype(BF16)
    parts[...] = jnp.broadcast_to(total[None], parts.shape)
    copy = pltpu.make_async_copy(parts, y_out.at[:, pl.ds(DATA, SHARE), :], sem)
    copy.start()
    copy.wait()


def finish_kernel(back_ref, cot_ref, value_ref, first_ref, second_ref, pos_ref, pos_bias_ref, mid_ref, mid_bias_ref, total):
    step = pl.program_id(0)
    value_ref[...] = back_ref[:, 2 * CHANNELS : DATA, :]
    first_ref[...] = back_ref[:, CHANNELS : 2 * CHANNELS, :]
    second_ref[...] = (cot_ref[...].astype(F32) * back_ref[:, :CHANNELS, :].astype(F32)).astype(BF16)
    part = jnp.zeros(total.shape, F32)
    for i in range(back_ref.shape[0] // PEERS):
        part = part + back_ref[i * PEERS : (i + 1) * PEERS, DATA:, :].astype(F32)

    @pl.when(step == 0)
    def _():
        total[...] = part

    @pl.when(step > 0)
    def _():
        total[...] += part

    @pl.when(step == pl.num_programs(0) - 1)
    def _():
        whole = jnp.concatenate([total[j] for j in range(PEERS)], axis=0)
        mid_ref[...] = whole.T[:WIDTH, :]
        pos_ref[...] = whole[:PE, WIDTH:]
        pos_bias_ref[...] = whole[PE : PE + 1, WIDTH:]
        mid_bias_ref[...] = whole[PE_BLOCK + 1 : PE_BLOCK + 2, WIDTH:]


def full(shape):
    return pl.BlockSpec(shape, lambda i: (0,) * len(shape))


def params(limit=VMEM_BYTES):
    return pltpu.CompilerParams(vmem_limit_bytes=limit)


def pack(value, first, second, cot):
    anywhere = pl.BlockSpec(memory_space=pltpu.HBM)
    buffer = pltpu.VMEM(value.shape, BF16)
    return pl.pallas_call(
        pack_kernel,
        in_specs=[anywhere] * 4,
        out_specs=anywhere,
        out_shape=jax.ShapeDtypeStruct((value.shape[0], DATA, RADIX), BF16),
        scratch_shapes=[buffer] * 2
        + [pltpu.VMEM((value.shape[0], DATA, RADIX), BF16), pltpu.SemaphoreType.DMA((5 * PACK_PARTS,))],
        compiler_params=params(),
        cost_estimate=pl.CostEstimate(flops=1 << 17, bytes_accessed=1 << 20, transcendentals=0),
    )(value, first, second, cot)


def network_forward(pos_weight, pos_bias, mid_weight, mid_bias, out_weight, decay_rates, tables, stack, ramp):
    left, back, right, right_inv, twid_cos, twid_sin = tables
    block = pl.BlockSpec((2 * WIDTH, NET_CHUNK), lambda i: (0, i))
    tabs = (left, right, twid_cos, twid_sin)
    args = (pos_weight.T, pos_bias[None, :], mid_weight, mid_bias[None, :], out_weight.T, decay_rates[None, :])
    outs = [
        jax.ShapeDtypeStruct((2 * WIDTH, SEQLEN), BF16),
        jax.ShapeDtypeStruct((2 * WIDTH, SEQLEN), BF16),
        jax.ShapeDtypeStruct((2, CHANNELS * KROWS, 2 * RADIX), F32),
        jax.ShapeDtypeStruct((2 * WIDTH, RADIX), BF16),
        jax.ShapeDtypeStruct((ROWS, RADIX), F32),
    ]
    return pl.pallas_call(
        network_kernel,
        grid=(SEQLEN // NET_CHUNK,),
        in_specs=[block, pl.BlockSpec((1, NET_CHUNK), lambda i: (0, i))]
        + [full(a.shape) for a in tabs]
        + [full(a.shape) for a in args],
        out_specs=[block] * 2 + [full(o.shape) for o in outs[2:]],
        out_shape=outs,
        scratch_shapes=[
            pltpu.VMEM((HALF_ROWS * ROWS, RADIX), F32),
            pltpu.VMEM((RADIX, RADIX), F32),
            pltpu.VMEM((2 * WIDTH, 2 * WIDTH), BF16),
            pltpu.VMEM((2 * WIDTH, 2 * WIDTH), BF16),
            pltpu.VMEM((2 * ROWS, 2 * WIDTH), BF16),
            pltpu.VMEM((WIDTH, RADIX), F32),
            pltpu.VMEM((ROWS, RADIX), F32),
        ],
        compiler_params=params(),
        cost_estimate=pl.CostEstimate(flops=1 << 30, bytes_accessed=10 << 20, transcendentals=1 << 20),
    )(stack, ramp, *tabs, *args)


def chain(x, net, tables, tail, ramp):
    act, cos, spec, own, own_rate = net
    left, back, right, right_inv, twid_cos, twid_sin = tables
    spectrum = pltpu.VMEM((CHANNELS * KROWS, 2 * RADIX), F32)
    wide = pltpu.VMEM((HALF_ROWS, CHANNELS * RADIX), F32)
    tall = 2 * WIDTH + PE_BLOCK
    small = (x, left, back, right, right_inv, twid_cos, twid_sin, own, own_rate, ramp)
    anywhere = pl.BlockSpec(memory_space=pltpu.HBM)
    within = pl.BlockSpec(memory_space=pltpu.VMEM)
    return pl.pallas_call(
        chain_kernel,
        in_specs=[anywhere] * 14,
        out_specs=[within] * 2 + [anywhere] * 3,
        out_shape=[
            jax.ShapeDtypeStruct((WIDTH, RADIX), F32),
            jax.ShapeDtypeStruct((ROWS, WIDTH), F32),
            jax.ShapeDtypeStruct((CHANNELS * KROWS, 2 * RADIX), F32),
            jax.ShapeDtypeStruct((CHANNELS * KROWS, 2 * RADIX), F32),
            jax.ShapeDtypeStruct((HALF_ROWS, CHANNELS * RADIX), BF16),
        ],
        scratch_shapes=[pltpu.VMEM(a.shape, a.dtype) for a in small]
        + [pltpu.VMEM(x.shape, F32)]
        + [spectrum] * 4
        + [wide] * 2
        + [
            pltpu.VMEM((HALF_ROWS, CHANNELS * RADIX), BF16),
            pltpu.VMEM((HALF_ROWS * ROWS, RADIX), F32),
            pltpu.VMEM(spec.shape, F32),
            pltpu.VMEM((tall, SEQLEN), BF16),
            pltpu.VMEM((2 * WIDTH, SEQLEN), BF16),
            pltpu.VMEM((2 * WIDTH + ROWS, SEQLEN), BF16),
            pltpu.VMEM((tall, 2 * WIDTH + ROWS), F32),
            pltpu.SemaphoreType.DMA((7 + len(small),)),
        ],
        compiler_params=params(CHAIN_BYTES),
        cost_estimate=pl.CostEstimate(flops=3 << 30, bytes_accessed=8 << 20, transcendentals=1 << 17),
    )(*small, spec, act, cos, tail)


def outputs(spec, sz, sg1, prod, tables):
    left, back, right, right_inv, twid_cos, twid_sin = tables
    anywhere = pl.BlockSpec(memory_space=pltpu.HBM)
    args = (spec, sz, sg1, prod, back, right_inv, twid_cos, twid_sin)
    return pl.pallas_call(
        output_kernel,
        in_specs=[anywhere] * len(args),
        out_specs=anywhere,
        out_shape=jax.ShapeDtypeStruct((HALF_ROWS, SEND, RADIX), BF16),
        scratch_shapes=[pltpu.VMEM(a.shape, a.dtype) for a in args]
        + [
            pltpu.VMEM((HALF_ROWS * DATA, RADIX), F32),
            pltpu.VMEM((HALF_ROWS, DATA, RADIX), BF16),
            pltpu.SemaphoreType.DMA((len(args) + 2,)),
        ],
        compiler_params=params(),
        cost_estimate=pl.CostEstimate(flops=1 << 29, bytes_accessed=4 << 20, transcendentals=0),
    )(*args)


def add_total(y, near):
    anywhere = pl.BlockSpec(memory_space=pltpu.HBM)
    return pl.pallas_call(
        total_kernel,
        in_specs=[anywhere, pl.BlockSpec(memory_space=pltpu.VMEM)],
        out_specs=anywhere,
        out_shape=jax.ShapeDtypeStruct(y.shape, BF16),
        input_output_aliases={0: 0},
        scratch_shapes=[pltpu.VMEM((y.shape[0], SHARE, RADIX), BF16), pltpu.SemaphoreType.DMA(())],
        compiler_params=params(ADD_BYTES),
        cost_estimate=pl.CostEstimate(flops=1 << 16, bytes_accessed=1 << 17, transcendentals=0),
    )(y, near)


def finish(back, cot):
    devices = cot.shape[0]
    steps = 2
    data = pl.BlockSpec((devices // steps, CHANNELS, RADIX), lambda i: (i, 0, 0))
    outs = [jax.ShapeDtypeStruct(cot.shape, BF16)] * 3 + [
        jax.ShapeDtypeStruct((PE, WIDTH), F32),
        jax.ShapeDtypeStruct((1, WIDTH), F32),
        jax.ShapeDtypeStruct((WIDTH, WIDTH), F32),
        jax.ShapeDtypeStruct((1, WIDTH), F32),
    ]
    return pl.pallas_call(
        finish_kernel,
        grid=(steps,),
        in_specs=[pl.BlockSpec((devices // steps, SEND, RADIX), lambda i: (i, 0, 0)), data],
        out_specs=[data] * 3 + [full(o.shape) for o in outs[3:]],
        out_shape=outs,
        scratch_shapes=[pltpu.VMEM((PEERS, SHARE, RADIX), F32)],
        compiler_params=params(FIN_BYTES),
        cost_estimate=pl.CostEstimate(flops=1 << 20, bytes_accessed=1 << 20, transcendentals=0),
    )(back, cot)


SEQ = ("z", "yhi", "ylo", "x")
NEAR = ("ylo", "x")


def on_device(
    value_branch, first_gate, second_gate, out_cotangent,
    pos_weight, pos_bias, mid_weight, mid_bias, out_weight, decay_rates,
):
    devices = lax.axis_size(SEQ)
    tables = dft_tables()
    stack, tail = feature_tables()
    ramp = (np.arange(SEQLEN) / SEQLEN).astype(np.float32)[None, :]
    blocks = (devices, CHANNELS, RADIX)
    cot = out_cotangent.reshape(blocks)
    sent = pack(value_branch.reshape(blocks), first_gate.reshape(blocks), second_gate.reshape(blocks), cot)
    x = lax.all_to_all(sent, SEQ, 0, 0, tiled=True)
    net = network_forward(
        pos_weight, pos_bias, mid_weight, mid_bias, out_weight, decay_rates, tables, stack, ramp
    )
    share, out_weight_grad, sz, sg1, prod = chain(x.reshape(HALF_ROWS * DATA, RADIX), net, tables, tail, ramp)
    near = lax.all_to_all(share.reshape(PEERS, SHARE, RADIX), NEAR, 0, 0, tiled=True)
    y = outputs(net[2], sz, sg1, prod, tables)
    back = lax.all_to_all(add_total(y, near), SEQ, 0, 0, tiled=True)
    value_grad, first_grad, second_grad, pos_grad, pos_bias_grad, mid_grad, mid_bias_grad = finish(back, cot)
    shape = value_branch.shape
    return (
        value_grad.reshape(shape),
        first_grad.reshape(shape),
        second_grad.reshape(shape),
        pos_grad.T,
        pos_bias_grad[0],
        mid_grad,
        mid_bias_grad[0],
        out_weight_grad,
    )


def solution(mesh):
    grid = Mesh(mesh.devices.reshape(mesh.shape["dp"], 2, 4, 2, 4), ("dp",) + SEQ)
    part = P(None, ("dp",) + SEQ)
    in_specs = (part,) * 4 + (P(),) * 6
    out_specs = (part,) * 3 + (P("dp", None), P("dp"), P("dp", None), P("dp"), P(SEQ, "dp"))
    return jax.shard_map(on_device, mesh=grid, in_specs=in_specs, out_specs=out_specs, check_vma=False)
```

```python
import math

import jax
import jax.numpy as jnp
import numpy as np
from jax import lax
from jax.experimental import pallas as pl
from jax.experimental.pallas import tpu as pltpu
from jax.sharding import Mesh
from jax.sharding import PartitionSpec as P

F32 = jnp.float32
BF16 = jnp.bfloat16
RADIX = 128
HALF_ROWS = 64
SEQLEN = HALF_ROWS * RADIX
KROWS = 72
WIDTH = 64
PE = 33
PE_BLOCK = 40
NET_CHUNK = 8192
CHANNELS = 8
ROWS = 2 * CHANNELS
SHARE = 8
DATA = 3 * CHANNELS
SEND = DATA + SHARE
PEERS = 8
PACK_PARTS = 2
ADD_BYTES = 64 << 20
FIN_BYTES = 64 << 20
VMEM_BYTES = 64 << 20
CHAIN_BYTES = 64 << 20


def dft_tables():
    n1, n2 = 2 * HALF_ROWS, RADIX
    k1 = np.arange(KROWS)[:, None]
    live = (k1 <= n1 // 2).astype(np.float64)
    angle_one = 2.0 * np.pi * ((k1 * np.arange(n1 // 2)[None, :]) % n1) / n1
    cos_one = np.cos(angle_one) * live
    sin_one = np.sin(angle_one) * live
    left = np.concatenate([cos_one, -sin_one], axis=0)
    weight = np.where((k1 == 0) | (k1 == n1 // 2), 1.0, 2.0) / (n1 * n2)
    back = np.concatenate([cos_one * weight, -sin_one * weight], axis=0).T
    grid = np.arange(n2)
    angle_two = 2.0 * np.pi * ((grid[:, None] * grid[None, :]) % n2) / n2
    cos_two, sin_two = np.cos(angle_two), np.sin(angle_two)
    right = np.block([[cos_two, -sin_two], [sin_two, cos_two]])
    right_inv = np.block([[cos_two, sin_two], [-sin_two, cos_two]])
    angle_tw = 2.0 * np.pi * ((k1 * grid[None, :]) % (n1 * n2)) / (n1 * n2)
    bf = lambda a: np.asarray(a, np.float32).astype(jnp.bfloat16)
    return (
        bf(left),
        bf(back),
        bf(right),
        bf(right_inv),
        np.cos(angle_tw).astype(np.float32),
        np.sin(angle_tw).astype(np.float32),
    )


def features():
    positions = np.arange(SEQLEN)
    bands = np.arange(1, (PE - 1) // 2 + 1)
    angles = 2.0 * np.pi * ((bands[:, None] * positions[None, :]) % SEQLEN) / SEQLEN
    ramp = positions[None, :] / SEQLEN
    return np.concatenate([ramp, np.cos(angles), np.sin(angles)], axis=0).astype(np.float32)


def np_split(value, parts):
    pieces = []
    for _ in range(parts):
        piece = value.astype(jnp.bfloat16)
        pieces.append(piece)
        value = value - piece.astype(np.float32)
    return pieces


def feature_tables():
    table = np.zeros((PE_BLOCK, SEQLEN), np.float32)
    table[:PE] = features()
    table[PE] = 1.0
    pieces = np_split(table, 3)
    pad = np.zeros((2 * WIDTH - 3 * PE_BLOCK, SEQLEN), jnp.bfloat16)
    return np.concatenate(pieces + [pad], axis=0), pieces[0]


def poly_tables():
    top = math.pi**2 * 1.0001
    nodes = (np.cos(np.pi * (np.arange(64) + 0.5) / 64) + 1) * top / 2
    root = np.sqrt(nodes)
    cheb = np.polynomial.chebyshev.Chebyshev
    sin_fit = cheb.fit(nodes, math.sqrt(2) * np.sin(root / 2) / root, 4, domain=[0, top])
    cos_fit = cheb.fit(nodes, math.sqrt(2) * np.cos(root / 2), 4, domain=[0, top])
    to_poly = lambda c: [float(x) for x in c.convert(kind=np.polynomial.Polynomial).coef]
    return to_poly(sin_fit), to_poly(cos_fit)


SIN_COEF, COS_COEF = poly_tables()
TURN_HI = 6.28125
TURN_LO = float(np.float32(2 * math.pi - TURN_HI))


def sin_cos(value):
    turns = jnp.round(value * (0.5 / math.pi))
    rest = (value - turns * TURN_HI) - turns * TURN_LO
    square = rest * rest

    def horner(coefs):
        total = square * coefs[-1] + coefs[-2]
        for coef in coefs[-3::-1]:
            total = total * square + coef
        return total

    half = rest * horner(SIN_COEF)
    return half * horner(COS_COEF), 1.0 - half * half


def dot(left, right):
    return lax.dot_general(left, right, (((1,), (0,)), ((), ())), preferred_element_type=F32)


def dot_last(left, right):
    return lax.dot_general(left, right, (((1,), (1,)), ((), ())), preferred_element_type=F32)


def split_two(value):
    high = value.astype(BF16)
    return high, (value - high.astype(F32)).astype(BF16)


def forward_pair(signal, left, right, twid_cos, twid_sin):
    stacked = dot(left, signal)
    rows = []
    for j in range(2):
        cols = slice(j * RADIX, (j + 1) * RADIX)
        real_a, imag_a = stacked[:KROWS, cols], stacked[KROWS:, cols]
        real_b = real_a * twid_cos + imag_a * twid_sin
        imag_b = imag_a * twid_cos - real_a * twid_sin
        rows.append(jnp.concatenate([real_b, imag_b], axis=1))
    return dot(jnp.concatenate(rows, axis=0).astype(BF16), right)


def inverse_pair(product, back, right_inv, twid_cos, twid_sin):
    section = dot(product, right_inv)
    cols = []
    for j in range(2):
        real_q = section[j * KROWS : (j + 1) * KROWS, :RADIX]
        imag_q = section[j * KROWS : (j + 1) * KROWS, RADIX:]
        real_r = real_q * twid_cos - imag_q * twid_sin
        imag_r = imag_q * twid_cos + real_q * twid_sin
        cols.append(jnp.concatenate([real_r, imag_r], axis=0))
    return dot(back, jnp.concatenate(cols, axis=1).astype(BF16))


def spectral_product(left, right, sign_left, sign_right):
    left_re, left_im = left[:, :RADIX], left[:, RADIX:]
    right_re, right_im = right[:, :RADIX], right[:, RADIX:]
    cross = left_im * right_im
    real = left_re * right_re + cross if sign_left * sign_right < 0 else left_re * right_re - cross
    one, two = left_im * right_re, left_re * right_im
    if sign_left > 0:
        imag = one + two if sign_right > 0 else one - two
    else:
        imag = two - one
    return jnp.concatenate([real.astype(BF16), imag.astype(BF16)], axis=1)


def pack_kernel(v_hbm, x1_hbm, x2_hbm, cot_hbm, out_hbm, x2, cot, sent, sems):
    size = x2.shape[0] // PACK_PARTS
    spans = [pl.ds(i * size, size) for i in range(PACK_PARTS)]
    loads, stores = [], []
    for i, span in enumerate(spans):
        moves = (
            (v_hbm.at[span], sent.at[span, pl.ds(0, CHANNELS)]),
            (x1_hbm.at[span], sent.at[span, pl.ds(CHANNELS, CHANNELS)]),
            (x2_hbm.at[span], x2.at[span]),
            (cot_hbm.at[span], cot.at[span]),
        )
        loads.append([pltpu.make_async_copy(src, dst, sems.at[5 * i + j]) for j, (src, dst) in enumerate(moves)])
        for copy in loads[-1]:
            copy.start()
    for i, span in enumerate(spans):
        for copy in loads[i]:
            copy.wait()
        sent[span, 2 * CHANNELS :, :] = (cot[span].astype(F32) * x2[span].astype(F32)).astype(BF16)
        stores.append(pltpu.make_async_copy(sent.at[span], out_hbm.at[span], sems.at[5 * i + 4]))
        stores[-1].start()
    for copy in stores:
        copy.wait()


def network_kernel(
    pe_ref, ramp_ref, left_ref, right_ref, tc_ref, ts_ref,
    pos_ref, pos_bias_ref, mid_ref, mid_bias_ref, out_ref, rate_ref,
    act_ref, cos_ref, spec_ref, own_ref, own_rate_ref,
    filt, square, wp, wm, wo, bias, decay,
):
    step = pl.program_id(0)

    @pl.when(step == 0)
    def _():
        rank = lax.axis_index(SEQ)
        lane = pl.multiple_of(rank // 8 * RADIX, RADIX)
        first = pl.multiple_of(rank % 8 * ROWS, ROWS)

        square[...] = jnp.zeros_like(square)
        for i in range(3):
            square[i * PE_BLOCK : i * PE_BLOCK + PE, :WIDTH] = pos_ref[...]
            square[i * PE_BLOCK + PE : i * PE_BLOCK + PE + 1, :WIDTH] = pos_bias_ref[...]
        wp[...] = jnp.concatenate(split_two(square[...].T[:WIDTH, :]), axis=0)

        square[...] = jnp.zeros_like(square)
        square[:WIDTH, :WIDTH] = mid_ref[...]
        own_ref[WIDTH:, :] = square[...].T[:WIDTH, :].astype(BF16)
        square[:WIDTH, WIDTH:] = mid_ref[...]
        wm[...] = jnp.concatenate(split_two(square[:WIDTH, :]), axis=0)

        square[:, :WIDTH] = jnp.broadcast_to(mid_bias_ref[...], (RADIX, WIDTH))
        bias[...] = square[...].T[:WIDTH, :]

        square[...] = jnp.broadcast_to(rate_ref[:, pl.ds(lane, RADIX)], (RADIX, RADIX)).T
        decay[...] = square[pl.ds(first, ROWS), :]
        own_rate_ref[...] = decay[...]

        block = out_ref[:, pl.ds(lane, RADIX)]
        square[...] = jnp.concatenate([block, block], axis=0).T
        mine = square[pl.ds(first, ROWS), :]
        wo[...] = jnp.concatenate(split_two(mine), axis=0)
        square[...] = jnp.zeros_like(square)
        square[:ROWS, :] = mine
        own_ref[:WIDTH, :] = square[...].T[:WIDTH, :].astype(BF16)

    span = 256
    parts = [slice(p * span, (p + 1) * span) for p in range(NET_CHUNK // span)]
    wide_bias = jnp.concatenate([bias[...]] * (span // RADIX), axis=1)
    wide_rate = jnp.concatenate([decay[...]] * (span // RADIX), axis=1)
    pres = []
    for cols in parts:
        both = dot(wp[...], pe_ref[:, cols])
        pres.append(both[:WIDTH] + both[WIDTH:])
    stacks = []
    for pre, cols in zip(pres, parts):
        act, slope = sin_cos(pre)
        pieces = split_two(act)
        act_ref[:WIDTH, cols] = pieces[0]
        cos_ref[:WIDTH, cols] = slope.astype(BF16)
        stacks.append(jnp.concatenate(pieces, axis=0))
    pres = []
    for stack in stacks:
        both = dot(wm[...], stack)
        pres.append(both[:WIDTH] + both[WIDTH:] + wide_bias)
    stacks = []
    for pre, cols in zip(pres, parts):
        act, slope = sin_cos(pre)
        pieces = split_two(act)
        act_ref[WIDTH:, cols] = pieces[0]
        cos_ref[WIDTH:, cols] = slope.astype(BF16)
        stacks.append(jnp.concatenate(pieces, axis=0))
    for part, (stack, cols) in enumerate(zip(stacks, parts)):
        both = dot(wo[...], stack)
        rows = (both[:ROWS] + both[ROWS:]) * jnp.exp(-wide_rate * ramp_ref[:, cols])
        for j in range(span // RADIX):
            base = pl.multiple_of(step * (NET_CHUNK // RADIX * ROWS) + (part * (span // RADIX) + j) * ROWS, ROWS)
            filt[pl.ds(base, ROWS), :] = rows[:, j * RADIX : (j + 1) * RADIX]

    @pl.when(step == SEQLEN // NET_CHUNK - 1)
    def _():
        for o in range(2):
            for pair in range(CHANNELS // 2):
                signal = jnp.concatenate(
                    [filt[pl.ds(2 * (2 * pair + j) + o, HALF_ROWS, stride=ROWS), :] for j in range(2)], axis=1
                ).astype(BF16)
                spec_ref[o, pair * 2 * KROWS : (pair + 1) * 2 * KROWS, :] = forward_pair(
                    signal, left_ref[...], right_ref[...], tc_ref[...], ts_ref[...]
                )


def chain_kernel(
    x_hbm, left_hbm, back_hbm, right_hbm, inv_hbm, tc_hbm, ts_hbm, own_hbm, rate_hbm, ramp_hbm,
    spec_hbm, act_hbm, cos_hbm, tail_hbm,
    share_ref, out_ref, sz_hbm, sg1_hbm, prod_hbm,
    x_ref, left_ref, back_ref, right_ref, inv_ref, tc_ref, ts_ref, own_ref, rate_ref, ramp_ref,
    xs, sv, sg2, sz, sg1, conv, dz, prod, dh, spec, act, cos, stat, acc, sems,
):
    sources = (x_hbm, left_hbm, right_hbm, tc_hbm, ts_hbm, back_hbm, inv_hbm, own_hbm, rate_hbm, ramp_hbm)
    targets = (x_ref, left_ref, right_ref, tc_ref, ts_ref, back_ref, inv_ref, own_ref, rate_ref, ramp_ref)
    small = [pltpu.make_async_copy(s, d, sems.at[7 + i]) for i, (s, d) in enumerate(zip(sources, targets))]
    for copy in small:
        copy.start()
    first_load = pltpu.make_async_copy(spec_hbm, spec, sems.at[0])
    loads = [
        pltpu.make_async_copy(cos_hbm, cos, sems.at[1]),
        pltpu.make_async_copy(act_hbm, act.at[pl.ds(0, 2 * WIDTH)], sems.at[2]),
        pltpu.make_async_copy(tail_hbm, act.at[pl.ds(2 * WIDTH, PE_BLOCK)], sems.at[3]),
    ]
    first_load.start()
    for copy in loads:
        copy.start()
    for copy in small[:5]:
        copy.wait()
    xs[...] = x_ref[...].astype(F32)
    tables_f = (left_ref[...], right_ref[...], tc_ref[...], ts_ref[...])
    pairs = range(CHANNELS // 2)

    def signal(kind, pair):
        return jnp.concatenate(
            [xs[pl.ds(kind * CHANNELS + 2 * pair + j, HALF_ROWS, stride=DATA), :] for j in range(2)], axis=1
        )

    def rows(pair):
        return slice(pair * 2 * KROWS, (pair + 1) * 2 * KROWS)

    def lanes(pair):
        return slice(pair * 2 * RADIX, (pair + 1) * 2 * RADIX)

    def emit_filter(o, pair, value):
        for j in range(2):
            dh[pl.ds(2 * (2 * pair + j) + o, HALF_ROWS, stride=ROWS), :] = value[:, j * RADIX : (j + 1) * RADIX]

    for p in pairs:
        sv[rows(p), :] = forward_pair(signal(0, p).astype(BF16), *tables_f)
    for p in pairs:
        sg2[rows(p), :] = forward_pair(signal(2, p).astype(BF16), *tables_f)
    first_load.wait()
    for copy in small[5:]:
        copy.wait()
    tables_i = (back_ref[...], inv_ref[...], tc_ref[...], ts_ref[...])
    for p in pairs:
        conv[:, lanes(p)] = inverse_pair(spectral_product(spec[0, rows(p), :], sv[rows(p), :], 1, 1), *tables_i)
    for p in pairs:
        dz[:, lanes(p)] = inverse_pair(spectral_product(spec[1, rows(p), :], sg2[rows(p), :], -1, 1), *tables_i)
    for p in pairs:
        gated = (signal(1, p) * conv[:, lanes(p)]).astype(BF16)
        sz[rows(p), :] = forward_pair(gated, *tables_f)
    for p in pairs:
        prod[:, lanes(p)] = (dz[:, lanes(p)] * conv[:, lanes(p)]).astype(BF16)
        grad = (dz[:, lanes(p)] * signal(1, p)).astype(BF16)
        sg1[rows(p), :] = forward_pair(grad, *tables_f)
    stores = [
        pltpu.make_async_copy(sz, sz_hbm, sems.at[4]),
        pltpu.make_async_copy(sg1, sg1_hbm, sems.at[5]),
        pltpu.make_async_copy(prod, prod_hbm, sems.at[6]),
    ]
    for copy in stores:
        copy.start()
    for p in pairs:
        emit_filter(1, p, inverse_pair(spectral_product(sg2[rows(p), :], sz[rows(p), :], 1, -1), *tables_i))
    for p in pairs:
        emit_filter(0, p, inverse_pair(spectral_product(sg1[rows(p), :], sv[rows(p), :], 1, -1), *tables_i))

    span = 256
    columns = [slice(i * span, (i + 1) * span) for i in range(SEQLEN // span)]
    wide_rate = jnp.concatenate([rate_ref[...]] * (span // RADIX), axis=1)
    for cols in columns:
        first = cols.start // RADIX
        wide = jnp.concatenate([dh[(first + i) * ROWS : (first + i + 1) * ROWS, :] for i in range(span // RADIX)], axis=1)
        grad = wide * (jnp.exp(-wide_rate * ramp_ref[:, cols]) * (1.0 / SEQLEN))
        stat[2 * WIDTH :, cols] = grad.astype(BF16)
    for copy in loads:
        copy.wait()
    for cols in columns:
        stat[:WIDTH, cols] = (dot(own_ref[:WIDTH, :ROWS], stat[2 * WIDTH :, cols]) * cos[WIDTH:, cols].astype(F32)).astype(BF16)
    for cols in columns:
        stat[WIDTH : 2 * WIDTH, cols] = (
            dot(own_ref[WIDTH:, :WIDTH], stat[:WIDTH, cols]) * cos[:WIDTH, cols].astype(F32)
        ).astype(BF16)
    acc[...] = dot_last(act[...], stat[...])
    out_ref[...] = acc[WIDTH : 2 * WIDTH, 2 * WIDTH :].T
    tail = 2 * WIDTH
    share_ref[...] = jnp.zeros_like(share_ref)
    share_ref[:, :WIDTH] = acc[:WIDTH, :WIDTH]
    share_ref[:PE_BLOCK, WIDTH:] = acc[tail:, WIDTH : 2 * WIDTH]
    share_ref[PE_BLOCK : PE_BLOCK + 8, WIDTH:] = acc[tail + 32 :, :WIDTH]
    for copy in stores:
        copy.wait()


def output_kernel(
    spec_hbm, sz_hbm, sg1_hbm, prod_hbm, back_hbm, inv_hbm, tc_hbm, ts_hbm,
    y_hbm,
    spec, sz, sg1, prod, back_ref, inv_ref, tc_ref, ts_ref, ys, data, sems,
):
    sources = (spec_hbm.at[1], sz_hbm, inv_hbm, tc_hbm, ts_hbm, back_hbm, spec_hbm.at[0], sg1_hbm, prod_hbm)
    targets = (spec.at[1], sz, inv_ref, tc_ref, ts_ref, back_ref, spec.at[0], sg1, prod)
    loads = [pltpu.make_async_copy(s, d, sems.at[i]) for i, (s, d) in enumerate(zip(sources, targets))]
    for copy in loads:
        copy.start()
    for copy in loads[:6]:
        copy.wait()
    tables_i = (back_ref[...], inv_ref[...], tc_ref[...], ts_ref[...])

    def emit(kind, pair, value):
        for j in range(2):
            ys[pl.ds(kind * CHANNELS + 2 * pair + j, HALF_ROWS, stride=DATA), :] = value[
                :, j * RADIX : (j + 1) * RADIX
            ]

    for p in range(CHANNELS // 2):
        rows = slice(p * 2 * KROWS, (p + 1) * 2 * KROWS)
        emit(0, p, inverse_pair(spectral_product(spec[1, rows, :], sz[rows, :], 1, 1), *tables_i))
    for copy in loads[6:]:
        copy.wait()
    for p in range(CHANNELS // 2):
        rows = slice(p * 2 * KROWS, (p + 1) * 2 * KROWS)
        emit(2, p, inverse_pair(spectral_product(spec[0, rows, :], sg1[rows, :], -1, 1), *tables_i))
        emit(1, p, prod[:, p * 2 * RADIX : (p + 1) * 2 * RADIX].astype(F32))
    for i in range(HALF_ROWS):
        data[i] = ys[i * DATA : (i + 1) * DATA, :].astype(BF16)
    last = pltpu.make_async_copy(data, y_hbm.at[:, pl.ds(0, DATA), :], sems.at[9])
    last.start()
    last.wait()


def total_kernel(y_in, near_ref, y_out, parts, sem):
    total = jnp.sum(near_ref[...], axis=0).astype(BF16)
    parts[...] = jnp.broadcast_to(total[None], parts.shape)
    copy = pltpu.make_async_copy(parts, y_out.at[:, pl.ds(DATA, SHARE), :], sem)
    copy.start()
    copy.wait()


def finish_kernel(back_ref, cot_ref, value_ref, first_ref, second_ref, pos_ref, pos_bias_ref, mid_ref, mid_bias_ref, total):
    step = pl.program_id(0)
    value_ref[...] = back_ref[:, 2 * CHANNELS : DATA, :]
    first_ref[...] = back_ref[:, CHANNELS : 2 * CHANNELS, :]
    second_ref[...] = (cot_ref[...].astype(F32) * back_ref[:, :CHANNELS, :].astype(F32)).astype(BF16)
    part = jnp.zeros(total.shape, F32)
    for i in range(back_ref.shape[0] // PEERS):
        part = part + back_ref[i * PEERS : (i + 1) * PEERS, DATA:, :].astype(F32)

    @pl.when(step == 0)
    def _():
        total[...] = part

    @pl.when(step > 0)
    def _():
        total[...] += part

    @pl.when(step == pl.num_programs(0) - 1)
    def _():
        whole = jnp.concatenate([total[j] for j in range(PEERS)], axis=0)
        mid_ref[...] = whole.T[:WIDTH, :]
        pos_ref[...] = whole[:PE, WIDTH:]
        pos_bias_ref[...] = whole[PE : PE + 1, WIDTH:]
        mid_bias_ref[...] = whole[PE_BLOCK + 1 : PE_BLOCK + 2, WIDTH:]


def full(shape):
    return pl.BlockSpec(shape, lambda i: (0,) * len(shape))


def params(limit=VMEM_BYTES):
    return pltpu.CompilerParams(vmem_limit_bytes=limit)


def pack(value, first, second, cot):
    anywhere = pl.BlockSpec(memory_space=pltpu.HBM)
    buffer = pltpu.VMEM(value.shape, BF16)
    return pl.pallas_call(
        pack_kernel,
        in_specs=[anywhere] * 4,
        out_specs=anywhere,
        out_shape=jax.ShapeDtypeStruct((value.shape[0], DATA, RADIX), BF16),
        scratch_shapes=[buffer] * 2
        + [pltpu.VMEM((value.shape[0], DATA, RADIX), BF16), pltpu.SemaphoreType.DMA((5 * PACK_PARTS,))],
        compiler_params=params(),
        cost_estimate=pl.CostEstimate(flops=1 << 17, bytes_accessed=1 << 20, transcendentals=0),
    )(value, first, second, cot)


def network_forward(pos_weight, pos_bias, mid_weight, mid_bias, out_weight, decay_rates, tables, stack, ramp):
    left, back, right, right_inv, twid_cos, twid_sin = tables
    block = pl.BlockSpec((2 * WIDTH, NET_CHUNK), lambda i: (0, i))
    tabs = (left, right, twid_cos, twid_sin)
    args = (pos_weight.T, pos_bias[None, :], mid_weight, mid_bias[None, :], out_weight.T, decay_rates[None, :])
    outs = [
        jax.ShapeDtypeStruct((2 * WIDTH, SEQLEN), BF16),
        jax.ShapeDtypeStruct((2 * WIDTH, SEQLEN), BF16),
        jax.ShapeDtypeStruct((2, CHANNELS * KROWS, 2 * RADIX), F32),
        jax.ShapeDtypeStruct((2 * WIDTH, RADIX), BF16),
        jax.ShapeDtypeStruct((ROWS, RADIX), F32),
    ]
    return pl.pallas_call(
        network_kernel,
        grid=(SEQLEN // NET_CHUNK,),
        in_specs=[block, pl.BlockSpec((1, NET_CHUNK), lambda i: (0, i))]
        + [full(a.shape) for a in tabs]
        + [full(a.shape) for a in args],
        out_specs=[block] * 2 + [full(o.shape) for o in outs[2:]],
        out_shape=outs,
        scratch_shapes=[
            pltpu.VMEM((HALF_ROWS * ROWS, RADIX), F32),
            pltpu.VMEM((RADIX, RADIX), F32),
            pltpu.VMEM((2 * WIDTH, 2 * WIDTH), BF16),
            pltpu.VMEM((2 * WIDTH, 2 * WIDTH), BF16),
            pltpu.VMEM((2 * ROWS, 2 * WIDTH), BF16),
            pltpu.VMEM((WIDTH, RADIX), F32),
            pltpu.VMEM((ROWS, RADIX), F32),
        ],
        compiler_params=params(),
        cost_estimate=pl.CostEstimate(flops=1 << 30, bytes_accessed=10 << 20, transcendentals=1 << 20),
    )(stack, ramp, *tabs, *args)


def chain(x, net, tables, tail, ramp):
    act, cos, spec, own, own_rate = net
    left, back, right, right_inv, twid_cos, twid_sin = tables
    spectrum = pltpu.VMEM((CHANNELS * KROWS, 2 * RADIX), F32)
    wide = pltpu.VMEM((HALF_ROWS, CHANNELS * RADIX), F32)
    tall = 2 * WIDTH + PE_BLOCK
    small = (x, left, back, right, right_inv, twid_cos, twid_sin, own, own_rate, ramp)
    anywhere = pl.BlockSpec(memory_space=pltpu.HBM)
    within = pl.BlockSpec(memory_space=pltpu.VMEM)
    return pl.pallas_call(
        chain_kernel,
        in_specs=[anywhere] * 14,
        out_specs=[within] * 2 + [anywhere] * 3,
        out_shape=[
            jax.ShapeDtypeStruct((WIDTH, RADIX), F32),
            jax.ShapeDtypeStruct((ROWS, WIDTH), F32),
            jax.ShapeDtypeStruct((CHANNELS * KROWS, 2 * RADIX), F32),
            jax.ShapeDtypeStruct((CHANNELS * KROWS, 2 * RADIX), F32),
            jax.ShapeDtypeStruct((HALF_ROWS, CHANNELS * RADIX), BF16),
        ],
        scratch_shapes=[pltpu.VMEM(a.shape, a.dtype) for a in small]
        + [pltpu.VMEM(x.shape, F32)]
        + [spectrum] * 4
        + [wide] * 2
        + [
            pltpu.VMEM((HALF_ROWS, CHANNELS * RADIX), BF16),
            pltpu.VMEM((HALF_ROWS * ROWS, RADIX), F32),
            pltpu.VMEM(spec.shape, F32),
            pltpu.VMEM((tall, SEQLEN), BF16),
            pltpu.VMEM((2 * WIDTH, SEQLEN), BF16),
            pltpu.VMEM((2 * WIDTH + ROWS, SEQLEN), BF16),
            pltpu.VMEM((tall, 2 * WIDTH + ROWS), F32),
            pltpu.SemaphoreType.DMA((7 + len(small),)),
        ],
        compiler_params=params(CHAIN_BYTES),
        cost_estimate=pl.CostEstimate(flops=3 << 30, bytes_accessed=8 << 20, transcendentals=1 << 17),
    )(*small, spec, act, cos, tail)


def outputs(spec, sz, sg1, prod, tables):
    left, back, right, right_inv, twid_cos, twid_sin = tables
    anywhere = pl.BlockSpec(memory_space=pltpu.HBM)
    args = (spec, sz, sg1, prod, back, right_inv, twid_cos, twid_sin)
    return pl.pallas_call(
        output_kernel,
        in_specs=[anywhere] * len(args),
        out_specs=anywhere,
        out_shape=jax.ShapeDtypeStruct((HALF_ROWS, SEND, RADIX), BF16),
        scratch_shapes=[pltpu.VMEM(a.shape, a.dtype) for a in args]
        + [
            pltpu.VMEM((HALF_ROWS * DATA, RADIX), F32),
            pltpu.VMEM((HALF_ROWS, DATA, RADIX), BF16),
            pltpu.SemaphoreType.DMA((len(args) + 2,)),
        ],
        compiler_params=params(),
        cost_estimate=pl.CostEstimate(flops=1 << 29, bytes_accessed=4 << 20, transcendentals=0),
    )(*args)


def add_total(y, near):
    anywhere = pl.BlockSpec(memory_space=pltpu.HBM)
    return pl.pallas_call(
        total_kernel,
        in_specs=[anywhere, pl.BlockSpec(memory_space=pltpu.VMEM)],
        out_specs=anywhere,
        out_shape=jax.ShapeDtypeStruct(y.shape, BF16),
        input_output_aliases={0: 0},
        scratch_shapes=[pltpu.VMEM((y.shape[0], SHARE, RADIX), BF16), pltpu.SemaphoreType.DMA(())],
        compiler_params=params(ADD_BYTES),
        cost_estimate=pl.CostEstimate(flops=1 << 16, bytes_accessed=1 << 17, transcendentals=0),
    )(y, near)


def finish(back, cot):
    devices = cot.shape[0]
    steps = 1
    data = pl.BlockSpec((devices // steps, CHANNELS, RADIX), lambda i: (i, 0, 0))
    outs = [jax.ShapeDtypeStruct(cot.shape, BF16)] * 3 + [
        jax.ShapeDtypeStruct((PE, WIDTH), F32),
        jax.ShapeDtypeStruct((1, WIDTH), F32),
        jax.ShapeDtypeStruct((WIDTH, WIDTH), F32),
        jax.ShapeDtypeStruct((1, WIDTH), F32),
    ]
    return pl.pallas_call(
        finish_kernel,
        grid=(steps,),
        in_specs=[pl.BlockSpec((devices // steps, SEND, RADIX), lambda i: (i, 0, 0)), data],
        out_specs=[data] * 3 + [full(o.shape) for o in outs[3:]],
        out_shape=outs,
        scratch_shapes=[pltpu.VMEM((PEERS, SHARE, RADIX), F32)],
        compiler_params=params(FIN_BYTES),
        cost_estimate=pl.CostEstimate(flops=1 << 20, bytes_accessed=1 << 20, transcendentals=0),
    )(back, cot)


SEQ = ("z", "yhi", "ylo", "x")
NEAR = ("ylo", "x")


def on_device(
    value_branch, first_gate, second_gate, out_cotangent,
    pos_weight, pos_bias, mid_weight, mid_bias, out_weight, decay_rates,
):
    devices = lax.axis_size(SEQ)
    tables = dft_tables()
    stack, tail = feature_tables()
    ramp = (np.arange(SEQLEN) / SEQLEN).astype(np.float32)[None, :]
    blocks = (devices, CHANNELS, RADIX)
    cot = out_cotangent.reshape(blocks)
    sent = pack(value_branch.reshape(blocks), first_gate.reshape(blocks), second_gate.reshape(blocks), cot)
    x = lax.all_to_all(sent, SEQ, 0, 0, tiled=True)
    net = network_forward(
        pos_weight, pos_bias, mid_weight, mid_bias, out_weight, decay_rates, tables, stack, ramp
    )
    share, out_weight_grad, sz, sg1, prod = chain(x.reshape(HALF_ROWS * DATA, RADIX), net, tables, tail, ramp)
    near = lax.all_to_all(share.reshape(PEERS, SHARE, RADIX), NEAR, 0, 0, tiled=True)
    y = outputs(net[2], sz, sg1, prod, tables)
    back = lax.all_to_all(add_total(y, near), SEQ, 0, 0, tiled=True)
    value_grad, first_grad, second_grad, pos_grad, pos_bias_grad, mid_grad, mid_bias_grad = finish(back, cot)
    shape = value_branch.shape
    return (
        value_grad.reshape(shape),
        first_grad.reshape(shape),
        second_grad.reshape(shape),
        pos_grad.T,
        pos_bias_grad[0],
        mid_grad,
        mid_bias_grad[0],
        out_weight_grad,
    )


def solution(mesh):
    grid = Mesh(mesh.devices.reshape(mesh.shape["dp"], 2, 4, 2, 4), ("dp",) + SEQ)
    part = P(None, ("dp",) + SEQ)
    in_specs = (part,) * 4 + (P(),) * 6
    out_specs = (part,) * 3 + (P("dp", None), P("dp"), P("dp", None), P("dp"), P(SEQ, "dp"))
    return jax.shard_map(on_device, mesh=grid, in_specs=in_specs, out_specs=out_specs, check_vma=False)
```
